32 devices in a mesh: cell: 4 (over y, x), blk: 8 (over z, core).
Axes of the slice: x: 2, y: 2, z: 4, core: 2. Of those that a mesh axis runs over, the one named last changes fastest.
Arguments:
- positions: float32 [3, 16384], P(None, ('cell', 'blk')), parts along dimension 1, as said below
- species: int32 [16384], P(('cell', 'blk')), parts along dimension 0, may hold values from 0 to 3
- neighbors: int32 [32, 16384], P(None, ('cell', 'blk')), parts along dimension 1, may hold values from -1 to 4095, as said below
- pair_lists: int32 [2, 1024], P(None, ('cell', 'blk')), parts along dimension 1, may hold values from -1 to 31, as said below
- hardness: float32 [4], replicated, may hold values from 0.5 to 2
- w_first: float32 [4, 25, 64], replicated, may hold values from -0.75 to 0.75
- b_first: float32 [4, 25], replicated, may hold values from -3 to 3
- w_second: float32 [4, 25, 25], replicated, may hold values from -1.25 to 1.25
- b_second: float32 [4, 25], replicated, may hold values from -3 to 3
- w_out: float32 [4, 25], replicated, may hold values from -1.25 to 1.25
- b_out: float32 [4], replicated, may hold values from -3 to 3
Outputs:
- charges: float32 [16384], P(('cell', 'blk')), parts along dimension 0
- forces: float32 [3, 16384], P(None, ('cell', 'blk')), parts along dimension 1
The draws below stay inside these ranges and needn't reach their ends.
There are 4 independent parts, one for each index of `cell`. The reference program is written for one: setup_inputs(seed, part) draws one part's arguments, and reference() takes and returns one part's arrays. A program takes and returns all parts, laid end to end along the dimension named above; an argument that names none is the same for every part. Nothing has to cross between parts.
Inputs may be any that keep to these rules, and one draw needn't show every extreme that they name: `positions`: coordinates of an ionic-liquid film at a density of 0.1 atoms per unit volume; each block of 128 atoms fills one box of the film. `neighbors`: each atom's column lists distinct other atoms of its cell within distance 7 first and -1 after them; every block holds atoms with all 32 entries. `pair_lists`: each device has 32 slots; live slots come first and hold (row block, column block), empty ones -1 in both rows. The first 4 slots of a device pair each of its own 4 blocks with itself; the other live slots pair one of its blocks with a different block that adjoins it in space. The row block of a live slot is always a block of the slot's device.
All inputs are finite; a program needn't handle non-finite values.
Results may differ from the reference program's by a relative error of at most 0.0003.
Values sent between devices are 32-bit elements; how exact they have to be, the bound alone decides.
No kernel may reach another device: no remote copies, remote signals or barrier semaphores. Data moves between devices by JAX's collectives and lax.ppermute only.
A program may use at most 128 MiB of HBM per device.

```python
import math
import jax
import jax.numpy as jnp
import numpy as np
from jax import lax

ELEM = 4
RAD = 16
DESC = 64
HID = 25
BLOCK = 128
BLOCKS_DEV = 4
NBR = 32
ITERS = 3
NATOM = 4096
NB = 32
PAIRS_DEV = 32


lattice_spacing = 10.0 ** (1.0 / 3.0)


def grid_sizes():
    rest = NB // 2
    across = 1
    for count in range(1, rest + 1):
        if rest % count == 0 and count * count <= rest:
            across = count
    return (across, rest // across)


def lattice_site(atom_ids):
    across, along = grid_sizes()
    block_ids = atom_ids // BLOCK
    local = atom_ids % BLOCK
    layer = block_ids // (across * along)
    column = block_ids // along % across
    place = block_ids % along
    return (layer * 4 + local // 32, column * 4 + local // 8 % 4, place * 8 + local % 8)


def atom_at(first, second, third):
    across, along = grid_sizes()
    block_ids = (first // 4 * across + second // 4) * along + third // 8
    return block_ids * BLOCK + first % 4 * 32 + second % 4 * 8 + third % 8


def offset_table():
    found = []
    for step_one in range(-2, 3):
        for step_two in range(-2, 3):
            for step_three in range(-2, 3):
                length = step_one * step_one + step_two * step_two + step_three * step_three
                if 1 <= length <= 4:
                    found.append((length, step_one, step_two, step_three))
    found.sort()
    return np.array([[entry[1], entry[2], entry[3]] for entry in found[:NBR]], dtype=np.int32)


def draw_positions(key, part):
    atom_ids = jnp.arange(NATOM, dtype=jnp.int32)
    first, second, third = lattice_site(atom_ids)
    sites = jnp.stack([first, second, third]).astype(jnp.float32) * lattice_spacing
    jitter = 0.1 * jnp.clip(jax.random.normal(jax.random.fold_in(key, 42), (3, NATOM), jnp.float32), -2.5, 2.5)
    return (sites + lattice_spacing * jitter).astype(jnp.float32)


def draw_neighbors(key, part):
    across, along = grid_sizes()
    table = jnp.asarray(offset_table())
    atom_ids = jnp.arange(NATOM, dtype=jnp.int32)
    first, second, third = lattice_site(atom_ids)
    slot_ids = jnp.arange(NBR, dtype=jnp.int32)[:, None]
    scores = jax.random.randint(jax.random.fold_in(key, 31), (NBR, NATOM), 0, 1 << 20) * NBR + slot_ids
    order = jnp.argsort(scores, axis=0)
    picked = table[order]
    near_first = first[None] + picked[:, :, 0]
    near_second = second[None] + picked[:, :, 1]
    near_third = third[None] + picked[:, :, 2]
    inside = (near_first >= 0) & (near_first < 8) & (near_second >= 0) & (near_second < 4 * across)
    inside = inside & (near_third >= 0) & (near_third < 8 * along)
    counts = jax.random.randint(jax.random.fold_in(key, 32), (NATOM,), NBR // 2, NBR + 1)
    local = atom_ids % BLOCK
    layer = first // 4
    column = second // 4
    full = (local // 32 == 3 - 2 * layer) & (local // 8 % 4 == 1 + (column == 0).astype(jnp.int32)) & (local % 8 == 2)
    counts = jnp.where(full, NBR, counts)
    live = inside & (slot_ids < counts[None, :])
    target = atom_at(jnp.clip(near_first, 0, 7), jnp.clip(near_second, 0, 4 * across - 1), jnp.clip(near_third, 0, 8 * along - 1))
    packing = jnp.argsort(jnp.logical_not(live).astype(jnp.int32), axis=0, stable=True)
    target = jnp.take_along_axis(target, packing, axis=0)
    live = jnp.take_along_axis(live, packing, axis=0)
    return jnp.where(live, target, -1).astype(jnp.int32)


def draw_pair_lists(key, part):
    across, along = grid_sizes()
    device_count = NB // BLOCKS_DEV
    off_total = PAIRS_DEV - BLOCKS_DEV
    moves = jnp.array([[0, 0, 1], [0, 1, 0], [1, 0, 0], [0, 1, 1], [1, 0, 1], [1, 1, 0], [1, 1, 1]], dtype=jnp.int32)
    device_ids = jnp.arange(device_count, dtype=jnp.int32)[:, None]
    slot_ids = jnp.arange(PAIRS_DEV, dtype=jnp.int32)[None, :]
    remaining = device_count - device_ids
    off_count = off_total * remaining * remaining // (device_count * device_count)
    off_index = slot_ids - BLOCKS_DEV
    local_block = jnp.where(off_index < 0, slot_ids, jnp.maximum(off_index, 0) % BLOCKS_DEV)
    row_ids = device_ids * BLOCKS_DEV + local_block
    band = jnp.minimum(jnp.maximum(off_index, 0) // BLOCKS_DEV, 6)
    move = moves[band]
    layer = row_ids // (across * along) + move[:, :, 0]
    column = row_ids // along % across + move[:, :, 1]
    place = row_ids % along + move[:, :, 2]
    inside = (layer < 2) & (column < across) & (place < along)
    col_ids = (jnp.minimum(layer, 1) * across + jnp.minimum(column, across - 1)) * along + jnp.minimum(place, along - 1)
    col_ids = jnp.where(off_index < 0, row_ids, col_ids)
    noise = jax.random.randint(jax.random.fold_in(key, 21), (device_count, PAIRS_DEV), 0, 1000)
    rank_key = jnp.where(off_index < 0, 0, jnp.where(inside, 1 + noise, 2000))
    packing = jnp.argsort(rank_key, axis=1, stable=True)
    row_ids = jnp.take_along_axis(row_ids, packing, axis=1)
    col_ids = jnp.take_along_axis(col_ids, packing, axis=1)
    inside = jnp.take_along_axis(inside | (off_index < 0), packing, axis=1)
    live = (off_index < 0) | inside & (off_index < off_count)
    row_ids = jnp.where(live, row_ids, -1)
    col_ids = jnp.where(live, col_ids, -1)
    return jnp.stack([row_ids.reshape(-1), col_ids.reshape(-1)]).astype(jnp.int32)


def with_ends(entries, rng, low, top_value):
    index_at = [jax.random.randint(jax.random.fold_in(rng, axis), (), 0, length) for axis, length in enumerate(entries.shape)]
    main_axis = entries.shape.index(max(entries.shape))
    neighbour = index_at[:main_axis] + [(index_at[main_axis] + 1) % entries.shape[main_axis]] + index_at[main_axis + 1:]
    return entries.at[tuple(index_at)].set(low).at[tuple(neighbour)].set(top_value)


def bell_draw(stream_key, extent, spread, limit, kind=jnp.bfloat16):
    result = spread * jax.random.normal(stream_key, extent, jnp.float32)
    return jnp.clip(result, min=-limit, max=limit).astype(kind)


def setup_inputs(seed: int = 0, part: int = 0) -> dict:
    splits = jax.random.split(jax.random.key(seed), 12)
    part_splits = jax.random.split(jax.random.fold_in(splits[11], part), 12)
    return {
        "positions": draw_positions(jax.random.fold_in(jax.random.fold_in(splits[11], part), 71), part),
        "species": with_ends(jax.random.randint(part_splits[1], (NATOM,), 0, ELEM), jax.random.fold_in(part_splits[1], 1), 0, ELEM - 1).astype(jnp.int32),
        "neighbors": draw_neighbors(jax.random.fold_in(jax.random.fold_in(splits[11], part), 71), part),
        "pair_lists": draw_pair_lists(jax.random.fold_in(jax.random.fold_in(splits[11], part), 71), part),
        "hardness": jnp.clip(jnp.exp(jax.random.uniform(splits[4], (ELEM,), jnp.float32, math.log(0.5), math.log(2.0))), 0.5, 2.0),
        "w_first": bell_draw(splits[5], (ELEM, HID, DESC), DESC ** -0.5, 0.75, jnp.float32),
        "b_first": bell_draw(splits[6], (ELEM, HID), 0.5, 3.0, jnp.float32),
        "w_second": bell_draw(splits[7], (ELEM, HID, HID), HID ** -0.5, 1.25, jnp.float32),
        "b_second": bell_draw(splits[8], (ELEM, HID), 0.5, 3.0, jnp.float32),
        "w_out": bell_draw(splits[9], (ELEM, HID), HID ** -0.5, 1.25, jnp.float32),
        "b_out": bell_draw(splits[10], (ELEM,), 1.0, 3.0, jnp.float32),
    }


coulomb_scale = 0.5
sigma_sq = 4.0
cutoff_sq = 49.0
pair_group = 8
highest = lax.Precision.HIGHEST

def radial_rates(count):
    fraction = jnp.arange(count, dtype=jnp.float32) / (count - 1)
    return 0.005 * jnp.exp(fraction * jnp.log(200.0))

def descriptors(dist_sq, live_mask, neighbor_kind):
    rates = radial_rates(RAD)
    shell = live_mask * (1.0 - dist_sq / cutoff_sq) ** 2
    radial = shell[None] * jnp.exp(-rates[:, None, None] * dist_sq[None])
    channels = jnp.einsum('esa,ksa->eka', neighbor_kind, radial, precision=highest)
    return channels.reshape(ELEM * RAD, dist_sq.shape[1]) * (ELEM / NBR)

def network(features, own_kind, w_first, b_first, w_second, b_second, w_out, b_out):
    first = jnp.einsum('ehk,ka->eha', w_first, features, precision=highest) + b_first[:, :, None]
    hidden_one = jnp.tanh(jnp.einsum('ea,eha->ha', own_kind, first, precision=highest))
    second = jnp.einsum('ehk,ka->eha', w_second, hidden_one, precision=highest) + b_second[:, :, None]
    hidden_two = jnp.tanh(jnp.einsum('ea,eha->ha', own_kind, second, precision=highest))
    outputs = jnp.einsum('eh,ha->ea', w_out, hidden_two, precision=highest) + b_out[:, None]
    return lax.optimization_barrier(jnp.sum(own_kind * outputs, axis=0))

def neighbor_geometry(own_pos, neighbors, all_pos, all_kind):
    live_mask = (neighbors >= 0).astype(own_pos.dtype)
    neighbor_ids = jnp.maximum(neighbors, 0).astype(jnp.int32)
    neighbor_pos = all_pos[:, neighbor_ids]
    offsets = own_pos[:, None, :] - neighbor_pos
    dist_sq = lax.optimization_barrier(jnp.sum(offsets * offsets, axis=0))
    kinds = all_kind[neighbor_ids]
    neighbor_kind = (kinds[None] == jnp.arange(ELEM, dtype=jnp.int32)[:, None, None]).astype(own_pos.dtype)
    return (live_mask, neighbor_ids, offsets, dist_sq, neighbor_kind)

def pair_block(blocks_pos, row_blocks, col_blocks):
    live_mask = (row_blocks >= 0).astype(blocks_pos.dtype)
    row_ids = jnp.maximum(row_blocks, 0).astype(jnp.int32)
    col_ids = jnp.maximum(col_blocks, 0).astype(jnp.int32)
    row_pos = blocks_pos[:, row_ids]
    col_pos = blocks_pos[:, col_ids]
    offsets = row_pos[:, :, :, None] - col_pos[:, :, None, :]
    dist_sq = lax.optimization_barrier(jnp.sum(offsets * offsets, axis=0))
    same_block = (row_ids == col_ids).astype(blocks_pos.dtype)
    identity = jnp.eye(blocks_pos.shape[2], dtype=blocks_pos.dtype)
    keep_mask = live_mask[:, None, None] * (1.0 - same_block[:, None, None] * identity[None])
    kernel = coulomb_scale * jnp.exp(-dist_sq / (2.0 * sigma_sq)) * keep_mask
    cross_mask = live_mask * (1.0 - same_block)
    return (kernel, row_ids, col_ids, row_pos, col_pos, cross_mask)

def apply_group(accum, vectors, blocks_pos, row_blocks, col_blocks):
    kernel, row_ids, col_ids, row_pos, col_pos, cross_mask = pair_block(blocks_pos, row_blocks, col_blocks)
    forward = jnp.einsum('gij,vgj->vgi', kernel, vectors[:, col_ids], precision=highest)
    accum = accum.at[:, row_ids].add(forward)
    backward = jnp.einsum('gij,vgi->vgj', kernel, vectors[:, row_ids], precision=highest)
    return accum.at[:, col_ids].add(backward * cross_mask[None, :, None])

def force_group(accum, charge_blocks, blocks_pos, row_blocks, col_blocks):
    kernel, row_ids, col_ids, row_pos, col_pos, cross_mask = pair_block(blocks_pos, row_blocks, col_blocks)
    summed = charge_blocks[row_ids][:, :, None] + charge_blocks[col_ids][:, None, :]
    weight = kernel * summed * summed / (2.0 * sigma_sq)
    row_part = row_pos * lax.optimization_barrier(jnp.sum(weight, axis=2))[None] - jnp.einsum('gij,dgj->dgi', weight, col_pos, precision=highest)
    col_part = col_pos * lax.optimization_barrier(jnp.sum(weight, axis=1))[None] - jnp.einsum('gij,dgi->dgj', weight, row_pos, precision=highest)
    accum = accum.at[:, row_ids].add(row_part)
    return accum.at[:, col_ids].add(col_part * cross_mask[None, :, None])

def reference(positions, species, neighbors, pair_lists, hardness, w_first, b_first, w_second, b_second, w_out, b_out):
    natom = positions.shape[1]
    blocks = natom // BLOCK
    own_kind = (species[None] == jnp.arange(ELEM, dtype=jnp.int32)[:, None]).astype(positions.dtype)
    live_mask, neighbor_ids, offsets, dist_sq, neighbor_kind = neighbor_geometry(positions, neighbors, positions, species)

    def electroneg(dist_values):
        features = descriptors(dist_values, live_mask, neighbor_kind)
        return network(features, own_kind, w_first, b_first, w_second, b_second, w_out, b_out)
    chi, pullback = jax.vjp(electroneg, dist_sq)
    blocks_pos = positions.reshape(3, blocks, BLOCK)
    pair_groups = pair_lists.reshape(2, -1, pair_group).transpose(1, 0, 2)

    def apply_all(vectors):

        def add_group(accum, pair_slice):
            return (apply_group(accum, vectors, blocks_pos, pair_slice[0], pair_slice[1]), 0)
        return lax.scan(add_group, jnp.zeros_like(vectors), pair_groups)[0]
    hard_atoms = lax.optimization_barrier(jnp.sum(own_kind * hardness[:, None], axis=0))
    residual = -chi
    direction = residual
    solution = jnp.zeros_like(chi)
    res_sq = jnp.sum(residual * residual)
    diagonal = hard_atoms
    for iteration in range(ITERS):
        if iteration == 0:
            stacked = jnp.stack([jnp.ones_like(direction), direction]).reshape(2, blocks, BLOCK)
            images = apply_all(stacked).reshape(2, natom)
            diagonal = hard_atoms + images[0]
            coupled = images[1]
        else:
            coupled = apply_all(direction.reshape(1, blocks, BLOCK)).reshape(natom)
        image = diagonal * direction + coupled
        step_size = res_sq / jnp.sum(direction * image)
        solution = solution + step_size * direction
        residual = residual - step_size * image
        if iteration + 1 < ITERS:
            new_sq = jnp.sum(residual * residual)
            direction = residual + new_sq / res_sq * direction
            res_sq = new_sq
    charges = solution
    grad_sq, = pullback(charges)
    pushes = 2.0 * grad_sq[None] * offsets
    forces = jnp.zeros((3, natom), positions.dtype).at[:, neighbor_ids.reshape(-1)].add(pushes.reshape(3, -1))
    forces = forces - lax.optimization_barrier(jnp.sum(pushes, axis=1))
    charge_blocks = charges.reshape(blocks, BLOCK)

    def add_forces(accum, pair_slice):
        return (force_group(accum, charge_blocks, blocks_pos, pair_slice[0], pair_slice[1]), 0)
    pair_part = lax.scan(add_forces, jnp.zeros((3, blocks, BLOCK), positions.dtype), pair_groups)[0]
    forces = forces + pair_part.reshape(3, natom)
    return (charges, forces)
```

```python
import functools
import math

import jax
import jax.numpy as jnp
import numpy as np
from jax import lax
from jax.experimental import pallas as pl
from jax.experimental.pallas import tpu as pltpu
from jax.sharding import PartitionSpec as P

ELEM = 4
RAD = 16
DESC = ELEM * RAD
HPAD = 32
BLOCK = 128
NBR = 32
ITERS = 3
PACK = 24
STORE_LIMIT = 36 << 20

coulomb_scale = 0.5
sigma_sq = 4.0
cutoff_sq = 49.0
highest = lax.Precision.HIGHEST
RATES = [0.005 * 200.0 ** (k / (RAD - 1)) for k in range(RAD)]
VM = pltpu.VMEM
SM = pltpu.SMEM


def spec(space):
    return pl.BlockSpec(memory_space=space)


def piece_of(q, me, pow2):
    return q ^ me if pow2 else q


def dot(a, b):
    return jnp.dot(a, b, precision=highest, preferred_element_type=jnp.float32)


def column(row):
    return jnp.broadcast_to(row, (BLOCK, BLOCK)).T


def pick(kind, mats):
    out = jnp.where(kind == 0, mats[0], 0.0)
    for e in range(1, ELEM):
        out = jnp.where(kind == e, mats[e], out)
    return out


def chi_kernel(pow2, nd, bd, me_ref, g_ref, pos_ref, nbr_ref, kind_ref, w1, b1, w2, b2, wo, bo,
               chi_ref, d_ref, h_ref, f_ref):
    me = me_ref[0]
    for a in range(bd):
        lanes = slice(a * BLOCK, (a + 1) * BLOCK)
        idx = nbr_ref[:, lanes]
        hi = idx >> 7
        lo = idx & 127

        def look(q, vals):
            at = piece_of(q, me, pow2)
            for r in range(bd):
                hit = hi == q * bd + r
                new = []
                for d in range(4):
                    row = jnp.broadcast_to(g_ref[at, d * bd + r:d * bd + r + 1, :], (NBR, BLOCK))
                    new.append(jnp.where(hit, jnp.take_along_axis(row, lo, axis=1), vals[d]))
                vals = tuple(new)
            return vals

        zero = jnp.zeros((NBR, BLOCK), jnp.float32)
        vals = lax.fori_loop(0, nd, look, (zero,) * 4, unroll=2)
        live = idx >= 0
        offs = [jnp.where(live, pos_ref[d:d + 1, lanes] - vals[d], 0.0) for d in range(3)]
        for d in range(3):
            d_ref[d, :, lanes] = offs[d]
        nk = jnp.where(live, vals[3], -1.0)
        d_ref[3, :, lanes] = nk
        r2 = offs[0] * offs[0] + offs[1] * offs[1] + offs[2] * offs[2]
        u = 1.0 - r2 * (1.0 / cutoff_sq)
        shell = u * u * (ELEM / NBR)
        for k in range(RAD):
            val = shell * jnp.exp(-RATES[k] * r2)
            for e in range(ELEM):
                f_ref[e * RAD + k:e * RAD + k + 1, lanes] = jnp.sum(
                    jnp.where(nk == e, val, 0.0), axis=0, keepdims=True)
    kind = kind_ref[...]
    first = dot(w1[...], f_ref[...]) + b1[...]
    h1 = jnp.tanh(pick(kind, [first[e * HPAD:(e + 1) * HPAD] for e in range(ELEM)]))
    second = dot(w2[...], h1) + b2[...]
    h2 = jnp.tanh(pick(kind, [second[e * HPAD:(e + 1) * HPAD] for e in range(ELEM)]))
    h_ref[0] = h1
    h_ref[1] = h2
    wsel = pick(kind, [wo[e * HPAD:(e + 1) * HPAD] for e in range(ELEM)])
    bsel = pick(kind, [bo[e] for e in range(ELEM)])
    chi = jnp.sum(wsel * h2, axis=0, keepdims=True) + bsel
    for a in range(bd):
        chi_ref[a:a + 1, :] = chi[:, a * BLOCK:(a + 1) * BLOCK]


def masked(kind, vals):
    return jnp.concatenate([jnp.where(kind == e, vals, 0.0) for e in range(ELEM)], axis=0)


def pull_part(bd, kind_ref, d_ref, h_ref, w1t, w2t, wo, push_ref, f_ref):
    kind = kind_ref[...]
    h1 = h_ref[0]
    h2 = h_ref[1]
    wsel = pick(kind, [wo[e * HPAD:(e + 1) * HPAD] for e in range(ELEM)])
    pre2 = wsel * (1.0 - h2 * h2)
    pre1 = dot(w2t[...], masked(kind, pre2)) * (1.0 - h1 * h1)
    f_ref[...] = dot(w1t[...], masked(kind, pre1)) * (ELEM / NBR)
    for a in range(bd):
        lanes = slice(a * BLOCK, (a + 1) * BLOCK)
        offs = [d_ref[d, :, lanes] for d in range(3)]
        nk = d_ref[3, :, lanes]
        r2 = offs[0] * offs[0] + offs[1] * offs[1] + offs[2] * offs[2]
        u = 1.0 - r2 * (1.0 / cutoff_sq)
        s1 = jnp.zeros_like(r2)
        s2 = jnp.zeros_like(r2)
        for k in range(RAD):
            sel = jnp.zeros_like(r2)
            for e in range(ELEM):
                sel = jnp.where(nk == e, f_ref[e * RAD + k:e * RAD + k + 1, lanes], sel)
            term = sel * jnp.exp(-RATES[k] * r2)
            s1 = s1 + term
            s2 = s2 + RATES[k] * term
        grad = -u * ((2.0 / cutoff_sq) * s1 + u * s2)
        for d in range(3):
            push_ref[d, :, lanes] = 2.0 * grad * offs[d]


def gamma_block(rows, cols, same):
    r2 = None
    for d in range(3):
        diff = cols[d] - rows[d]
        r2 = diff * diff if r2 is None else r2 + diff * diff
    val = coulomb_scale * jnp.exp(r2 * (-0.5 / sigma_sq))
    shape = (BLOCK, BLOCK)
    ident = lax.broadcasted_iota(jnp.int32, shape, 0) == lax.broadcasted_iota(jnp.int32, shape, 1)
    return jnp.where(ident & same, 0.0, val)


def rows_at(g_ref, b, me, pow2, bd, count=3):
    at = piece_of(b // bd, me, pow2)
    r = b % bd
    return [g_ref[at, pl.ds(d * bd + r, 1), :] for d in range(count)]


def build_kernel(pow2, bd, nb, stored, me_ref, list_ref, start_ref, g_ref, kind_ref, d_ref, h_ref,
                 w1t, w2t, wo, push_ref, sums_ref, *rest):
    c_ref = rest[0] if stored else None
    f_ref = rest[-1]
    me = me_ref[0]
    pull_part(bd, kind_ref, d_ref, h_ref, w1t, w2t, wo, push_ref, f_ref)

    def block_row(i, carry):
        cols = [column(row) for row in rows_at(g_ref, i, me, pow2, bd)]

        def entry(t, acc):
            j = list_ref[t]
            val = gamma_block(rows_at(g_ref, j, me, pow2, bd), cols, i == j)
            if stored:
                c_ref[t] = val
            return acc + val

        acc = lax.fori_loop(start_ref[i], start_ref[i + 1], entry,
                            jnp.zeros((BLOCK, BLOCK), jnp.float32))
        sums_ref[pl.ds(i, 1), :] = jnp.sum(acc.T, axis=0, keepdims=True)
        return carry

    lax.fori_loop(0, nb, block_row, 0)


def solve_kernel(pow2, nd, bd, nb, stored, me_ref, list_ref, start_ref, hard_ref, g_ref, x_ref,
                 sums_ref, push_ref, nbr_ref, *rest):
    if stored:
        c_ref, charge_ref, part_ref, p_ref, y_ref, q_ref, diag_ref = rest
    else:
        c_ref = None
        charge_ref, part_ref, p_ref, y_ref, q_ref, diag_ref = rest
    me = me_ref[0]
    for q in range(nd):
        at = piece_of(q, me, pow2)
        span = slice(q * bd, (q + 1) * bd)
        p_ref[span, :] = -x_ref[at]
        kind = g_ref[at, 3 * bd:4 * bd, :]
        diag_ref[span, :] = pick(kind, [hard_ref[e] for e in range(ELEM)])
    diag = diag_ref[...] + sums_ref[...]

    def coupling(t, i, cols):
        if stored:
            return c_ref[t]
        j = list_ref[t]
        return gamma_block(rows_at(g_ref, j, me, pow2, bd), cols, i == j)

    def matvec():
        def block_row(i, carry):
            cols = None if stored else [column(row) for row in rows_at(g_ref, i, me, pow2, bd)]

            def entry(t, acc):
                return acc + coupling(t, i, cols) * p_ref[pl.ds(list_ref[t], 1), :]

            acc = lax.fori_loop(start_ref[i], start_ref[i + 1], entry,
                                jnp.zeros((BLOCK, BLOCK), jnp.float32))
            y_ref[pl.ds(i, 1), :] = jnp.sum(acc.T, axis=0, keepdims=True)
            return carry

        lax.fori_loop(0, nb, block_row, 0)

    def total(vals):
        return jnp.sum(jnp.sum(vals, axis=0, keepdims=True), axis=1, keepdims=True)

    res = p_ref[...]
    p = res
    x = jnp.zeros_like(res)
    rho = total(res * res)
    for it in range(ITERS):
        matvec()
        image = diag * p + y_ref[...]
        step = rho / total(p * image)
        x = x + step * p
        if it + 1 < ITERS:
            res = res - step * image
            rho2 = total(res * res)
            p = res + (rho2 / rho) * p
            rho = rho2
            p_ref[...] = p
    q_ref[...] = x
    for a in range(bd):
        charge_ref[a:a + 1, :] = q_ref[pl.ds(me * bd + a, 1), :]
    mine = jnp.concatenate([charge_ref[a:a + 1, :] for a in range(bd)], axis=1)
    width = bd * BLOCK

    def scatter(s, acc):
        idx = nbr_ref[pl.ds(s, 1), :]
        hit = lax.broadcasted_iota(jnp.int32, (nb, width), 0) == (idx >> 7)
        spot = lax.broadcasted_iota(jnp.int32, (BLOCK, width), 0) == (idx & 127)
        ones = jnp.where(spot, 1.0, 0.0).astype(jnp.bfloat16)
        upper = []
        lower = []
        for d in range(3):
            val = push_ref[d, pl.ds(s, 1), :] * mine
            top = val.astype(jnp.bfloat16).astype(jnp.float32)
            upper.append(jnp.where(hit, top, 0.0).astype(jnp.bfloat16))
            lower.append(jnp.where(hit, val - top, 0.0).astype(jnp.bfloat16))
        both = jnp.concatenate(upper + lower, axis=0)
        return acc + lax.dot_general(both, ones, (((1,), (1,)), ((), ())),
                                     preferred_element_type=jnp.float32)

    acc = lax.fori_loop(0, NBR, scatter, jnp.zeros((6 * nb, BLOCK), jnp.float32), unroll=2)
    acc = acc[:3 * nb] + acc[3 * nb:]
    for q in range(nd):
        for d in range(3):
            part_ref[q, d * bd:(d + 1) * bd, :] = acc[d * nb + q * bd:d * nb + (q + 1) * bd]
    for a in range(bd):
        i = me * bd + a
        own_rows = rows_at(g_ref, i, me, pow2, bd)
        cols = [column(row) for row in own_rows]
        qcol = column(q_ref[pl.ds(i, 1), :])

        def entry(t, accs):
            j = list_ref[t]
            rows = rows_at(g_ref, j, me, pow2, bd)
            both = qcol + q_ref[pl.ds(j, 1), :]
            weight = coupling(t, i, cols) * (both * both)
            return tuple(accs[d] + weight * (cols[d] - rows[d]) for d in range(3))

        zero = jnp.zeros((BLOCK, BLOCK), jnp.float32)
        accs = lax.fori_loop(start_ref[i], start_ref[i + 1], entry, (zero,) * 3)
        for d in range(3):
            pair = jnp.sum(accs[d].T, axis=0, keepdims=True) * (0.5 / sigma_sq)
            lanes = slice(a * BLOCK, (a + 1) * BLOCK)
            away = jnp.sum(push_ref[d, :, lanes], axis=0, keepdims=True) * charge_ref[a:a + 1, :]
            at = (me, slice(d * bd + a, d * bd + a + 1), slice(None))
            part_ref[at] = part_ref[at] + pair - away


def gather_all(own, n):
    if n & (n - 1):
        return lax.all_gather(own, "blk"), False
    got = own[None]
    step = 1
    while step < n:
        other = lax.ppermute(got, "blk", [(i, i ^ step) for i in range(n)])
        got = jnp.concatenate([got, other], axis=0)
        step *= 2
    return got, True


def sorted_pairs(rows, cols, nb):
    live = rows >= 0
    cross = live & (rows != cols)
    key = jnp.concatenate([jnp.where(live, rows, nb), jnp.where(cross, cols, nb)])
    other = jnp.concatenate([cols, rows])
    count = key.shape[0]
    unique = key * count + jnp.arange(count, dtype=jnp.int32)
    rank = jnp.sum((unique[None, :] < unique[:, None]).astype(jnp.int32), axis=1)
    places = jnp.arange(count - nb, dtype=jnp.int32)
    order = jnp.sum(jnp.where(rank[:, None] == places[None, :], other[:, None], 0), axis=0)
    blocks = jnp.arange(nb + 1, dtype=jnp.int32)
    starts = jnp.sum((key[:, None] < blocks[None, :]).astype(jnp.int32), axis=0)
    return jnp.maximum(order, 0), starts


def on_device(positions, species, neighbors, pair_lists, hardness, w_first, b_first, w_second,
              b_second, w_out, b_out):
    n = lax.axis_size("blk")
    me = lax.axis_index("blk")[None]
    atoms = positions.shape[1]
    bd = atoms // BLOCK
    nb = bd * n
    slots = pair_lists.shape[1]
    hid = w_first.shape[1]
    own = jnp.concatenate([
        positions.reshape(3 * bd, BLOCK),
        species.astype(jnp.float32).reshape(bd, BLOCK),
        jnp.pad(pair_lists.astype(jnp.float32).reshape(1, 2 * slots),
                ((0, PACK - 4 * bd - 1), (0, BLOCK - 2 * slots))),
    ], axis=0)
    whole, pow2 = gather_all(own, n)
    more = HPAD - hid
    w1 = jnp.pad(w_first, ((0, 0), (0, more), (0, 0))).reshape(ELEM * HPAD, DESC)
    b1 = jnp.pad(b_first, ((0, 0), (0, more))).reshape(ELEM * HPAD, 1)
    w2 = jnp.pad(w_second, ((0, 0), (0, more), (0, more)))
    w2f = w2.reshape(ELEM * HPAD, HPAD)
    b2 = jnp.pad(b_second, ((0, 0), (0, more))).reshape(ELEM * HPAD, 1)
    wo = jnp.pad(w_out, ((0, 0), (0, more))).reshape(ELEM * HPAD, 1)
    w1t = w1.T
    w2t = w2f.T
    kind = species.reshape(1, atoms)
    f32 = jnp.float32
    chi, offs, hidden = pl.pallas_call(
        functools.partial(chi_kernel, pow2, n, bd),
        out_shape=(jax.ShapeDtypeStruct((bd, BLOCK), f32),
                   jax.ShapeDtypeStruct((4, NBR, atoms), f32),
                   jax.ShapeDtypeStruct((2, HPAD, atoms), f32)),
        in_specs=[spec(SM)] + [spec(VM)] * 9 + [spec(SM)],
        out_specs=(spec(VM),) * 3,
        scratch_shapes=[VM((DESC, atoms), f32)],
        compiler_params=pltpu.CompilerParams(vmem_limit_bytes=16 << 20),
        name="chi",
    )(me, whole, positions, neighbors, kind, w1, b1, w2f, b2, wo, b_out)
    all_chi, _ = gather_all(chi, n)
    lists = whole[:, 4 * bd, :2 * slots].astype(jnp.int32)
    order, starts = sorted_pairs(lists[:, :slots].reshape(-1), lists[:, slots:].reshape(-1), nb)
    entries = order.shape[0]
    stored = entries * BLOCK * BLOCK * 4 <= STORE_LIMIT
    table = (pltpu.VMEM((entries, BLOCK, BLOCK), f32),) if stored else ()
    out = pl.pallas_call(
        functools.partial(build_kernel, pow2, bd, nb, stored),
        out_shape=(jax.ShapeDtypeStruct((3, NBR, atoms), f32),
                   jax.ShapeDtypeStruct((nb, BLOCK), f32)) + table,
        in_specs=[spec(SM)] * 3 + [spec(VM)] * 7,
        out_specs=(spec(VM),) * (2 + len(table)),
        scratch_shapes=[VM((DESC, atoms), f32)],
        compiler_params=pltpu.CompilerParams(vmem_limit_bytes=16 << 20),
        name="build",
    )(me, order, starts, whole, kind, offs, hidden, w1t, w2t, wo)
    push, sums = out[:2]
    charges, part = pl.pallas_call(
        functools.partial(solve_kernel, pow2, n, bd, nb, stored),
        out_shape=(jax.ShapeDtypeStruct((bd, BLOCK), f32),
                   jax.ShapeDtypeStruct((n, 3 * bd, BLOCK), f32)),
        in_specs=[spec(SM)] * 4 + [spec(VM)] * (5 + len(table)),
        out_specs=(spec(VM),) * 2,
        scratch_shapes=[VM((nb, BLOCK), f32)] * 4,
        compiler_params=pltpu.CompilerParams(vmem_limit_bytes=16 << 20),
        name="solve",
    )(me, order, starts, hardness, whole, all_chi, sums, push, neighbors, *out[2:])
    swapped = lax.all_to_all(part, "blk", 0, 0)
    forces = jnp.sum(swapped, axis=0)
    return charges.reshape(atoms), forces.reshape(3, atoms)


def solution(mesh):
    both = ("cell", "blk")
    placed = (P(None, both), P(both), P(None, both), P(None, both)) + (P(),) * 7
    return jax.shard_map(
        on_device,
        mesh=mesh,
        in_specs=placed,
        out_specs=(P(both), P(None, both)),
        check_vma=False,
    )
```

```python
import functools
import math

import jax
import jax.numpy as jnp
import numpy as np
from jax import lax
from jax.experimental import pallas as pl
from jax.experimental.pallas import tpu as pltpu
from jax.sharding import PartitionSpec as P

ELEM = 4
RAD = 16
DESC = ELEM * RAD
BLOCK = 128
NBR = 32
ITERS = 3
PACK = 24
STORE_LIMIT = 36 << 20

coulomb_scale = 0.5
sigma_sq = 4.0
cutoff_sq = 49.0
highest = lax.Precision.HIGHEST
RATES = [0.005 * 200.0 ** (k / (RAD - 1)) for k in range(RAD)]
VM = pltpu.VMEM
SM = pltpu.SMEM
SCALE = math.log2(math.e) / (2.0 * sigma_sq)


def spec(space):
    return pl.BlockSpec(memory_space=space)


def piece_of(q, me, pow2):
    return q ^ me if pow2 else q


def dot(a, b, lhs=1):
    return lax.dot_general(a, b, (((lhs,), (0,)), ((), ())), precision=highest,
                           preferred_element_type=jnp.float32)


def column(row):
    return jnp.broadcast_to(row, (BLOCK, BLOCK)).T


def pick(kind, mats):
    out = jnp.where(kind == 0, mats[0], 0.0)
    for e in range(1, ELEM):
        out = jnp.where(kind == e, mats[e], out)
    return out


def one_hot(kind):
    ids = lax.broadcasted_iota(jnp.int32, (ELEM, kind.shape[1]), 0)
    return jnp.where(ids == kind, 1.0, 0.0)


def pack_kernel(pos_ref, kind_ref, pairs_ref, own_ref):
    bd = pos_ref.shape[1] // BLOCK
    own_ref[...] = jnp.zeros_like(own_ref)
    for a in range(bd):
        lanes = slice(a * BLOCK, (a + 1) * BLOCK)
        for d in range(3):
            own_ref[d * bd + a:d * bd + a + 1, :] = pos_ref[d:d + 1, lanes]
        own_ref[3 * bd + a:3 * bd + a + 1, :] = kind_ref[:, lanes].astype(jnp.float32)
    slots = pairs_ref.shape[1]
    for side in range(2):
        own_ref[4 * bd + side:4 * bd + side + 1, :slots] = (
            pairs_ref[side:side + 1, :].astype(jnp.float32))


def chi_kernel(pow2, nd, bd, me_ref, g_ref, pos_ref, nbr_ref, kind_ref, w1, b1, w2, b2, wo, bo,
               chi_ref, d_ref, h_ref, f_ref):
    me = me_ref[0]
    chunk = min(nd, 8)
    for a in range(bd):
        lanes = slice(a * BLOCK, (a + 1) * BLOCK)

        def group(g, carry):
            rows8 = pl.ds(pl.multiple_of(g * 8, 8), 8)
            idx = nbr_ref[rows8, lanes]
            hi = idx >> 7
            lo = idx & 127

            def look(part, vals):
                for step in range(chunk):
                    q = part * chunk + step
                    at = piece_of(q, me, pow2)
                    for r in range(bd):
                        hit = hi == q * bd + r
                        new = []
                        for d in range(4):
                            row = jnp.broadcast_to(g_ref[at, d * bd + r:d * bd + r + 1, :],
                                                   (8, BLOCK))
                            new.append(jnp.where(hit, jnp.take_along_axis(row, lo, axis=1),
                                                 vals[d]))
                        vals = tuple(new)
                return vals

            vals = (jnp.zeros((8, BLOCK), jnp.float32),) * 4
            if nd == chunk:
                vals = look(0, vals)
            else:
                vals = lax.fori_loop(0, nd // chunk, look, vals)
            live = idx >= 0
            for d in range(3):
                d_ref[d, rows8, lanes] = jnp.where(live, pos_ref[d:d + 1, lanes] - vals[d], 0.0)
            d_ref[3, rows8, lanes] = jnp.where(live, vals[3], -1.0)
            return carry

        lax.fori_loop(0, NBR // 8, group, 0)
        offs = [d_ref[d, :, lanes] for d in range(3)]
        nk = d_ref[3, :, lanes]
        r2 = offs[0] * offs[0] + offs[1] * offs[1] + offs[2] * offs[2]
        u = 1.0 - r2 * (1.0 / cutoff_sq)
        shell = u * u * (ELEM / NBR)
        for k in range(RAD):
            val = shell * jnp.exp(-RATES[k] * r2)
            for e in range(ELEM):
                f_ref[e * RAD + k:e * RAD + k + 1, lanes] = jnp.sum(
                    jnp.where(nk == e, val, 0.0), axis=0, keepdims=True)
    kind = kind_ref[...]
    hot = one_hot(kind)
    feats = f_ref[...]
    h1 = jnp.tanh(pick(kind, [dot(w1[e], feats) for e in range(ELEM)]) + dot(b1[...], hot, 0))
    h2 = jnp.tanh(pick(kind, [dot(w2[e], h1) for e in range(ELEM)]) + dot(b2[...], hot, 0))
    h_ref[0] = h1
    h_ref[1] = h2
    bsel = pick(kind, [bo[e] for e in range(ELEM)])
    chi = jnp.sum(dot(wo[...], hot, 0) * h2, axis=0, keepdims=True) + bsel
    for a in range(bd):
        chi_ref[a:a + 1, :] = chi[:, a * BLOCK:(a + 1) * BLOCK]


def pull_kernel(bd, kind_ref, d_ref, h_ref, w1, w2, wo, push_ref, f_ref):
    kind = kind_ref[...]
    h1 = h_ref[0]
    h2 = h_ref[1]
    pre2 = dot(wo[...], one_hot(kind), 0) * (1.0 - h2 * h2)
    pre1 = sum(dot(w2[e], jnp.where(kind == e, pre2, 0.0), 0) for e in range(ELEM))
    pre1 = pre1 * (1.0 - h1 * h1)
    f_ref[...] = sum(dot(w1[e], jnp.where(kind == e, pre1, 0.0), 0)
                     for e in range(ELEM)) * (ELEM / NBR)
    for a in range(bd):
        lanes = slice(a * BLOCK, (a + 1) * BLOCK)
        offs = [d_ref[d, :, lanes] for d in range(3)]
        nk = d_ref[3, :, lanes]
        r2 = offs[0] * offs[0] + offs[1] * offs[1] + offs[2] * offs[2]
        u = 1.0 - r2 * (1.0 / cutoff_sq)
        s1 = jnp.zeros_like(r2)
        s2 = jnp.zeros_like(r2)
        for k in range(RAD):
            sel = jnp.zeros_like(r2)
            for e in range(ELEM):
                sel = jnp.where(nk == e, f_ref[e * RAD + k:e * RAD + k + 1, lanes], sel)
            term = sel * jnp.exp(-RATES[k] * r2)
            s1 = s1 + term
            s2 = s2 + RATES[k] * term
        grad = -u * ((2.0 / cutoff_sq) * s1 + u * s2)
        for d in range(3):
            push_ref[d, :, lanes] = 2.0 * grad * offs[d]


def fold(vals):
    return jnp.sum(vals.reshape(BLOCK // 8, 8, BLOCK), axis=0)


def solve_kernel(pow2, nd, bd, nb, stored, me_ref, row_ref, col_ref, count_ref, hard_ref, g_ref,
                 x_ref, push_ref, nbr_ref, charge_ref, part_ref, r_ref, p_ref, y_ref, s_ref,
                 c_ref, t_ref):
    me = me_ref[0]
    pairs = count_ref[0]
    own_lo = count_ref[1]
    own_hi = count_ref[2]
    sub = lax.broadcasted_iota(jnp.int32, (BLOCK, BLOCK), 0)
    ident = sub == lax.broadcasted_iota(jnp.int32, (BLOCK, BLOCK), 1)

    p_ref[...] = jnp.zeros_like(p_ref)
    r_ref[nb] = jnp.zeros((8, BLOCK), jnp.float32)
    hards = []
    for q in range(nd):
        at = piece_of(q, me, pow2)
        span = slice(q * bd, (q + 1) * bd)
        p_ref[span, :] = -x_ref[at]
        hards.append(pick(g_ref[at, 3 * bd:4 * bd, :], [hard_ref[e] for e in range(ELEM)]))
        for r in range(bd):
            for d in range(3):
                r_ref[q * bd + r, d:d + 1, :] = g_ref[at, d * bd + r:d * bd + r + 1, :]
    hard = jnp.concatenate(hards, axis=0)

    def centre(b):
        return [jnp.broadcast_to(r_ref[b, d:d + 1, 0:1], (1, BLOCK)) for d in range(3)]

    def relative(b, mid):
        rows = [r_ref[b, d:d + 1, :] - mid[d] for d in range(3)]
        size = rows[0] * rows[0] + rows[1] * rows[1] + rows[2] * rows[2]
        return rows, size * -SCALE

    def make_cols(b):
        rows, size = relative(b, centre(b))
        return [column(row * (2.0 * SCALE)) for row in rows] + [column(size - 1.0)]

    def cols_of(b):
        if stored:
            return [c_ref[d, b] for d in range(4)]
        return make_cols(b)

    def charge_col(b):
        return c_ref[4, b] if stored else column(p_ref[pl.ds(b, 1), :])

    def fill_charges(b, carry):
        c_ref[4, b] = column(p_ref[pl.ds(b, 1), :])
        return carry

    def fill_all(b, carry):
        cols = make_cols(b)
        for d in range(4):
            c_ref[d, b] = cols[d]
        return fill_charges(b, carry)

    def gamma(j, i):
        rows, size = relative(i, centre(j))
        cols = cols_of(j)
        power = cols[3] + size
        for d in range(3):
            power = power + cols[d] * rows[d]
        return jnp.exp2(power)

    def entry(t, j, i):
        if stored:
            return t_ref[t]
        val = gamma(j, i)
        return jnp.where(ident & (j == i), 0.0, val)

    if stored:
        lax.fori_loop(0, nb, fill_all, 0, unroll=2)

    def first_diag(b, carry):
        val = jnp.where(ident, 0.0, gamma(b, b))
        if stored:
            t_ref[b] = val
        s_ref[b] = fold(val)
        y_ref[b] = fold(val * charge_col(b))
        return carry

    lax.fori_loop(0, nb, first_diag, 0, unroll=2)

    def first_pair(e, carry):
        ends = (row_ref[e], col_ref[e])
        for side in range(2):
            j, i = ends[side], ends[1 - side]
            val = gamma(j, i)
            if stored:
                t_ref[nb + 2 * e + side] = val
            s_ref[i] = s_ref[i] + fold(val)
            y_ref[i] = y_ref[i] + fold(val * charge_col(j))
        return carry

    lax.fori_loop(0, pairs, first_pair, 0)

    def gathered(ref):
        return jnp.sum(ref[0:nb], axis=1)

    diag = hard + gathered(s_ref)

    def matvec():
        if stored:
            lax.fori_loop(0, nb, fill_charges, 0, unroll=4)

        def diag_part(b, carry):
            y_ref[b] = fold(entry(b, b, b) * charge_col(b))
            return carry

        lax.fori_loop(0, nb, diag_part, 0, unroll=4)

        def pair_part(e, carry):
            ends = (row_ref[e], col_ref[e])
            for side in range(2):
                j, i = ends[side], ends[1 - side]
                y_ref[i] = y_ref[i] + fold(entry(nb + 2 * e + side, j, i) * charge_col(j))
            return carry

        lax.fori_loop(0, pairs, pair_part, 0)

    def total(vals):
        return jnp.sum(jnp.sum(vals, axis=0, keepdims=True), axis=1, keepdims=True)

    res = p_ref[0:nb]
    p = res
    x = jnp.zeros_like(res)
    rho = total(res * res)
    for it in range(ITERS):
        if it:
            matvec()
        image = diag * p + gathered(y_ref)
        step = rho / total(p * image)
        x = x + step * p
        if it + 1 < ITERS:
            res = res - step * image
            rho2 = total(res * res)
            p = res + (rho2 / rho) * p
            rho = rho2
            p_ref[0:nb] = p
    p_ref[0:nb] = x
    for a in range(bd):
        charge_ref[a:a + 1, :] = p_ref[pl.ds(me * bd + a, 1), :]
    mine = jnp.concatenate([charge_ref[a:a + 1, :] for a in range(bd)], axis=1)
    width = bd * BLOCK

    def scatter(s, acc):
        idx = nbr_ref[pl.ds(s, 1), :]
        hit = lax.broadcasted_iota(jnp.int32, (nb, width), 0) == (idx >> 7)
        spot = lax.broadcasted_iota(jnp.int32, (BLOCK, width), 0) == (idx & 127)
        ones = jnp.where(spot, 1.0, 0.0).astype(jnp.bfloat16)
        upper = []
        lower = []
        for d in range(3):
            val = push_ref[d, pl.ds(s, 1), :] * mine
            top = val.astype(jnp.bfloat16).astype(jnp.float32)
            upper.append(jnp.where(hit, top, 0.0).astype(jnp.bfloat16))
            lower.append(jnp.where(hit, val - top, 0.0).astype(jnp.bfloat16))
        both = jnp.concatenate(upper + lower, axis=0)
        return acc + lax.dot_general(both, ones, (((1,), (1,)), ((), ())),
                                     preferred_element_type=jnp.float32)

    acc = lax.fori_loop(0, NBR, scatter, jnp.zeros((6 * nb, BLOCK), jnp.float32), unroll=2)
    acc = acc[:3 * nb] + acc[3 * nb:]
    for q in range(nd):
        for d in range(3):
            part_ref[q, d * bd:(d + 1) * bd, :] = acc[d * nb + q * bd:d * nb + (q + 1) * bd]

    def push_on(t, j, i):
        both = charge_col(j) + p_ref[pl.ds(i, 1), :]
        weight = entry(t, j, i) * (both * both)
        cols = cols_of(j)
        rows, _ = relative(i, centre(j))
        whole = jnp.sum(weight, axis=0, keepdims=True)
        for d in range(3):
            moment = jnp.sum(weight * cols[d], axis=0, keepdims=True) * (0.5 / SCALE)
            at = (i // bd, pl.ds(d * bd + i % bd, 1), slice(None))
            part_ref[at] = part_ref[at] + (rows[d] * whole - moment) * (0.5 / sigma_sq)

    if stored:
        for a in range(bd):
            fill_charges(me * bd + a, 0)
    for a in range(bd):
        b = me * bd + a
        push_on(b, b, b)
        lanes = slice(a * BLOCK, (a + 1) * BLOCK)
        for d in range(3):
            away = jnp.sum(push_ref[d, :, lanes], axis=0, keepdims=True) * charge_ref[a:a + 1, :]
            at = (me, slice(d * bd + a, d * bd + a + 1), slice(None))
            part_ref[at] = part_ref[at] - away

    def pair_force(e, carry):
        ends = (row_ref[e], col_ref[e])
        if stored:
            fill_charges(ends[1], 0)
        for side in range(2):
            push_on(nb + 2 * e + side, ends[side], ends[1 - side])
        return carry

    lax.fori_loop(own_lo, own_hi, pair_force, 0)


def gather_all(own, n):
    if n & (n - 1):
        return lax.all_gather(own, "blk"), False
    got = own[None]
    step = 1
    while step < n:
        other = lax.ppermute(got, "blk", [(i, i ^ step) for i in range(n)])
        got = jnp.concatenate([got, other], axis=0)
        step *= 2
    return got, True


def live_pairs(rows, cols, place):
    slots = rows.shape[1]
    rows = rows.reshape(-1)
    cols = cols.reshape(-1)
    cross = (rows >= 0) & (rows != cols)
    ids = jnp.arange(rows.shape[0], dtype=jnp.int32)
    before = cross[None, :] & (ids[None, :] < ids[:, None])
    rank = jnp.sum(before.astype(jnp.int32), axis=1)
    hit = cross[:, None] & (rank[:, None] == ids[None, :])
    order = [jnp.sum(jnp.where(hit, ends[:, None], 0), axis=0) for ends in (rows, cols)]
    owner = ids // slots
    counts = [cross, cross & (owner < place), cross & (owner <= place)]
    return order, jnp.stack([jnp.sum(c.astype(jnp.int32)) for c in counts])


def on_device(positions, species, neighbors, pair_lists, hardness, w_first, b_first, w_second,
              b_second, w_out, b_out):
    n = lax.axis_size("blk")
    me = lax.axis_index("blk")
    atoms = positions.shape[1]
    bd = atoms // BLOCK
    nb = bd * n
    slots = pair_lists.shape[1]
    hid = w_first.shape[1]
    f32 = jnp.float32
    kind = species.reshape(1, atoms)
    small = pltpu.CompilerParams(vmem_limit_bytes=24 << 20)
    own = pl.pallas_call(
        pack_kernel, out_shape=jax.ShapeDtypeStruct((PACK, BLOCK), f32),
        in_specs=[spec(VM)] * 3, out_specs=spec(VM), compiler_params=small, name="pack",
    )(positions, kind, pair_lists)
    whole, pow2 = gather_all(own, n)
    staged = (neighbors, w_first, b_first, w_second, b_second, w_out)
    chi, offs, hidden = pl.pallas_call(
        functools.partial(chi_kernel, pow2, n, bd),
        out_shape=(jax.ShapeDtypeStruct((bd, BLOCK), f32),
                   jax.ShapeDtypeStruct((4, NBR, atoms), f32),
                   jax.ShapeDtypeStruct((2, hid, atoms), f32)),
        in_specs=[spec(SM)] + [spec(VM)] * 9 + [spec(SM)],
        out_specs=(spec(VM),) * 3,
        scratch_shapes=[VM((DESC, atoms), f32)],
        compiler_params=small,
        name="chi",
    )(me[None], whole, positions, staged[0], kind, *staged[1:], b_out)
    all_chi, _ = gather_all(chi, n)
    lists = whole[:, 4 * bd:4 * bd + 2, :slots].astype(jnp.int32)
    (rows, cols), counts = live_pairs(lists[:, 0], lists[:, 1], 0 if pow2 else me)
    push = pl.pallas_call(
        functools.partial(pull_kernel, bd),
        out_shape=jax.ShapeDtypeStruct((3, NBR, atoms), f32),
        in_specs=[spec(VM)] * 6,
        out_specs=spec(VM),
        scratch_shapes=[VM((DESC, atoms), f32)],
        compiler_params=small,
        name="pull",
    )(kind, offs, hidden, staged[1], staged[3], staged[5])
    entries = nb + 2 * (n * slots - nb)
    stored = entries * BLOCK * BLOCK * 4 <= STORE_LIMIT
    charges, part = pl.pallas_call(
        functools.partial(solve_kernel, pow2, n, bd, nb, stored),
        out_shape=(jax.ShapeDtypeStruct((bd, BLOCK), f32),
                   jax.ShapeDtypeStruct((n, 3 * bd, BLOCK), f32)),
        in_specs=[spec(SM)] * 5 + [spec(VM)] * 4,
        out_specs=(spec(VM),) * 2,
        scratch_shapes=[VM((nb + 1, 8, BLOCK), f32), VM((nb + 8, BLOCK), f32),
                        VM((nb + 1, 8, BLOCK), f32), VM((nb + 1, 8, BLOCK), f32),
                        VM((5, nb, BLOCK, BLOCK) if stored else (8, BLOCK), f32),
                        VM((entries, BLOCK, BLOCK) if stored else (8, BLOCK), f32)],
        compiler_params=pltpu.CompilerParams(vmem_limit_bytes=58 << 20),
        name="solve",
    )(me[None], rows, cols, counts, hardness, whole, all_chi, push, neighbors)
    swapped = lax.all_to_all(part, "blk", 0, 0)
    forces = jnp.sum(swapped, axis=0)
    return charges.reshape(atoms), forces.reshape(3, atoms)


def solution(mesh):
    both = ("cell", "blk")
    placed = (P(None, both), P(both), P(None, both), P(None, both)) + (P(),) * 7
    return jax.shard_map(
        on_device,
        mesh=mesh,
        in_specs=placed,
        out_specs=(P(both), P(None, both)),
        check_vma=False,
    )
```

```python
import functools
import math

import jax
import jax.numpy as jnp
import numpy as np
from jax import lax
from jax.experimental import pallas as pl
from jax.experimental.pallas import tpu as pltpu
from jax.sharding import PartitionSpec as P

ELEM = 4
RAD = 16
DESC = ELEM * RAD
BLOCK = 128
NBR = 32
ITERS = 3
PACK = 24
STORE_LIMIT = 36 << 20

coulomb_scale = 0.5
sigma_sq = 4.0
cutoff_sq = 49.0
highest = lax.Precision.HIGHEST
RATES = [0.005 * 200.0 ** (k / (RAD - 1)) for k in range(RAD)]
VM = pltpu.VMEM
SM = pltpu.SMEM
SCALE = math.log2(math.e) / (2.0 * sigma_sq)


def spec(space):
    return pl.BlockSpec(memory_space=space)


def piece_of(q, me, pow2):
    return q ^ me if pow2 else q


def dot(a, b, lhs=1):
    return lax.dot_general(a, b, (((lhs,), (0,)), ((), ())), precision=highest,
                           preferred_element_type=jnp.float32)


def column(row):
    return jnp.broadcast_to(row, (BLOCK, BLOCK)).T


def pick(kind, mats):
    out = jnp.where(kind == 0, mats[0], 0.0)
    for e in range(1, ELEM):
        out = jnp.where(kind == e, mats[e], out)
    return out


def one_hot(kind):
    ids = lax.broadcasted_iota(jnp.int32, (ELEM, kind.shape[1]), 0)
    return jnp.where(ids == kind, 1.0, 0.0)


def pack_kernel(pos_ref, kind_ref, pairs_ref, own_ref):
    bd = pos_ref.shape[1] // BLOCK
    own_ref[...] = jnp.zeros_like(own_ref)
    for a in range(bd):
        lanes = slice(a * BLOCK, (a + 1) * BLOCK)
        for d in range(3):
            own_ref[d * bd + a:d * bd + a + 1, :] = pos_ref[d:d + 1, lanes]
        own_ref[3 * bd + a:3 * bd + a + 1, :] = kind_ref[:, lanes].astype(jnp.float32)
    slots = pairs_ref.shape[1]
    for side in range(2):
        own_ref[4 * bd + side:4 * bd + side + 1, :slots] = (
            pairs_ref[side:side + 1, :].astype(jnp.float32))


def chi_kernel(pow2, nd, bd, me_ref, g_ref, pos_ref, nbr_ref, kind_ref, w1, b1, w2, b2, wo, bo,
               chi_ref, d_ref, h_ref, f_ref):
    me = me_ref[0]
    chunk = min(nd, 8)
    for a in range(bd):
        lanes = slice(a * BLOCK, (a + 1) * BLOCK)

        def group(g, carry):
            rows8 = pl.ds(pl.multiple_of(g * 8, 8), 8)
            idx = nbr_ref[rows8, lanes]
            hi = idx >> 7
            lo = idx & 127

            def look(part, vals):
                for step in range(chunk):
                    q = part * chunk + step
                    at = piece_of(q, me, pow2)
                    for r in range(bd):
                        hit = hi == q * bd + r
                        new = []
                        for d in range(4):
                            row = jnp.broadcast_to(g_ref[at, d * bd + r:d * bd + r + 1, :],
                                                   (8, BLOCK))
                            new.append(jnp.where(hit, jnp.take_along_axis(row, lo, axis=1),
                                                 vals[d]))
                        vals = tuple(new)
                return vals

            vals = (jnp.zeros((8, BLOCK), jnp.float32),) * 4
            if nd == chunk:
                vals = look(0, vals)
            else:
                vals = lax.fori_loop(0, nd // chunk, look, vals)
            live = idx >= 0
            for d in range(3):
                d_ref[d, rows8, lanes] = jnp.where(live, pos_ref[d:d + 1, lanes] - vals[d], 0.0)
            d_ref[3, rows8, lanes] = jnp.where(live, vals[3], -1.0)
            return carry

        lax.fori_loop(0, NBR // 8, group, 0)
        offs = [d_ref[d, :, lanes] for d in range(3)]
        nk = d_ref[3, :, lanes]
        r2 = offs[0] * offs[0] + offs[1] * offs[1] + offs[2] * offs[2]
        u = 1.0 - r2 * (1.0 / cutoff_sq)
        shell = u * u * (ELEM / NBR)
        for k in range(RAD):
            val = shell * jnp.exp(-RATES[k] * r2)
            for e in range(ELEM):
                f_ref[e * RAD + k:e * RAD + k + 1, lanes] = jnp.sum(
                    jnp.where(nk == e, val, 0.0), axis=0, keepdims=True)
    kind = kind_ref[...]
    hot = one_hot(kind)
    feats = f_ref[...]
    h1 = jnp.tanh(pick(kind, [dot(w1[e], feats) for e in range(ELEM)]) + dot(b1[...], hot, 0))
    h2 = jnp.tanh(pick(kind, [dot(w2[e], h1) for e in range(ELEM)]) + dot(b2[...], hot, 0))
    h_ref[0] = h1
    h_ref[1] = h2
    bsel = pick(kind, [bo[e] for e in range(ELEM)])
    chi = jnp.sum(dot(wo[...], hot, 0) * h2, axis=0, keepdims=True) + bsel
    for a in range(bd):
        chi_ref[a:a + 1, :] = chi[:, a * BLOCK:(a + 1) * BLOCK]


def pull_kernel(bd, kind_ref, d_ref, h_ref, w1, w2, wo, push_ref, f_ref):
    kind = kind_ref[...]
    h1 = h_ref[0]
    h2 = h_ref[1]
    pre2 = dot(wo[...], one_hot(kind), 0) * (1.0 - h2 * h2)
    pre1 = sum(dot(w2[e], jnp.where(kind == e, pre2, 0.0), 0) for e in range(ELEM))
    pre1 = pre1 * (1.0 - h1 * h1)
    f_ref[...] = sum(dot(w1[e], jnp.where(kind == e, pre1, 0.0), 0)
                     for e in range(ELEM)) * (ELEM / NBR)
    for a in range(bd):
        lanes = slice(a * BLOCK, (a + 1) * BLOCK)
        offs = [d_ref[d, :, lanes] for d in range(3)]
        nk = d_ref[3, :, lanes]
        r2 = offs[0] * offs[0] + offs[1] * offs[1] + offs[2] * offs[2]
        u = 1.0 - r2 * (1.0 / cutoff_sq)
        s1 = jnp.zeros_like(r2)
        s2 = jnp.zeros_like(r2)
        for k in range(RAD):
            sel = jnp.zeros_like(r2)
            for e in range(ELEM):
                sel = jnp.where(nk == e, f_ref[e * RAD + k:e * RAD + k + 1, lanes], sel)
            term = sel * jnp.exp(-RATES[k] * r2)
            s1 = s1 + term
            s2 = s2 + RATES[k] * term
        grad = -u * ((2.0 / cutoff_sq) * s1 + u * s2)
        for d in range(3):
            push_ref[d, :, lanes] = 2.0 * grad * offs[d]


def fold(vals):
    tiles = vals.reshape(BLOCK // 8, 8, BLOCK)
    terms = [tiles[k] for k in range(BLOCK // 8)]
    while len(terms) > 1:
        terms = [terms[k] + terms[k + 1] for k in range(0, len(terms), 2)]
    return terms[0]


def split3(vals):
    parts = []
    for _ in range(3):
        top = vals.astype(jnp.bfloat16).astype(jnp.float32)
        parts.append(top)
        vals = vals - top
    return parts


def solve_kernel(pow2, nd, bd, nb, slots, stored, me_ref, pair_ref, count_ref, hard_ref, g_ref,
                 x_ref, push_ref, nbr_ref, charge_ref, part_ref, r_ref, mid_ref, a_ref, p_ref,
                 pc_ref, y_ref, s_ref, t_ref):
    me = me_ref[0]
    cross = slots - bd
    sub = lax.broadcasted_iota(jnp.int32, (BLOCK, BLOCK), 0)
    ident = sub == lax.broadcasted_iota(jnp.int32, (BLOCK, BLOCK), 1)
    sub8 = lax.broadcasted_iota(jnp.int32, (8, BLOCK), 0)

    r_ref[...] = jnp.zeros_like(r_ref)
    p_ref[...] = jnp.zeros_like(p_ref)
    hards = []
    for q in range(nd):
        at = piece_of(q, me, pow2)
        span = slice(q * bd, (q + 1) * bd)
        p_ref[span, :] = -x_ref[at]
        hards.append(pick(g_ref[at, 3 * bd:4 * bd, :], [hard_ref[e] for e in range(ELEM)]))
        for r in range(bd):
            for d in range(3):
                r_ref[q * bd + r, d:d + 1, :] = g_ref[at, d * bd + r:d * bd + r + 1, :]
    hard = jnp.concatenate(hards, axis=0)

    def set_block(b, carry):
        mid = jnp.broadcast_to(r_ref[b][:, 0:1], (8, BLOCK))
        mid_ref[b] = mid
        rel = r_ref[b] - mid
        size = jnp.sum(rel * rel, axis=0, keepdims=True)
        tile = jnp.where(sub8 == 3, 1.0,
                         jnp.where(sub8 == 4, size * -SCALE - 1.0, rel * (2.0 * SCALE)))
        q1, q2, q3 = split3(tile)
        a_ref[b] = jnp.concatenate([q1, q1, q2, q1, q3, q2], axis=0).T.astype(jnp.bfloat16)
        return set_charge(b, carry)

    def set_charge(b, carry):
        pc_ref[b] = column(p_ref[pl.ds(b, 1), :])
        return carry

    lax.fori_loop(0, nb + 1, set_block, 0, unroll=3)

    def gamma(j, i):
        rel = r_ref[i] - mid_ref[j]
        size = jnp.sum(rel * rel, axis=0, keepdims=True)
        tile = jnp.where(sub8 == 3, size * -SCALE, jnp.where(sub8 == 4, 1.0, rel))
        p1, p2, p3 = split3(tile)
        right = jnp.concatenate([p1, p2, p1, p3, p1, p2], axis=0).astype(jnp.bfloat16)
        return jnp.exp2(jnp.dot(a_ref[j], right, preferred_element_type=jnp.float32))

    def own_gamma(b):
        return jnp.where(ident, 0.0, gamma(b, b))

    def entry(t, j, i):
        return t_ref[t] if stored else gamma(j, i)

    def own_entry(b):
        return t_ref[b] if stored else own_gamma(b)

    def over_pairs(step):
        def piece(q, carry):
            def two(k, inner):
                ends = []
                for m in range(2):
                    e = bd + 2 * k + m
                    left, right = pair_ref[q, 0, e], pair_ref[q, 1, e]
                    t = nb + 2 * (q * cross + 2 * k + m)
                    ends += [(t, left, right), (t + 1, right, left)]
                step(ends)
                return inner

            return lax.fori_loop(0, (count_ref[q] - bd + 1) // 2, two, carry)

        lax.fori_loop(0, nd, piece, 0)

    def first_diag(b, carry):
        val = own_gamma(b)
        if stored:
            t_ref[b] = val
        s_ref[b] = fold(val)
        y_ref[b] = fold(val * pc_ref[b])
        return carry

    lax.fori_loop(0, nb, first_diag, 0, unroll=2)

    def first_step(ends):
        found = []
        for t, j, i in ends:
            val = gamma(j, i)
            if stored:
                t_ref[t] = val
            found.append((i, fold(val), fold(val * pc_ref[j])))
        for i, one, two in found:
            s_ref[i] = s_ref[i] + one
            y_ref[i] = y_ref[i] + two

    over_pairs(first_step)

    def gathered(ref):
        return jnp.sum(ref[0:nb], axis=1)

    diag = hard + gathered(s_ref)

    def next_step(ends):
        found = [(i, fold(entry(t, j, i) * pc_ref[j])) for t, j, i in ends]
        for i, one in found:
            y_ref[i] = y_ref[i] + one

    def next_diag(b, carry):
        y_ref[b] = fold(own_entry(b) * pc_ref[b])
        return carry

    def matvec():
        lax.fori_loop(0, nb, set_charge, 0, unroll=4)
        lax.fori_loop(0, nb, next_diag, 0, unroll=4)
        over_pairs(next_step)

    def total(vals):
        return jnp.sum(jnp.sum(vals, axis=0, keepdims=True), axis=1, keepdims=True)

    res = p_ref[0:nb]
    p = res
    x = jnp.zeros_like(res)
    rho = total(res * res)
    for it in range(ITERS):
        if it:
            matvec()
        image = diag * p + gathered(y_ref)
        step = rho / total(p * image)
        x = x + step * p
        if it + 1 < ITERS:
            res = res - step * image
            rho2 = total(res * res)
            p = res + (rho2 / rho) * p
            rho = rho2
            p_ref[0:nb] = p
    p_ref[0:nb] = x
    for a in range(bd):
        charge_ref[a:a + 1, :] = p_ref[pl.ds(me * bd + a, 1), :]
        set_charge(me * bd + a, 0)
    mine = jnp.concatenate([charge_ref[a:a + 1, :] for a in range(bd)], axis=1)
    width = bd * BLOCK

    def scatter(s, acc):
        idx = nbr_ref[pl.ds(s, 1), :]
        hit = lax.broadcasted_iota(jnp.int32, (nb, width), 0) == (idx >> 7)
        spot = lax.broadcasted_iota(jnp.int32, (BLOCK, width), 0) == (idx & 127)
        ones = jnp.where(spot, 1.0, 0.0).astype(jnp.bfloat16)
        upper = []
        lower = []
        for d in range(3):
            val = push_ref[d, pl.ds(s, 1), :] * mine
            top = val.astype(jnp.bfloat16).astype(jnp.float32)
            upper.append(jnp.where(hit, top, 0.0).astype(jnp.bfloat16))
            lower.append(jnp.where(hit, val - top, 0.0).astype(jnp.bfloat16))
        both = jnp.concatenate(upper + lower, axis=0)
        return acc + lax.dot_general(both, ones, (((1,), (1,)), ((), ())),
                                     preferred_element_type=jnp.float32)

    acc = lax.fori_loop(0, NBR, scatter, jnp.zeros((6 * nb, BLOCK), jnp.float32), unroll=2)
    acc = acc[:3 * nb] + acc[3 * nb:]
    for q in range(nd):
        for d in range(3):
            part_ref[q, d * bd:(d + 1) * bd, :] = acc[d * nb + q * bd:d * nb + (q + 1) * bd]

    def moments(rel, weights, side):
        tile = jnp.where(sub8 == 3, 1.0, rel)
        rows = jnp.concatenate(split3(tile) + [jnp.zeros_like(rel)], axis=0).astype(jnp.bfloat16)
        out = sum(lax.dot_general(rows, w, (((1,), (side,)), ((), ())),
                                  preferred_element_type=jnp.float32) for w in weights)
        return out[0:8] + out[8:16] + out[16:24]

    def add_force(b, rel, found):
        force = (rel * found[3:4] - found) * (0.5 / sigma_sq)
        for d in range(3):
            at = (b // bd, pl.ds(d * bd + b % bd, 1), slice(None))
            part_ref[at] = part_ref[at] + force[d:d + 1]

    def weigh(val, j, i):
        both = pc_ref[j] + p_ref[pl.ds(i, 1), :]
        weight = val * (both * both)
        top = weight.astype(jnp.bfloat16)
        return top, (weight - top.astype(jnp.float32)).astype(jnp.bfloat16)

    for a in range(bd):
        b = me * bd + a
        rel = r_ref[b] - mid_ref[b]
        add_force(b, rel, moments(rel, weigh(own_entry(b), b, b), 0))
        lanes = slice(a * BLOCK, (a + 1) * BLOCK)
        for d in range(3):
            away = jnp.sum(push_ref[d, :, lanes], axis=0, keepdims=True) * charge_ref[a:a + 1, :]
            at = (me, slice(d * bd + a, d * bd + a + 1), slice(None))
            part_ref[at] = part_ref[at] - away
    piece = piece_of(me, me, pow2)

    def pair_force(e, carry):
        j, i = pair_ref[piece, 0, bd + e], pair_ref[piece, 1, bd + e]
        mid = mid_ref[j]
        rel_j = r_ref[j] - mid
        rel_i = r_ref[i] - mid
        weights = weigh(entry(nb + 2 * (piece * cross + e), j, i), j, i)
        add_force(i, rel_i, moments(rel_j, weights, 0))
        add_force(j, rel_j, moments(rel_i, weights, 1))
        return carry

    lax.fori_loop(0, count_ref[piece] - bd, pair_force, 0)


def gather_all(own, n):
    if n & (n - 1):
        return lax.all_gather(own, "blk"), False
    got = own[None]
    step = 1
    while step < n:
        other = lax.ppermute(got, "blk", [(i, i ^ step) for i in range(n)])
        got = jnp.concatenate([got, other], axis=0)
        step *= 2
    return got, True


def on_device(positions, species, neighbors, pair_lists, hardness, w_first, b_first, w_second,
              b_second, w_out, b_out):
    n = lax.axis_size("blk")
    me = lax.axis_index("blk")
    atoms = positions.shape[1]
    bd = atoms // BLOCK
    nb = bd * n
    slots = pair_lists.shape[1]
    hid = w_first.shape[1]
    f32 = jnp.float32
    kind = species.reshape(1, atoms)
    small = pltpu.CompilerParams(vmem_limit_bytes=24 << 20)
    own = pl.pallas_call(
        pack_kernel, out_shape=jax.ShapeDtypeStruct((PACK, BLOCK), f32),
        in_specs=[spec(VM)] * 3, out_specs=spec(VM), compiler_params=small, name="pack",
    )(positions, kind, pair_lists)
    whole, pow2 = gather_all(own, n)
    staged = (neighbors, w_first, b_first, w_second, b_second, w_out)
    chi, offs, hidden = pl.pallas_call(
        functools.partial(chi_kernel, pow2, n, bd),
        out_shape=(jax.ShapeDtypeStruct((bd, BLOCK), f32),
                   jax.ShapeDtypeStruct((4, NBR, atoms), f32),
                   jax.ShapeDtypeStruct((2, hid, atoms), f32)),
        in_specs=[spec(SM)] + [spec(VM)] * 9 + [spec(SM)],
        out_specs=(spec(VM),) * 3,
        scratch_shapes=[VM((DESC, atoms), f32)],
        compiler_params=small,
        name="chi",
    )(me[None], whole, positions, staged[0], kind, *staged[1:], b_out)
    all_chi, _ = gather_all(chi, n)
    lists = whole[:, 4 * bd:4 * bd + 2, :slots].astype(jnp.int32)
    counts = jnp.sum((lists[:, 0] >= 0).astype(jnp.int32), axis=1)
    lists = jnp.where(lists < 0, nb, lists)
    push = pl.pallas_call(
        functools.partial(pull_kernel, bd),
        out_shape=jax.ShapeDtypeStruct((3, NBR, atoms), f32),
        in_specs=[spec(VM)] * 6,
        out_specs=spec(VM),
        scratch_shapes=[VM((DESC, atoms), f32)],
        compiler_params=small,
        name="pull",
    )(kind, offs, hidden, staged[1], staged[3], staged[5])
    entries = nb + 2 * (n * slots - nb)
    stored = entries * BLOCK * BLOCK * 4 <= STORE_LIMIT
    charges, part = pl.pallas_call(
        functools.partial(solve_kernel, pow2, n, bd, nb, slots, stored),
        out_shape=(jax.ShapeDtypeStruct((bd, BLOCK), f32),
                   jax.ShapeDtypeStruct((n, 3 * bd, BLOCK), f32)),
        in_specs=[spec(SM)] * 4 + [spec(VM)] * 4,
        out_specs=(spec(VM),) * 2,
        scratch_shapes=[VM((nb + 1, 8, BLOCK), f32), VM((nb + 1, 8, BLOCK), f32),
                        VM((nb + 1, BLOCK, 48), jnp.bfloat16), VM((nb + 8, BLOCK), f32),
                        VM((nb + 1, BLOCK, BLOCK), f32), VM((nb + 1, 8, BLOCK), f32),
                        VM((nb + 1, 8, BLOCK), f32),
                        VM((entries if stored else 1, BLOCK, BLOCK), f32)],
        compiler_params=pltpu.CompilerParams(vmem_limit_bytes=58 << 20),
        name="solve",
    )(me[None], lists, counts, hardness, whole, all_chi, push, neighbors)
    swapped = lax.all_to_all(part, "blk", 0, 0)
    forces = jnp.sum(swapped, axis=0)
    return charges.reshape(atoms), forces.reshape(3, atoms)


def solution(mesh):
    both = ("cell", "blk")
    placed = (P(None, both), P(both), P(None, both), P(None, both)) + (P(),) * 7
    return jax.shard_map(
        on_device,
        mesh=mesh,
        in_specs=placed,
        out_specs=(P(both), P(None, both)),
        check_vma=False,
    )
```

```python
import functools
import math

import jax
import jax.numpy as jnp
import numpy as np
from jax import lax
from jax.experimental import pallas as pl
from jax.experimental.pallas import tpu as pltpu
from jax.sharding import PartitionSpec as P

ELEM = 4
RAD = 16
DESC = ELEM * RAD
BLOCK = 128
NBR = 32
ITERS = 3
PACK = 24
STORE_LIMIT = 36 << 20

coulomb_scale = 0.5
sigma_sq = 4.0
cutoff_sq = 49.0
highest = lax.Precision.HIGHEST
RATES = [0.005 * 200.0 ** (k / (RAD - 1)) for k in range(RAD)]
VM = pltpu.VMEM
SM = pltpu.SMEM
SCALE = math.log2(math.e) / (2.0 * sigma_sq)


def spec(space):
    return pl.BlockSpec(memory_space=space)


def piece_of(q, me, pow2):
    return q ^ me if pow2 else q


def dot(a, b, lhs=1):
    return lax.dot_general(a, b, (((lhs,), (0,)), ((), ())), precision=highest,
                           preferred_element_type=jnp.float32)


def column(row):
    return jnp.broadcast_to(row, (BLOCK, BLOCK)).T


def pick(kind, mats):
    out = jnp.where(kind == 0, mats[0], 0.0)
    for e in range(1, ELEM):
        out = jnp.where(kind == e, mats[e], out)
    return out


def one_hot(kind):
    ids = lax.broadcasted_iota(jnp.int32, (ELEM, kind.shape[1]), 0)
    return jnp.where(ids == kind, 1.0, 0.0)


def pack_kernel(pos_ref, kind_ref, pairs_ref, own_ref):
    bd = pos_ref.shape[1] // BLOCK
    own_ref[...] = jnp.zeros_like(own_ref)
    for a in range(bd):
        lanes = slice(a * BLOCK, (a + 1) * BLOCK)
        for d in range(3):
            own_ref[d * bd + a:d * bd + a + 1, :] = pos_ref[d:d + 1, lanes]
        own_ref[3 * bd + a:3 * bd + a + 1, :] = kind_ref[:, lanes].astype(jnp.float32)
    slots = pairs_ref.shape[1]
    for side in range(2):
        own_ref[4 * bd + side:4 * bd + side + 1, :slots] = (
            pairs_ref[side:side + 1, :].astype(jnp.float32))


def join_pieces(pieces, out_ref):
    first = 0
    for piece in pieces:
        count = piece.shape[0]
        out_ref[first:first + count] = piece[...]
        first += count


def chi_kernel(pow2, nd, bd, parts, me_ref, *refs):
    pieces = refs[:parts]
    (pos_ref, nbr_ref, kind_ref, w1, b1, w2, b2, wo, bo,
     chi_ref, d_ref, h_ref, g_ref, f_ref) = refs[parts:]
    me = me_ref[0]
    chunk = min(nd, 8)
    join_pieces(pieces, g_ref)
    for a in range(bd):
        lanes = slice(a * BLOCK, (a + 1) * BLOCK)

        def group(g, carry):
            rows8 = pl.ds(pl.multiple_of(g * 8, 8), 8)
            idx = nbr_ref[rows8, lanes]
            hi = idx >> 7
            lo = idx & 127

            def look(part, vals):
                for step in range(chunk):
                    q = part * chunk + step
                    at = piece_of(q, me, pow2)
                    for r in range(bd):
                        hit = hi == q * bd + r
                        new = []
                        for d in range(4):
                            row = jnp.broadcast_to(g_ref[at, d * bd + r:d * bd + r + 1, :],
                                                   (8, BLOCK))
                            new.append(jnp.where(hit, jnp.take_along_axis(row, lo, axis=1),
                                                 vals[d]))
                        vals = tuple(new)
                return vals

            vals = (jnp.zeros((8, BLOCK), jnp.float32),) * 4
            if nd == chunk:
                vals = look(0, vals)
            else:
                vals = lax.fori_loop(0, nd // chunk, look, vals)
            live = idx >= 0
            for d in range(3):
                d_ref[d, rows8, lanes] = jnp.where(live, pos_ref[d:d + 1, lanes] - vals[d], 0.0)
            d_ref[3, rows8, lanes] = jnp.where(live, vals[3], -1.0)
            return carry

        lax.fori_loop(0, NBR // 8, group, 0, unroll=4 if nd == chunk else 1)
        offs = [d_ref[d, :, lanes] for d in range(3)]
        nk = d_ref[3, :, lanes]
        r2 = offs[0] * offs[0] + offs[1] * offs[1] + offs[2] * offs[2]
        u = 1.0 - r2 * (1.0 / cutoff_sq)
        shell = u * u * (ELEM / NBR)
        for k in range(RAD):
            val = shell * jnp.exp(-RATES[k] * r2)
            for e in range(ELEM):
                f_ref[e * RAD + k:e * RAD + k + 1, lanes] = jnp.sum(
                    jnp.where(nk == e, val, 0.0), axis=0, keepdims=True)
    kind = kind_ref[...]
    hot = one_hot(kind)
    feats = f_ref[...]
    h1 = jnp.tanh(pick(kind, [dot(w1[e], feats) for e in range(ELEM)]) + dot(b1[...], hot, 0))
    h2 = jnp.tanh(pick(kind, [dot(w2[e], h1) for e in range(ELEM)]) + dot(b2[...], hot, 0))
    h_ref[0] = h1
    h_ref[1] = h2
    bsel = pick(kind, [bo[e] for e in range(ELEM)])
    chi = jnp.sum(dot(wo[...], hot, 0) * h2, axis=0, keepdims=True) + bsel
    for a in range(bd):
        chi_ref[a:a + 1, :] = chi[:, a * BLOCK:(a + 1) * BLOCK]


def fold(vals):
    tiles = vals.reshape(BLOCK // 8, 8, BLOCK)
    terms = [tiles[k] for k in range(BLOCK // 8)]
    while len(terms) > 1:
        terms = [terms[k] + terms[k + 1] for k in range(0, len(terms), 2)]
    return terms[0]


def split3(vals):
    parts = []
    for _ in range(3):
        top = vals.astype(jnp.bfloat16).astype(jnp.float32)
        parts.append(top)
        vals = vals - top
    return parts


def pull_kernel(pow2, nd, bd, nb, me_ref, g_ref, kind_ref, d_ref, h_ref, w1, w2, wo, push_ref,
                r_ref, mid_ref, a_ref, f_ref):
    me = me_ref[0]
    sub8 = lax.broadcasted_iota(jnp.int32, (8, BLOCK), 0)
    r_ref[...] = jnp.zeros_like(r_ref)
    for q in range(nd):
        at = piece_of(q, me, pow2)
        for r in range(bd):
            for d in range(3):
                r_ref[q * bd + r, d:d + 1, :] = g_ref[at, d * bd + r:d * bd + r + 1, :]

    def set_block(b, carry):
        mid = jnp.broadcast_to(r_ref[b][:, 0:1], (8, BLOCK))
        mid_ref[b] = mid
        rel = r_ref[b] - mid
        size = jnp.sum(rel * rel, axis=0, keepdims=True)
        tile = jnp.where(sub8 == 3, 1.0,
                         jnp.where(sub8 == 4, size * -SCALE - 1.0, rel * (2.0 * SCALE)))
        q1, q2, q3 = split3(tile)
        a_ref[b] = jnp.concatenate([q1, q1, q2, q1, q3, q2], axis=0).T.astype(jnp.bfloat16)
        return carry

    lax.fori_loop(0, nb + 1, set_block, 0, unroll=11 if nb + 1 == 33 else 1)
    kind = kind_ref[...]
    h1 = h_ref[0]
    h2 = h_ref[1]
    pre2 = dot(wo[...], one_hot(kind), 0) * (1.0 - h2 * h2)
    pre1 = sum(dot(w2[e], jnp.where(kind == e, pre2, 0.0), 0) for e in range(ELEM))
    pre1 = pre1 * (1.0 - h1 * h1)
    f_ref[...] = sum(dot(w1[e], jnp.where(kind == e, pre1, 0.0), 0)
                     for e in range(ELEM)) * (ELEM / NBR)
    for a in range(bd):
        lanes = slice(a * BLOCK, (a + 1) * BLOCK)
        offs = [d_ref[d, :, lanes] for d in range(3)]
        nk = d_ref[3, :, lanes]
        r2 = offs[0] * offs[0] + offs[1] * offs[1] + offs[2] * offs[2]
        u = 1.0 - r2 * (1.0 / cutoff_sq)
        s1 = jnp.zeros_like(r2)
        s2 = jnp.zeros_like(r2)
        for k in range(RAD):
            sel = jnp.zeros_like(r2)
            for e in range(ELEM):
                sel = jnp.where(nk == e, f_ref[e * RAD + k:e * RAD + k + 1, lanes], sel)
            term = sel * jnp.exp(-RATES[k] * r2)
            s1 = s1 + term
            s2 = s2 + RATES[k] * term
        grad = -u * ((2.0 / cutoff_sq) * s1 + u * s2)
        for d in range(3):
            push_ref[d, :, lanes] = 2.0 * grad * offs[d]


def solve_kernel(pow2, nd, bd, nb, slots, stored, parts, me_ref, pair_ref, count_ref, hard_ref,
                 *refs):
    pieces = refs[:parts]
    (g_ref, r_ref, mid_ref, a_ref, push_ref, nbr_ref, charge_ref, part_ref, x_ref, p_ref, pc_ref,
     y_ref, s_ref, t_ref) = refs[parts:]
    me = me_ref[0]
    cross = slots - bd
    sub = lax.broadcasted_iota(jnp.int32, (BLOCK, BLOCK), 0)
    ident = sub == lax.broadcasted_iota(jnp.int32, (BLOCK, BLOCK), 1)
    sub8 = lax.broadcasted_iota(jnp.int32, (8, BLOCK), 0)

    join_pieces(pieces, x_ref)
    p_ref[...] = jnp.zeros_like(p_ref)
    hards = []
    for q in range(nd):
        at = piece_of(q, me, pow2)
        span = slice(q * bd, (q + 1) * bd)
        p_ref[span, :] = -x_ref[at]
        hards.append(pick(g_ref[at, 3 * bd:4 * bd, :], [hard_ref[e] for e in range(ELEM)]))
    hard = jnp.concatenate(hards, axis=0)

    def set_charge(b, carry):
        pc_ref[b] = column(p_ref[pl.ds(b, 1), :])
        return carry

    def set_charges():
        if nb > 64:
            lax.fori_loop(0, nb, set_charge, 0)
            return
        turned = p_ref[0:nb].T
        for b in range(nb):
            pc_ref[b] = jnp.broadcast_to(turned[:, b:b + 1], (BLOCK, BLOCK))

    pc_ref[nb] = jnp.zeros((BLOCK, BLOCK), jnp.float32)
    set_charges()

    def gamma(j, i):
        rel = r_ref[i] - mid_ref[j]
        size = jnp.sum(rel * rel, axis=0, keepdims=True)
        tile = jnp.where(sub8 == 3, size * -SCALE, jnp.where(sub8 == 4, 1.0, rel))
        p1, p2, p3 = split3(tile)
        right = jnp.concatenate([p1, p2, p1, p3, p1, p2], axis=0).astype(jnp.bfloat16)
        return jnp.exp2(jnp.dot(a_ref[j], right, preferred_element_type=jnp.float32))

    def own_gamma(b):
        return jnp.where(ident, 0.0, gamma(b, b))

    def entry(t, j, i):
        return t_ref[t] if stored else gamma(j, i)

    def own_entry(b):
        return t_ref[b] if stored else own_gamma(b)

    def over_pairs(step, width):
        width = width if cross % width == 0 else 1

        def piece(q, carry):
            def several(k, inner):
                ends = []
                for m in range(width):
                    e = bd + width * k + m
                    left, right = pair_ref[q, 0, e], pair_ref[q, 1, e]
                    t = nb + 2 * (q * cross + width * k + m)
                    ends += [(t, left, right), (t + 1, right, left)]
                step(ends)
                return inner

            return lax.fori_loop(0, (count_ref[q] - bd + width - 1) // width, several, carry)

        lax.fori_loop(0, nd, piece, 0)

    def first_diag(b, carry):
        val = own_gamma(b)
        if stored:
            t_ref[b] = val
        s_ref[b] = fold(val)
        y_ref[b] = fold(val * pc_ref[b])
        return carry

    lax.fori_loop(0, nb, first_diag, 0, unroll=4)

    def first_step(ends):
        found = []
        for t, j, i in ends:
            val = gamma(j, i)
            if stored:
                t_ref[t] = val
            found.append((i, fold(val), fold(val * pc_ref[j])))
        for i, one, two in found:
            s_ref[i] = s_ref[i] + one
            y_ref[i] = y_ref[i] + two

    over_pairs(first_step, 4)

    def gathered(ref):
        return jnp.sum(ref[0:nb], axis=1)

    diag = hard + gathered(s_ref)

    def next_step(ends):
        found = [(i, fold(entry(t, j, i) * pc_ref[j])) for t, j, i in ends]
        for i, one in found:
            y_ref[i] = y_ref[i] + one

    def next_diag(b, carry):
        y_ref[b] = fold(own_entry(b) * pc_ref[b])
        return carry

    def matvec():
        set_charges()
        lax.fori_loop(0, nb, next_diag, 0, unroll=8)
        over_pairs(next_step, 4)

    def total(vals):
        return jnp.sum(jnp.sum(vals, axis=0, keepdims=True), axis=1, keepdims=True)

    res = p_ref[0:nb]
    p = res
    x = jnp.zeros_like(res)
    rho = total(res * res)
    for it in range(ITERS):
        if it:
            matvec()
        image = diag * p + gathered(y_ref)
        step = rho / total(p * image)
        x = x + step * p
        if it + 1 < ITERS:
            res = res - step * image
            rho2 = total(res * res)
            p = res + (rho2 / rho) * p
            rho = rho2
            p_ref[0:nb] = p
    p_ref[0:nb] = x
    for a in range(bd):
        charge_ref[a:a + 1, :] = p_ref[pl.ds(me * bd + a, 1), :]
        set_charge(me * bd + a, 0)
    mine = jnp.concatenate([charge_ref[a:a + 1, :] for a in range(bd)], axis=1)
    width = bd * BLOCK

    several = 4

    def scatter(k, acc):
        lefts = []
        rights = []
        for m in range(several):
            s = k * several + m
            idx = nbr_ref[pl.ds(s, 1), :]
            hit = lax.broadcasted_iota(jnp.int32, (nb, width), 0) == (idx >> 7)
            spot = lax.broadcasted_iota(jnp.int32, (BLOCK, width), 0) == (idx & 127)
            rights.append(jnp.where(spot, 1.0, 0.0).astype(jnp.bfloat16))
            upper = []
            lower = []
            for d in range(3):
                val = push_ref[d, pl.ds(s, 1), :] * mine
                top = val.astype(jnp.bfloat16).astype(jnp.float32)
                upper.append(jnp.where(hit, top, 0.0).astype(jnp.bfloat16))
                lower.append(jnp.where(hit, val - top, 0.0).astype(jnp.bfloat16))
            lefts.append(jnp.concatenate(upper + lower, axis=0))
        return acc + lax.dot_general(jnp.concatenate(lefts, axis=1),
                                     jnp.concatenate(rights, axis=1), (((1,), (1,)), ((), ())),
                                     preferred_element_type=jnp.float32)

    acc = lax.fori_loop(0, NBR // several, scatter, jnp.zeros((6 * nb, BLOCK), jnp.float32))
    acc = acc[:3 * nb] + acc[3 * nb:]
    for q in range(nd):
        for d in range(3):
            part_ref[q, d * bd:(d + 1) * bd, :] = acc[d * nb + q * bd:d * nb + (q + 1) * bd]

    def moments(rel, weights, side):
        tile = jnp.where(sub8 == 3, 1.0, rel)
        rows = jnp.concatenate(split3(tile) + [jnp.zeros_like(rel)], axis=0).astype(jnp.bfloat16)
        out = sum(lax.dot_general(rows, w, (((1,), (side,)), ((), ())),
                                  preferred_element_type=jnp.float32) for w in weights)
        return out[0:8] + out[8:16] + out[16:24]

    def force_of(rel, found):
        return (rel * found[3:4] - found) * (0.5 / sigma_sq)

    def weigh(val, j, i):
        both = pc_ref[j] + p_ref[pl.ds(i, 1), :]
        weight = val * (both * both)
        top = weight.astype(jnp.bfloat16)
        return top, (weight - top.astype(jnp.float32)).astype(jnp.bfloat16)

    s_ref[...] = jnp.zeros_like(s_ref)
    for a in range(bd):
        b = me * bd + a
        rel = r_ref[b] - mid_ref[b]
        force = force_of(rel, moments(rel, weigh(own_entry(b), b, b), 0))
        lanes = slice(a * BLOCK, (a + 1) * BLOCK)
        for d in range(3):
            away = jnp.sum(push_ref[d, :, lanes], axis=0, keepdims=True) * charge_ref[a:a + 1, :]
            force = jnp.where(sub8 == d, force - away, force)
        s_ref[b] = force
    piece = piece_of(me, me, pow2)
    together = 2 if cross % 2 == 0 else 1

    def pair_force(k, carry):
        found = []
        for m in range(together):
            e = k * together + m
            j, i = pair_ref[piece, 0, bd + e], pair_ref[piece, 1, bd + e]
            mid = mid_ref[j]
            rel_j = r_ref[j] - mid
            rel_i = r_ref[i] - mid
            weights = weigh(entry(nb + 2 * (piece * cross + e), j, i), j, i)
            found.append((i, force_of(rel_i, moments(rel_j, weights, 0))))
            found.append((j, force_of(rel_j, moments(rel_i, weights, 1))))
        for b, force in found:
            s_ref[b] = s_ref[b] + force
        return carry

    lax.fori_loop(0, (count_ref[piece] - bd + together - 1) // together, pair_force, 0)
    for q in range(nd):
        for d in range(3):
            for r in range(bd):
                at = slice(d * bd + r, d * bd + r + 1)
                part_ref[q, at, :] = part_ref[q, at, :] + s_ref[q * bd + r, d:d + 1, :]


def gather_all(own, n):
    if n & (n - 1):
        return [lax.all_gather(own, "blk")]

    def swap(vals, step):
        return lax.ppermute(vals, "blk", [(i, i ^ step) for i in range(n)])

    got = own[None]
    step = 1
    while step < n:
        if step == 2 and n == 8:
            return [got] + [swap(got, k) for k in (2, 4, 6)]
        got = jnp.concatenate([got, swap(got, step)], axis=0)
        step *= 2
    return [got]


def on_device(positions, species, neighbors, pair_lists, hardness, w_first, b_first, w_second,
              b_second, w_out, b_out):
    n = lax.axis_size("blk")
    me = lax.axis_index("blk")
    atoms = positions.shape[1]
    bd = atoms // BLOCK
    nb = bd * n
    slots = pair_lists.shape[1]
    hid = w_first.shape[1]
    f32 = jnp.float32
    kind = species.reshape(1, atoms)
    small = pltpu.CompilerParams(vmem_limit_bytes=24 << 20)
    own = pl.pallas_call(
        pack_kernel, out_shape=jax.ShapeDtypeStruct((PACK, BLOCK), f32),
        in_specs=[spec(VM)] * 3, out_specs=spec(VM), name="pack",
    )(positions, kind, pair_lists)
    pow2 = n & (n - 1) == 0
    places = gather_all(own, n)
    staged = (neighbors, w_first, b_first, w_second, b_second, w_out)
    chi, offs, hidden, whole = pl.pallas_call(
        functools.partial(chi_kernel, pow2, n, bd, len(places)),
        out_shape=(jax.ShapeDtypeStruct((bd, BLOCK), f32),
                   jax.ShapeDtypeStruct((4, NBR, atoms), f32),
                   jax.ShapeDtypeStruct((2, hid, atoms), f32),
                   jax.ShapeDtypeStruct((n, PACK, BLOCK), f32)),
        in_specs=[spec(SM)] + [spec(VM)] * (8 + len(places)) + [spec(SM)],
        out_specs=(spec(VM),) * 4,
        scratch_shapes=[VM((DESC, atoms), f32)],
        compiler_params=small,
        name="chi",
    )(me[None], *places, positions, staged[0], kind, *staged[1:], b_out)
    all_chi = gather_all(chi, n)
    lists = whole[:, 4 * bd:4 * bd + 2, :slots].astype(jnp.int32)
    counts = jnp.sum((lists[:, 0] >= 0).astype(jnp.int32), axis=1)
    lists = jnp.where(lists < 0, nb, lists)
    push, rows, mids, left = pl.pallas_call(
        functools.partial(pull_kernel, pow2, n, bd, nb),
        out_shape=(jax.ShapeDtypeStruct((3, NBR, atoms), f32),
                   jax.ShapeDtypeStruct((nb + 1, 8, BLOCK), f32),
                   jax.ShapeDtypeStruct((nb + 1, 8, BLOCK), f32),
                   jax.ShapeDtypeStruct((nb + 1, BLOCK, 48), jnp.bfloat16)),
        in_specs=[spec(SM)] + [spec(VM)] * 7,
        out_specs=(spec(VM),) * 4,
        scratch_shapes=[VM((DESC, atoms), f32)],
        compiler_params=small,
        name="pull",
    )(me[None], whole, kind, offs, hidden, staged[1], staged[3], staged[5])
    entries = nb + 2 * (n * slots - nb)
    stored = entries * BLOCK * BLOCK * 4 <= STORE_LIMIT
    charges, part = pl.pallas_call(
        functools.partial(solve_kernel, pow2, n, bd, nb, slots, stored, len(all_chi)),
        out_shape=(jax.ShapeDtypeStruct((bd, BLOCK), f32),
                   jax.ShapeDtypeStruct((n, 3 * bd, BLOCK), f32)),
        in_specs=[spec(SM)] * 4 + [spec(VM)] * (6 + len(all_chi)),
        out_specs=(spec(VM),) * 2,
        scratch_shapes=[VM((n, bd, BLOCK), f32), VM((nb + 8, BLOCK), f32),
                        VM((nb + 1, BLOCK, BLOCK), f32), VM((nb + 1, 8, BLOCK), f32),
                        VM((nb + 1, 8, BLOCK), f32),
                        VM((entries if stored else 1, BLOCK, BLOCK), f32)],
        compiler_params=pltpu.CompilerParams(vmem_limit_bytes=58 << 20),
        name="solve",
    )(me[None], lists, counts, hardness, *all_chi, whole, rows, mids, left, push, neighbors)
    swapped = lax.all_to_all(part, "blk", 0, 0)
    forces = jnp.sum(swapped, axis=0)
    return charges.reshape(atoms), forces.reshape(3, atoms)


def solution(mesh):
    both = ("cell", "blk")
    placed = (P(None, both), P(both), P(None, both), P(None, both)) + (P(),) * 7
    return jax.shard_map(
        on_device,
        mesh=mesh,
        in_specs=placed,
        out_specs=(P(both), P(None, both)),
        check_vma=False,
    )
```

```python
import functools
import math

import jax
import jax.numpy as jnp
import numpy as np
from jax import lax
from jax.experimental import pallas as pl
from jax.experimental.pallas import tpu as pltpu
from jax.sharding import PartitionSpec as P

ELEM = 4
RAD = 16
DESC = ELEM * RAD
BLOCK = 128
NBR = 32
ITERS = 3
PACK = 24
STORE_LIMIT = 36 << 20

coulomb_scale = 0.5
sigma_sq = 4.0
cutoff_sq = 49.0
highest = lax.Precision.HIGHEST
RATES = [0.005 * 200.0 ** (k / (RAD - 1)) for k in range(RAD)]
VM = pltpu.VMEM
SM = pltpu.SMEM
SCALE = math.log2(math.e) / (2.0 * sigma_sq)


def spec(space):
    return pl.BlockSpec(memory_space=space)


def piece_of(q, me, pow2):
    return q ^ me if pow2 else q


def dot(a, b, lhs=1):
    return lax.dot_general(a, b, (((lhs,), (0,)), ((), ())), precision=highest,
                           preferred_element_type=jnp.float32)


def column(row):
    return jnp.broadcast_to(row, (BLOCK, BLOCK)).T


def pick(kind, mats):
    out = jnp.where(kind == 0, mats[0], 0.0)
    for e in range(1, ELEM):
        out = jnp.where(kind == e, mats[e], out)
    return out


def one_hot(kind):
    ids = lax.broadcasted_iota(jnp.int32, (ELEM, kind.shape[1]), 0)
    return jnp.where(ids == kind, 1.0, 0.0)


def pack_kernel(count, *refs):
    sources = refs[:count]
    own_ref = refs[count]
    held = refs[count + 1:2 * count + 1]
    sems = refs[-1]
    copies = [pltpu.make_async_copy(sources[k], held[k], sems.at[k]) for k in range(count)]
    for copy in copies:
        copy.start()
    own_ref[...] = jnp.zeros_like(own_ref)
    for copy in copies[:3]:
        copy.wait()
    pos_ref, kind_ref, pairs_ref = held[:3]
    bd = pos_ref.shape[1] // BLOCK
    for a in range(bd):
        lanes = slice(a * BLOCK, (a + 1) * BLOCK)
        for d in range(3):
            own_ref[d * bd + a:d * bd + a + 1, :] = pos_ref[d:d + 1, lanes]
        own_ref[3 * bd + a:3 * bd + a + 1, :] = kind_ref[:, lanes].astype(jnp.float32)
    slots = pairs_ref.shape[1]
    for side in range(2):
        own_ref[4 * bd + side:4 * bd + side + 1, :slots] = (
            pairs_ref[side:side + 1, :].astype(jnp.float32))
    for copy in copies[3:]:
        copy.wait()


def join_pieces(pieces, out_ref):
    first = 0
    for piece in pieces:
        count = piece.shape[0]
        out_ref[first:first + count] = piece[...]
        first += count


def chi_kernel(pow2, nd, bd, parts, me_ref, *refs):
    pieces = refs[:parts]
    (pos_ref, nbr_ref, kind_ref, w1, b1, w2, b2, wo, bo,
     chi_ref, d_ref, h_ref, g_ref, f_ref) = refs[parts:]
    me = me_ref[0]
    chunk = min(nd, 8)
    join_pieces(pieces, g_ref)
    for a in range(bd):
        lanes = slice(a * BLOCK, (a + 1) * BLOCK)

        def group(g, carry):
            rows8 = pl.ds(pl.multiple_of(g * 8, 8), 8)
            idx = nbr_ref[rows8, lanes]
            hi = idx >> 7
            lo = idx & 127

            def look(part, vals):
                for step in range(chunk):
                    q = part * chunk + step
                    at = piece_of(q, me, pow2)
                    for r in range(bd):
                        hit = hi == q * bd + r
                        new = []
                        for d in range(4):
                            row = jnp.broadcast_to(g_ref[at, d * bd + r:d * bd + r + 1, :],
                                                   (8, BLOCK))
                            new.append(jnp.where(hit, jnp.take_along_axis(row, lo, axis=1),
                                                 vals[d]))
                        vals = tuple(new)
                return vals

            vals = (jnp.zeros((8, BLOCK), jnp.float32),) * 4
            if nd == chunk:
                vals = look(0, vals)
            else:
                vals = lax.fori_loop(0, nd // chunk, look, vals)
            live = idx >= 0
            for d in range(3):
                d_ref[d, rows8, lanes] = jnp.where(live, pos_ref[d:d + 1, lanes] - vals[d], 0.0)
            d_ref[3, rows8, lanes] = jnp.where(live, vals[3], -1.0)
            return carry

        lax.fori_loop(0, NBR // 8, group, 0, unroll=4 if nd == chunk else 1)
        offs = [d_ref[d, :, lanes] for d in range(3)]
        nk = d_ref[3, :, lanes]
        r2 = offs[0] * offs[0] + offs[1] * offs[1] + offs[2] * offs[2]
        u = 1.0 - r2 * (1.0 / cutoff_sq)
        shell = u * u * (ELEM / NBR)
        for k in range(RAD):
            val = shell * jnp.exp(-RATES[k] * r2)
            for e in range(ELEM):
                f_ref[e * RAD + k:e * RAD + k + 1, lanes] = jnp.sum(
                    jnp.where(nk == e, val, 0.0), axis=0, keepdims=True)
    kind = kind_ref[...]
    hot = one_hot(kind)
    feats = f_ref[...]
    h1 = jnp.tanh(pick(kind, [dot(w1[e], feats) for e in range(ELEM)]) + dot(b1[...], hot, 0))
    h2 = jnp.tanh(pick(kind, [dot(w2[e], h1) for e in range(ELEM)]) + dot(b2[...], hot, 0))
    h_ref[0] = h1
    h_ref[1] = h2
    chi = jnp.sum(dot(wo[...], hot, 0) * h2, axis=0, keepdims=True) + dot(bo[...], hot)
    for a in range(bd):
        chi_ref[a:a + 1, :] = chi[:, a * BLOCK:(a + 1) * BLOCK]


def fold(vals):
    tiles = vals.reshape(BLOCK // 8, 8, BLOCK)
    terms = [tiles[k] for k in range(BLOCK // 8)]
    while len(terms) > 1:
        terms = [terms[k] + terms[k + 1] for k in range(0, len(terms), 2)]
    return terms[0]


def split3(vals):
    parts = []
    for _ in range(3):
        top = vals.astype(jnp.bfloat16).astype(jnp.float32)
        parts.append(top)
        vals = vals - top
    return parts


def pull_kernel(pow2, nd, bd, nb, me_ref, g_ref, kind_ref, d_ref, h_ref, w1, w2, wo, push_ref,
                r_ref, mid_ref, a_ref, f_ref):
    me = me_ref[0]
    sub8 = lax.broadcasted_iota(jnp.int32, (8, BLOCK), 0)
    r_ref[...] = jnp.zeros_like(r_ref)
    for q in range(nd):
        at = piece_of(q, me, pow2)
        for r in range(bd):
            for d in range(3):
                r_ref[q * bd + r, d:d + 1, :] = g_ref[at, d * bd + r:d * bd + r + 1, :]

    def set_block(b, carry):
        mid = jnp.broadcast_to(r_ref[b][:, 0:1], (8, BLOCK))
        mid_ref[b] = mid
        rel = r_ref[b] - mid
        size = jnp.sum(rel * rel, axis=0, keepdims=True)
        tile = jnp.where(sub8 == 3, 1.0,
                         jnp.where(sub8 == 4, size * -SCALE - 1.0, rel * (2.0 * SCALE)))
        q1, q2, q3 = split3(tile)
        a_ref[b] = jnp.concatenate([q1, q1, q2, q1, q3, q2], axis=0).T.astype(jnp.bfloat16)
        return carry

    lax.fori_loop(0, nb + 1, set_block, 0, unroll=11 if nb + 1 == 33 else 1)
    kind = kind_ref[...]
    h1 = h_ref[0]
    h2 = h_ref[1]
    pre2 = dot(wo[...], one_hot(kind), 0) * (1.0 - h2 * h2)
    pre1 = sum(dot(w2[e], jnp.where(kind == e, pre2, 0.0), 0) for e in range(ELEM))
    pre1 = pre1 * (1.0 - h1 * h1)
    f_ref[...] = sum(dot(w1[e], jnp.where(kind == e, pre1, 0.0), 0)
                     for e in range(ELEM)) * (ELEM / NBR)
    for a in range(bd):
        lanes = slice(a * BLOCK, (a + 1) * BLOCK)
        offs = [d_ref[d, :, lanes] for d in range(3)]
        nk = d_ref[3, :, lanes]
        r2 = offs[0] * offs[0] + offs[1] * offs[1] + offs[2] * offs[2]
        u = 1.0 - r2 * (1.0 / cutoff_sq)
        s1 = jnp.zeros_like(r2)
        s2 = jnp.zeros_like(r2)
        for k in range(RAD):
            sel = jnp.zeros_like(r2)
            for e in range(ELEM):
                sel = jnp.where(nk == e, f_ref[e * RAD + k:e * RAD + k + 1, lanes], sel)
            term = sel * jnp.exp(-RATES[k] * r2)
            s1 = s1 + term
            s2 = s2 + RATES[k] * term
        grad = -u * ((2.0 / cutoff_sq) * s1 + u * s2)
        for d in range(3):
            push_ref[d, :, lanes] = 2.0 * grad * offs[d]


def solve_kernel(pow2, nd, bd, nb, slots, stored, parts, me_ref, pair_ref, count_ref, hard_ref,
                 *refs):
    pieces = refs[:parts]
    (g_ref, r_ref, mid_ref, a_ref, push_ref, nbr_ref, charge_ref, part_ref, x_ref, p_ref, pc_ref,
     y_ref, s_ref, t_ref) = refs[parts:]
    me = me_ref[0]
    cross = slots - bd
    sub = lax.broadcasted_iota(jnp.int32, (BLOCK, BLOCK), 0)
    ident = sub == lax.broadcasted_iota(jnp.int32, (BLOCK, BLOCK), 1)
    sub8 = lax.broadcasted_iota(jnp.int32, (8, BLOCK), 0)

    join_pieces(pieces, x_ref)
    p_ref[...] = jnp.zeros_like(p_ref)
    hards = []
    for q in range(nd):
        at = piece_of(q, me, pow2)
        span = slice(q * bd, (q + 1) * bd)
        p_ref[span, :] = -x_ref[at]
        hards.append(pick(g_ref[at, 3 * bd:4 * bd, :], [hard_ref[e] for e in range(ELEM)]))
    hard = jnp.concatenate(hards, axis=0)

    def set_charge(b, carry):
        pc_ref[b] = column(p_ref[pl.ds(b, 1), :])
        return carry

    def set_charges():
        if nb > 64:
            lax.fori_loop(0, nb, set_charge, 0)
            return
        turned = jnp.concatenate(split3(p_ref[0:nb]), axis=0).T.astype(jnp.bfloat16)
        ids = lax.broadcasted_iota(jnp.int32, (3 * nb, BLOCK), 0) % nb
        for b in range(0, nb, 2):
            chosen = [jnp.where(ids == b + m, 1.0, 0.0).astype(jnp.bfloat16) for m in range(2)]
            cols = jnp.dot(turned, jnp.concatenate(chosen, axis=1),
                           preferred_element_type=jnp.float32)
            for m in range(2):
                pc_ref[b + m] = cols[:, m * BLOCK:(m + 1) * BLOCK]

    pc_ref[nb] = jnp.zeros((BLOCK, BLOCK), jnp.float32)
    set_charges()

    def gamma(j, i):
        rel = r_ref[i] - mid_ref[j]
        size = jnp.sum(rel * rel, axis=0, keepdims=True)
        tile = jnp.where(sub8 == 3, size * -SCALE, jnp.where(sub8 == 4, 1.0, rel))
        p1, p2, p3 = split3(tile)
        right = jnp.concatenate([p1, p2, p1, p3, p1, p2], axis=0).astype(jnp.bfloat16)
        return jnp.exp2(jnp.dot(a_ref[j], right, preferred_element_type=jnp.float32))

    def own_gamma(b):
        return jnp.where(ident, 0.0, gamma(b, b))

    def entry(t, j, i):
        return t_ref[t] if stored else gamma(j, i)

    def own_entry(b):
        return t_ref[b] if stored else own_gamma(b)

    def over_pairs(step, width):
        width = width if cross % width == 0 else 1

        def piece(q, carry):
            def several(k, inner):
                ends = []
                for m in range(width):
                    e = bd + width * k + m
                    left, right = pair_ref[q, 0, e], pair_ref[q, 1, e]
                    t = nb + 2 * (q * cross + width * k + m)
                    ends += [(t, left, right), (t + 1, right, left)]
                step(ends)
                return inner

            return lax.fori_loop(0, (count_ref[q] - bd + width - 1) // width, several, carry)

        lax.fori_loop(0, nd, piece, 0)

    def first_diag(b, carry):
        val = own_gamma(b)
        if stored:
            t_ref[b] = val
        s_ref[b] = fold(val)
        y_ref[b] = fold(val * pc_ref[b])
        return carry

    lax.fori_loop(0, nb, first_diag, 0, unroll=4)

    def first_step(ends):
        found = []
        for t, j, i in ends:
            val = gamma(j, i)
            if stored:
                t_ref[t] = val
            found.append((i, fold(val), fold(val * pc_ref[j])))
        for i, one, two in found:
            s_ref[i] = s_ref[i] + one
            y_ref[i] = y_ref[i] + two

    over_pairs(first_step, 4)

    def gathered(ref):
        return jnp.sum(ref[0:nb], axis=1)

    diag = hard + gathered(s_ref)

    def next_step(ends):
        found = [(i, fold(entry(t, j, i) * pc_ref[j])) for t, j, i in ends]
        for i, one in found:
            y_ref[i] = y_ref[i] + one

    def next_diag(b, carry):
        y_ref[b] = fold(own_entry(b) * pc_ref[b])
        return carry

    def matvec():
        set_charges()
        lax.fori_loop(0, nb, next_diag, 0, unroll=8)
        over_pairs(next_step, 4)

    def total(vals):
        return jnp.sum(jnp.sum(vals, axis=0, keepdims=True), axis=1, keepdims=True)

    res = p_ref[0:nb]
    p = res
    x = jnp.zeros_like(res)
    rho = total(res * res)
    for it in range(ITERS):
        if it:
            matvec()
        image = diag * p + gathered(y_ref)
        step = rho / total(p * image)
        x = x + step * p
        if it + 1 < ITERS:
            res = res - step * image
            rho2 = total(res * res)
            p = res + (rho2 / rho) * p
            rho = rho2
            p_ref[0:nb] = p
    p_ref[0:nb] = x
    for a in range(bd):
        charge_ref[a:a + 1, :] = p_ref[pl.ds(me * bd + a, 1), :]
        set_charge(me * bd + a, 0)
    mine = jnp.concatenate([charge_ref[a:a + 1, :] for a in range(bd)], axis=1)
    width = bd * BLOCK

    several = 4

    def scatter(k, acc):
        lefts = []
        rights = []
        for m in range(several):
            s = k * several + m
            idx = nbr_ref[pl.ds(s, 1), :]
            hit = lax.broadcasted_iota(jnp.int32, (nb, width), 0) == (idx >> 7)
            spot = lax.broadcasted_iota(jnp.int32, (BLOCK, width), 0) == (idx & 127)
            rights.append(jnp.where(spot, 1.0, 0.0).astype(jnp.bfloat16))
            upper = []
            lower = []
            for d in range(3):
                val = push_ref[d, pl.ds(s, 1), :] * mine
                top = val.astype(jnp.bfloat16).astype(jnp.float32)
                upper.append(jnp.where(hit, top, 0.0).astype(jnp.bfloat16))
                lower.append(jnp.where(hit, val - top, 0.0).astype(jnp.bfloat16))
            lefts.append(jnp.concatenate(upper + lower, axis=0))
        return acc + lax.dot_general(jnp.concatenate(lefts, axis=1),
                                     jnp.concatenate(rights, axis=1), (((1,), (1,)), ((), ())),
                                     preferred_element_type=jnp.float32)

    acc = lax.fori_loop(0, NBR // several, scatter, jnp.zeros((6 * nb, BLOCK), jnp.float32))
    acc = acc[:3 * nb] + acc[3 * nb:]
    for q in range(nd):
        for d in range(3):
            part_ref[q, d * bd:(d + 1) * bd, :] = acc[d * nb + q * bd:d * nb + (q + 1) * bd]

    def moments(rel, weights, side):
        tile = jnp.where(sub8 == 3, 1.0, rel)
        rows = jnp.concatenate(split3(tile) + [jnp.zeros_like(rel)], axis=0).astype(jnp.bfloat16)
        out = sum(lax.dot_general(rows, w, (((1,), (side,)), ((), ())),
                                  preferred_element_type=jnp.float32) for w in weights)
        return out[0:8] + out[8:16] + out[16:24]

    def force_of(rel, found):
        return (rel * found[3:4] - found) * (0.5 / sigma_sq)

    def weigh(val, j, i):
        both = pc_ref[j] + p_ref[pl.ds(i, 1), :]
        weight = val * (both * both)
        top = weight.astype(jnp.bfloat16)
        return top, (weight - top.astype(jnp.float32)).astype(jnp.bfloat16)

    s_ref[...] = jnp.zeros_like(s_ref)
    for a in range(bd):
        b = me * bd + a
        rel = r_ref[b] - mid_ref[b]
        force = force_of(rel, moments(rel, weigh(own_entry(b), b, b), 0))
        lanes = slice(a * BLOCK, (a + 1) * BLOCK)
        for d in range(3):
            away = jnp.sum(push_ref[d, :, lanes], axis=0, keepdims=True) * charge_ref[a:a + 1, :]
            force = jnp.where(sub8 == d, force - away, force)
        s_ref[b] = force
    piece = piece_of(me, me, pow2)
    together = 4 if cross % 4 == 0 else 1

    def pair_force(k, carry):
        found = []
        for m in range(together):
            e = k * together + m
            j, i = pair_ref[piece, 0, bd + e], pair_ref[piece, 1, bd + e]
            mid = mid_ref[j]
            rel_j = r_ref[j] - mid
            rel_i = r_ref[i] - mid
            weights = weigh(entry(nb + 2 * (piece * cross + e), j, i), j, i)
            found.append((i, force_of(rel_i, moments(rel_j, weights, 0))))
            found.append((j, force_of(rel_j, moments(rel_i, weights, 1))))
        for b, force in found:
            s_ref[b] = s_ref[b] + force
        return carry

    lax.fori_loop(0, (count_ref[piece] - bd + together - 1) // together, pair_force, 0)
    for q in range(nd):
        for d in range(3):
            for r in range(bd):
                at = slice(d * bd + r, d * bd + r + 1)
                part_ref[q, at, :] = part_ref[q, at, :] + s_ref[q * bd + r, d:d + 1, :]


def gather_all(own, n):
    if n & (n - 1):
        return [lax.all_gather(own, "blk")]

    def swap(vals, step):
        return lax.ppermute(vals, "blk", [(i, i ^ step) for i in range(n)])

    got = own[None]
    step = 1
    while step < n:
        got = jnp.concatenate([got, swap(got, step)], axis=0)
        step *= 2
    return [got]


def on_device(positions, species, neighbors, pair_lists, hardness, w_first, b_first, w_second,
              b_second, w_out, b_out):
    n = lax.axis_size("blk")
    me = lax.axis_index("blk")
    atoms = positions.shape[1]
    bd = atoms // BLOCK
    nb = bd * n
    slots = pair_lists.shape[1]
    hid = w_first.shape[1]
    f32 = jnp.float32
    kind = species.reshape(1, atoms)
    small = pltpu.CompilerParams(vmem_limit_bytes=24 << 20)
    raw = (positions, kind, pair_lists, neighbors, b_first, b_second, w_out, b_out.reshape(1, ELEM))
    raw = tuple(pltpu.with_memory_space_constraint(r, pltpu.HBM) for r in raw)
    own, pos, kinds, _, nbr, b1, b2, wo, bo = pl.pallas_call(
        functools.partial(pack_kernel, len(raw)),
        out_shape=(jax.ShapeDtypeStruct((PACK, BLOCK), f32),)
        + tuple(jax.ShapeDtypeStruct(r.shape, r.dtype) for r in raw),
        in_specs=[spec(pltpu.HBM)] * len(raw), out_specs=(spec(VM),) * (1 + len(raw)),
        scratch_shapes=[pltpu.SemaphoreType.DMA((len(raw),))],
        compiler_params=small, name="pack",
    )(*raw)
    pow2 = n & (n - 1) == 0
    places = gather_all(own, n)
    chi, offs, hidden, whole = pl.pallas_call(
        functools.partial(chi_kernel, pow2, n, bd, len(places)),
        out_shape=(jax.ShapeDtypeStruct((bd, BLOCK), f32),
                   jax.ShapeDtypeStruct((4, NBR, atoms), f32),
                   jax.ShapeDtypeStruct((2, hid, atoms), f32),
                   jax.ShapeDtypeStruct((n, PACK, BLOCK), f32)),
        in_specs=[spec(SM)] + [spec(VM)] * (9 + len(places)),
        out_specs=(spec(VM),) * 4,
        scratch_shapes=[VM((DESC, atoms), f32)],
        compiler_params=small,
        name="chi",
    )(me[None], *places, pos, nbr, kinds, w_first, b1, w_second, b2, wo, bo)
    all_chi = gather_all(chi, n)
    lists = whole[:, 4 * bd:4 * bd + 2, :slots].astype(jnp.int32)
    counts = jnp.sum((lists[:, 0] >= 0).astype(jnp.int32), axis=1)
    lists = jnp.where(lists < 0, nb, lists)
    push, rows, mids, left = pl.pallas_call(
        functools.partial(pull_kernel, pow2, n, bd, nb),
        out_shape=(jax.ShapeDtypeStruct((3, NBR, atoms), f32),
                   jax.ShapeDtypeStruct((nb + 1, 8, BLOCK), f32),
                   jax.ShapeDtypeStruct((nb + 1, 8, BLOCK), f32),
                   jax.ShapeDtypeStruct((nb + 1, BLOCK, 48), jnp.bfloat16)),
        in_specs=[spec(SM)] + [spec(VM)] * 7,
        out_specs=(spec(VM),) * 4,
        scratch_shapes=[VM((DESC, atoms), f32)],
        compiler_params=small,
        name="pull",
    )(me[None], whole, kinds, offs, hidden, w_first, w_second, wo)
    entries = nb + 2 * (n * slots - nb)
    stored = entries * BLOCK * BLOCK * 4 <= STORE_LIMIT
    charges, part = pl.pallas_call(
        functools.partial(solve_kernel, pow2, n, bd, nb, slots, stored, len(all_chi)),
        out_shape=(jax.ShapeDtypeStruct((bd, BLOCK), f32),
                   jax.ShapeDtypeStruct((n, 3 * bd, BLOCK), f32)),
        in_specs=[spec(SM)] * 4 + [spec(VM)] * (6 + len(all_chi)),
        out_specs=(spec(VM),) * 2,
        scratch_shapes=[VM((n, bd, BLOCK), f32), VM((nb + 8, BLOCK), f32),
                        VM((nb + 1, BLOCK, BLOCK), f32), VM((nb + 1, 8, BLOCK), f32),
                        VM((nb + 1, 8, BLOCK), f32),
                        VM((entries if stored else 1, BLOCK, BLOCK), f32)],
        compiler_params=pltpu.CompilerParams(vmem_limit_bytes=(42 if stored else 58) << 20),
        name="solve",
    )(me[None], lists, counts, hardness, *all_chi, whole, rows, mids, left, push, nbr)
    swapped = lax.all_to_all(part, "blk", 0, 0)
    forces = jnp.sum(swapped, axis=0)
    return charges.reshape(atoms), forces.reshape(3, atoms)


def solution(mesh):
    both = ("cell", "blk")
    placed = (P(None, both), P(both), P(None, both), P(None, both)) + (P(),) * 7
    return jax.shard_map(
        on_device,
        mesh=mesh,
        in_specs=placed,
        out_specs=(P(both), P(None, both)),
        check_vma=False,
    )
```

```python
import functools
import math

import jax
import jax.numpy as jnp
import numpy as np
from jax import lax
from jax.experimental import pallas as pl
from jax.experimental.pallas import tpu as pltpu
from jax.sharding import PartitionSpec as P

ELEM = 4
RAD = 16
DESC = ELEM * RAD
BLOCK = 128
NBR = 32
ITERS = 3
PACK = 24
STORE_LIMIT = 36 << 20

coulomb_scale = 0.5
sigma_sq = 4.0
cutoff_sq = 49.0
highest = lax.Precision.HIGHEST
RATES = [0.005 * 200.0 ** (k / (RAD - 1)) for k in range(RAD)]
VM = pltpu.VMEM
SM = pltpu.SMEM
SCALE = math.log2(math.e) / (2.0 * sigma_sq)


def spec(space):
    return pl.BlockSpec(memory_space=space)


def piece_of(q, me, pow2):
    return q ^ me if pow2 else q


def dot(a, b, lhs=1):
    return lax.dot_general(a, b, (((lhs,), (0,)), ((), ())), precision=highest,
                           preferred_element_type=jnp.float32)


def column(row):
    return jnp.broadcast_to(row, (BLOCK, BLOCK)).T


def pick(kind, mats):
    out = jnp.where(kind == 0, mats[0], 0.0)
    for e in range(1, ELEM):
        out = jnp.where(kind == e, mats[e], out)
    return out


def one_hot(kind):
    ids = lax.broadcasted_iota(jnp.int32, (ELEM, kind.shape[1]), 0)
    return jnp.where(ids == kind, 1.0, 0.0)


def pack_kernel(count, *refs):
    sources = refs[:count]
    own_ref = refs[count]
    held = refs[count + 1:2 * count + 1]
    sems = refs[-1]
    copies = [pltpu.make_async_copy(sources[k], held[k], sems.at[k]) for k in range(count)]
    for copy in copies:
        copy.start()
    own_ref[...] = jnp.zeros_like(own_ref)
    for copy in copies[:3]:
        copy.wait()
    pos_ref, kind_ref, pairs_ref = held[:3]
    bd = pos_ref.shape[1] // BLOCK
    for a in range(bd):
        lanes = slice(a * BLOCK, (a + 1) * BLOCK)
        for d in range(3):
            own_ref[d * bd + a:d * bd + a + 1, :] = pos_ref[d:d + 1, lanes]
        own_ref[3 * bd + a:3 * bd + a + 1, :] = kind_ref[:, lanes].astype(jnp.float32)
    slots = pairs_ref.shape[1]
    for side in range(2):
        own_ref[4 * bd + side:4 * bd + side + 1, :slots] = (
            pairs_ref[side:side + 1, :].astype(jnp.float32))
    for copy in copies[3:]:
        copy.wait()


def join_pieces(pieces, out_ref):
    first = 0
    for piece in pieces:
        count = piece.shape[0]
        out_ref[first:first + count] = piece[...]
        first += count


def chi_kernel(pow2, nd, bd, parts, me_ref, *refs):
    pieces = refs[:parts]
    (pos_ref, nbr_ref, kind_ref, w1, b1, w2, b2, wo, bo,
     chi_ref, d_ref, h_ref, g_ref, f_ref) = refs[parts:]
    me = me_ref[0]
    chunk = min(nd, 8)
    join_pieces(pieces, g_ref)
    for a in range(bd):
        lanes = slice(a * BLOCK, (a + 1) * BLOCK)

        def group(g, carry):
            rows8 = pl.ds(pl.multiple_of(g * 8, 8), 8)
            idx = nbr_ref[rows8, lanes]
            hi = idx >> 7
            lo = idx & 127

            def look(part, vals):
                for step in range(chunk):
                    q = part * chunk + step
                    at = piece_of(q, me, pow2)
                    for r in range(bd):
                        hit = hi == q * bd + r
                        new = []
                        for d in range(4):
                            row = jnp.broadcast_to(g_ref[at, d * bd + r:d * bd + r + 1, :],
                                                   (8, BLOCK))
                            new.append(jnp.where(hit, jnp.take_along_axis(row, lo, axis=1),
                                                 vals[d]))
                        vals = tuple(new)
                return vals

            vals = (jnp.zeros((8, BLOCK), jnp.float32),) * 4
            if nd == chunk:
                vals = look(0, vals)
            else:
                vals = lax.fori_loop(0, nd // chunk, look, vals)
            live = idx >= 0
            for d in range(3):
                d_ref[d, rows8, lanes] = jnp.where(live, pos_ref[d:d + 1, lanes] - vals[d], 0.0)
            d_ref[3, rows8, lanes] = jnp.where(live, vals[3], -1.0)
            return carry

        lax.fori_loop(0, NBR // 8, group, 0, unroll=4 if nd == chunk else 1)
        offs = [d_ref[d, :, lanes] for d in range(3)]
        nk = d_ref[3, :, lanes]
        r2 = offs[0] * offs[0] + offs[1] * offs[1] + offs[2] * offs[2]
        u = 1.0 - r2 * (1.0 / cutoff_sq)
        shell = u * u * (ELEM / NBR)
        for k in range(RAD):
            val = shell * jnp.exp(-RATES[k] * r2)
            for e in range(ELEM):
                f_ref[e * RAD + k:e * RAD + k + 1, lanes] = jnp.sum(
                    jnp.where(nk == e, val, 0.0), axis=0, keepdims=True)
    kind = kind_ref[...]
    hot = one_hot(kind)
    feats = f_ref[...]
    h1 = jnp.tanh(pick(kind, [dot(w1[e], feats) for e in range(ELEM)]) + dot(b1[...], hot, 0))
    h2 = jnp.tanh(pick(kind, [dot(w2[e], h1) for e in range(ELEM)]) + dot(b2[...], hot, 0))
    h_ref[0] = h1
    h_ref[1] = h2
    chi = jnp.sum(dot(wo[...], hot, 0) * h2, axis=0, keepdims=True) + dot(bo[...], hot)
    for a in range(bd):
        chi_ref[a:a + 1, :] = chi[:, a * BLOCK:(a + 1) * BLOCK]


def fold(vals):
    tiles = vals.reshape(BLOCK // 8, 8, BLOCK)
    terms = [tiles[k] for k in range(BLOCK // 8)]
    while len(terms) > 1:
        terms = [terms[k] + terms[k + 1] for k in range(0, len(terms), 2)]
    return terms[0]


def split3(vals):
    parts = []
    for _ in range(3):
        top = vals.astype(jnp.bfloat16).astype(jnp.float32)
        parts.append(top)
        vals = vals - top
    return parts


def tile_kernel(pow2, nd, bd, nb, me_ref, g_ref, r_ref, mid_ref, a_ref):
    me = me_ref[0]
    sub8 = lax.broadcasted_iota(jnp.int32, (8, BLOCK), 0)
    r_ref[...] = jnp.zeros_like(r_ref)
    for q in range(nd):
        at = piece_of(q, me, pow2)
        for r in range(bd):
            for d in range(3):
                r_ref[q * bd + r, d:d + 1, :] = g_ref[at, d * bd + r:d * bd + r + 1, :]

    def set_block(b, carry):
        mid = jnp.broadcast_to(r_ref[b][:, 0:1], (8, BLOCK))
        mid_ref[b] = mid
        rel = r_ref[b] - mid
        size = jnp.sum(rel * rel, axis=0, keepdims=True)
        tile = jnp.where(sub8 == 3, 1.0,
                         jnp.where(sub8 == 4, size * -SCALE - 1.0, rel * (2.0 * SCALE)))
        q1, q2, q3 = split3(tile)
        a_ref[b] = jnp.concatenate([q1, q1, q2, q1, q3, q2], axis=0).T.astype(jnp.bfloat16)
        return carry

    lax.fori_loop(0, nb + 1, set_block, 0, unroll=11 if nb + 1 == 33 else 1)


def pull_kernel(bd, kind_ref, d_ref, h_ref, w1, w2, wo, push_ref, f_ref):
    kind = kind_ref[...]
    h1 = h_ref[0]
    h2 = h_ref[1]
    pre2 = dot(wo[...], one_hot(kind), 0) * (1.0 - h2 * h2)
    pre1 = sum(dot(w2[e], jnp.where(kind == e, pre2, 0.0), 0) for e in range(ELEM))
    pre1 = pre1 * (1.0 - h1 * h1)
    f_ref[...] = sum(dot(w1[e], jnp.where(kind == e, pre1, 0.0), 0)
                     for e in range(ELEM)) * (ELEM / NBR)
    for a in range(bd):
        lanes = slice(a * BLOCK, (a + 1) * BLOCK)
        offs = [d_ref[d, :, lanes] for d in range(3)]
        nk = d_ref[3, :, lanes]
        r2 = offs[0] * offs[0] + offs[1] * offs[1] + offs[2] * offs[2]
        u = 1.0 - r2 * (1.0 / cutoff_sq)
        s1 = jnp.zeros_like(r2)
        s2 = jnp.zeros_like(r2)
        for k in range(RAD):
            sel = jnp.zeros_like(r2)
            for e in range(ELEM):
                sel = jnp.where(nk == e, f_ref[e * RAD + k:e * RAD + k + 1, lanes], sel)
            term = sel * jnp.exp(-RATES[k] * r2)
            s1 = s1 + term
            s2 = s2 + RATES[k] * term
        grad = -u * ((2.0 / cutoff_sq) * s1 + u * s2)
        for d in range(3):
            push_ref[d, :, lanes] = 2.0 * grad * offs[d]


def solve_kernel(pow2, nd, bd, nb, slots, stored, parts, me_ref, pair_ref, count_ref, hard_ref,
                 *refs):
    pieces = refs[:parts]
    (g_ref, r_ref, mid_ref, a_ref, push_ref, nbr_ref, charge_ref, part_ref, x_ref, p_ref, pc_ref,
     y_ref, s_ref, t_ref, e0_ref, e1_ref, group_ref) = refs[parts:]
    me = me_ref[0]
    cross = slots - bd
    sub = lax.broadcasted_iota(jnp.int32, (BLOCK, BLOCK), 0)
    ident = sub == lax.broadcasted_iota(jnp.int32, (BLOCK, BLOCK), 1)
    sub8 = lax.broadcasted_iota(jnp.int32, (8, BLOCK), 0)

    join_pieces(pieces, x_ref)
    p_ref[...] = jnp.zeros_like(p_ref)
    hards = []
    for q in range(nd):
        at = piece_of(q, me, pow2)
        span = slice(q * bd, (q + 1) * bd)
        p_ref[span, :] = -x_ref[at]
        hards.append(pick(g_ref[at, 3 * bd:4 * bd, :], [hard_ref[e] for e in range(ELEM)]))
    hard = jnp.concatenate(hards, axis=0)

    def set_charge(b, carry):
        pc_ref[b] = column(p_ref[pl.ds(b, 1), :])
        return carry

    def set_charges():
        if nb > 64:
            lax.fori_loop(0, nb, set_charge, 0)
            return
        turned = jnp.concatenate(split3(p_ref[0:nb]), axis=0).T.astype(jnp.bfloat16)
        ids = lax.broadcasted_iota(jnp.int32, (3 * nb, BLOCK), 0) % nb
        for b in range(0, nb, 2):
            chosen = [jnp.where(ids == b + m, 1.0, 0.0).astype(jnp.bfloat16) for m in range(2)]
            cols = jnp.dot(turned, jnp.concatenate(chosen, axis=1),
                           preferred_element_type=jnp.float32)
            for m in range(2):
                pc_ref[b + m] = cols[:, m * BLOCK:(m + 1) * BLOCK]

    pc_ref[nb] = jnp.zeros((BLOCK, BLOCK), jnp.float32)
    set_charges()

    def power(j, i):
        rel = r_ref[i] - mid_ref[j]
        size = jnp.sum(rel * rel, axis=0, keepdims=True)
        tile = jnp.where(sub8 == 3, size * -SCALE, jnp.where(sub8 == 4, 1.0, rel))
        p1, p2, p3 = split3(tile)
        right = jnp.concatenate([p1, p2, p1, p3, p1, p2], axis=0).astype(jnp.bfloat16)
        return jnp.dot(a_ref[j], right, preferred_element_type=jnp.float32)

    def gamma(j, i):
        return jnp.exp2(power(j, i))

    def own_gamma(b):
        return jnp.where(ident, 0.0, gamma(b, b))

    def entry(t, j, i):
        return t_ref[t] if stored else gamma(j, i)

    def own_entry(b):
        return t_ref[b] if stored else own_gamma(b)

    size = 4 if cross % 4 == 0 else 1

    def list_piece(q, groups):
        def list_group(k, g):
            group_ref[0, g] = q
            group_ref[1, g] = bd + size * k
            group_ref[2, g] = nb + 2 * (q * cross + size * k)
            return g + 1

        return lax.fori_loop(0, (count_ref[q] - bd + size - 1) // size, list_group, groups)

    groups = lax.fori_loop(0, nd, list_piece, 0)
    for extra in range(2):
        group_ref[0, groups + extra] = nd
        group_ref[1, groups + extra] = bd
        group_ref[2, groups + extra] = nb + 2 * nd * cross

    def ends_of(g):
        q, e, t = group_ref[0, g], group_ref[1, g], group_ref[2, g]
        ends = []
        for m in range(size):
            left, right = pair_ref[q, 0, e + m], pair_ref[q, 1, e + m]
            ends += [(t + 2 * m, left, right), (t + 2 * m + 1, right, left)]
        return ends

    def first_diag(b, carry):
        val = own_gamma(b)
        if stored:
            t_ref[b] = val
        s_ref[b] = fold(val)
        y_ref[b] = fold(val * pc_ref[b])
        return carry

    lax.fori_loop(0, nb, first_diag, 0, unroll=4)

    def raise_powers(g, e_ref):
        for m, (_, j, i) in enumerate(ends_of(g)):
            e_ref[m] = power(j, i)

    def first_step(g, e_ref):
        found = []
        for m, (t, j, i) in enumerate(ends_of(g)):
            val = jnp.exp2(e_ref[m])
            if stored:
                t_ref[t] = val
            found.append((i, fold(val), fold(val * pc_ref[j])))
        for i, one, two in found:
            s_ref[i] = s_ref[i] + one
            y_ref[i] = y_ref[i] + two

    def first_steps(k, carry):
        raise_powers(2 * k + 1, e1_ref)
        first_step(2 * k, e0_ref)
        raise_powers(jnp.minimum(2 * k + 2, groups), e0_ref)
        first_step(2 * k + 1, e1_ref)
        return carry

    raise_powers(0, e0_ref)
    lax.fori_loop(0, (groups + 1) // 2, first_steps, 0)

    def gathered(ref):
        return jnp.sum(ref[0:nb], axis=1)

    diag = hard + gathered(s_ref)

    def next_step(g, carry):
        found = [(i, fold(entry(t, j, i) * pc_ref[j])) for t, j, i in ends_of(g)]
        for i, one in found:
            y_ref[i] = y_ref[i] + one
        return carry

    def next_diag(b, carry):
        y_ref[b] = fold(own_entry(b) * pc_ref[b])
        return carry

    def matvec():
        set_charges()
        lax.fori_loop(0, nb, next_diag, 0, unroll=8)
        lax.fori_loop(0, groups, next_step, 0)

    def total(vals):
        return jnp.sum(jnp.sum(vals, axis=0, keepdims=True), axis=1, keepdims=True)

    res = p_ref[0:nb]
    p = res
    x = jnp.zeros_like(res)
    rho = total(res * res)
    for it in range(ITERS):
        if it:
            matvec()
        image = diag * p + gathered(y_ref)
        step = rho / total(p * image)
        x = x + step * p
        if it + 1 < ITERS:
            res = res - step * image
            rho2 = total(res * res)
            p = res + (rho2 / rho) * p
            rho = rho2
            p_ref[0:nb] = p
    p_ref[0:nb] = x
    for a in range(bd):
        charge_ref[a:a + 1, :] = p_ref[pl.ds(me * bd + a, 1), :]
        set_charge(me * bd + a, 0)
    mine = jnp.concatenate([charge_ref[a:a + 1, :] for a in range(bd)], axis=1)
    width = bd * BLOCK

    several = 4

    bf16 = jnp.bfloat16
    zero16 = jnp.zeros((16, width), bf16)
    one16 = jnp.ones((16, width), bf16)
    lines = lax.broadcasted_iota(jnp.int32, (16, width), 0).astype(jnp.float32)
    wanted = [(lines + 16.0 * k).astype(bf16) for k in range(max(BLOCK, nb) // 16)]

    def spread(row):
        return jnp.broadcast_to(row, (16, width)).astype(bf16)

    def scatter(k, acc):
        lefts = []
        rights = []
        for m in range(several):
            s = k * several + m
            idx = nbr_ref[pl.ds(s, 1), :]
            block = spread((idx >> 7).astype(jnp.float32))
            lane = spread((idx & 127).astype(jnp.float32))
            rights.append(jnp.concatenate(
                [jnp.where(wanted[r] == lane, one16, zero16) for r in range(BLOCK // 16)], axis=0))
            hits = [wanted[r] == block for r in range(nb // 16)]
            upper = []
            lower = []
            for d in range(3):
                val = push_ref[d, pl.ds(s, 1), :] * mine
                top = val.astype(bf16).astype(jnp.float32)
                top16 = spread(top)
                low16 = spread(val - top)
                upper += [jnp.where(hit, top16, zero16) for hit in hits]
                lower += [jnp.where(hit, low16, zero16) for hit in hits]
            lefts.append(jnp.concatenate(upper + lower, axis=0))
        return acc + lax.dot_general(jnp.concatenate(lefts, axis=1),
                                     jnp.concatenate(rights, axis=1), (((1,), (1,)), ((), ())),
                                     preferred_element_type=jnp.float32)

    acc = lax.fori_loop(0, NBR // several, scatter, jnp.zeros((6 * nb, BLOCK), jnp.float32))
    acc = acc[:3 * nb] + acc[3 * nb:]
    for q in range(nd):
        for d in range(3):
            part_ref[q, d * bd:(d + 1) * bd, :] = acc[d * nb + q * bd:d * nb + (q + 1) * bd]

    def moments(rel, weights, side):
        tile = jnp.where(sub8 == 3, 1.0, rel)
        rows = jnp.concatenate(split3(tile) + [jnp.zeros_like(rel)], axis=0).astype(jnp.bfloat16)
        out = sum(lax.dot_general(rows, w, (((1,), (side,)), ((), ())),
                                  preferred_element_type=jnp.float32) for w in weights)
        return out[0:8] + out[8:16] + out[16:24]

    def force_of(rel, found):
        return (rel * found[3:4] - found) * (0.5 / sigma_sq)

    def weigh(val, j, i):
        both = pc_ref[j] + p_ref[pl.ds(i, 1), :]
        weight = val * (both * both)
        top = weight.astype(jnp.bfloat16)
        return top, (weight - top.astype(jnp.float32)).astype(jnp.bfloat16)

    s_ref[...] = jnp.zeros_like(s_ref)
    for a in range(bd):
        b = me * bd + a
        rel = r_ref[b] - mid_ref[b]
        force = force_of(rel, moments(rel, weigh(own_entry(b), b, b), 0))
        lanes = slice(a * BLOCK, (a + 1) * BLOCK)
        for d in range(3):
            away = jnp.sum(push_ref[d, :, lanes], axis=0, keepdims=True) * charge_ref[a:a + 1, :]
            force = jnp.where(sub8 == d, force - away, force)
        s_ref[b] = force
    piece = piece_of(me, me, pow2)
    together = 4 if cross % 4 == 0 else 1

    def pair_force(k, carry):
        found = []
        for m in range(together):
            e = k * together + m
            j, i = pair_ref[piece, 0, bd + e], pair_ref[piece, 1, bd + e]
            mid = mid_ref[j]
            rel_j = r_ref[j] - mid
            rel_i = r_ref[i] - mid
            weights = weigh(entry(nb + 2 * (piece * cross + e), j, i), j, i)
            found.append((i, force_of(rel_i, moments(rel_j, weights, 0))))
            found.append((j, force_of(rel_j, moments(rel_i, weights, 1))))
        for b, force in found:
            s_ref[b] = s_ref[b] + force
        return carry

    lax.fori_loop(0, (count_ref[piece] - bd + together - 1) // together, pair_force, 0)
    for q in range(nd):
        for d in range(3):
            for r in range(bd):
                at = slice(d * bd + r, d * bd + r + 1)
                part_ref[q, at, :] = part_ref[q, at, :] + s_ref[q * bd + r, d:d + 1, :]


def gather_all(own, n, beside=()):
    if n & (n - 1):
        return [lax.all_gather(own, "blk")], beside

    def swap(vals, step):
        return lax.ppermute(vals, "blk", [(i, i ^ step) for i in range(n)])

    got = own[None]
    step = 1
    while step < n:
        got = jnp.concatenate([got, swap(got, step)], axis=0)
        if step == n // 4:
            got, beside = lax.optimization_barrier((got, beside))
        step *= 2
    return [got], beside


def on_device(positions, species, neighbors, pair_lists, hardness, w_first, b_first, w_second,
              b_second, w_out, b_out):
    n = lax.axis_size("blk")
    me = lax.axis_index("blk")
    atoms = positions.shape[1]
    bd = atoms // BLOCK
    nb = bd * n
    slots = pair_lists.shape[1]
    hid = w_first.shape[1]
    f32 = jnp.float32
    kind = species.reshape(1, atoms)
    small = pltpu.CompilerParams(vmem_limit_bytes=24 << 20)
    raw = (positions, kind, pair_lists, neighbors, b_first, b_second, w_out, b_out.reshape(1, ELEM))
    raw = tuple(pltpu.with_memory_space_constraint(r, pltpu.HBM) for r in raw)
    own, pos, kinds, _, nbr, b1, b2, wo, bo = pl.pallas_call(
        functools.partial(pack_kernel, len(raw)),
        out_shape=(jax.ShapeDtypeStruct((PACK, BLOCK), f32),)
        + tuple(jax.ShapeDtypeStruct(r.shape, r.dtype) for r in raw),
        in_specs=[spec(pltpu.HBM)] * len(raw), out_specs=(spec(VM),) * (1 + len(raw)),
        scratch_shapes=[pltpu.SemaphoreType.DMA((len(raw),))],
        compiler_params=small, name="pack",
    )(*raw)
    pow2 = n & (n - 1) == 0
    places, _ = gather_all(own, n)
    chi, offs, hidden, whole = pl.pallas_call(
        functools.partial(chi_kernel, pow2, n, bd, len(places)),
        out_shape=(jax.ShapeDtypeStruct((bd, BLOCK), f32),
                   jax.ShapeDtypeStruct((4, NBR, atoms), f32),
                   jax.ShapeDtypeStruct((2, hid, atoms), f32),
                   jax.ShapeDtypeStruct((n, PACK, BLOCK), f32)),
        in_specs=[spec(SM)] + [spec(VM)] * (9 + len(places)),
        out_specs=(spec(VM),) * 4,
        scratch_shapes=[VM((DESC, atoms), f32)],
        compiler_params=small,
        name="chi",
    )(me[None], *places, pos, nbr, kinds, w_first, b1, w_second, b2, wo, bo)
    tiles = pl.pallas_call(
        functools.partial(tile_kernel, pow2, n, bd, nb),
        out_shape=(jax.ShapeDtypeStruct((nb + 1, 8, BLOCK), f32),
                   jax.ShapeDtypeStruct((nb + 1, 8, BLOCK), f32),
                   jax.ShapeDtypeStruct((nb + 1, BLOCK, 48), jnp.bfloat16)),
        in_specs=[spec(SM), spec(VM)],
        out_specs=(spec(VM),) * 3,
        compiler_params=small,
        name="tiles",
    )(me[None], whole)
    all_chi, (rows, mids, left) = gather_all(chi, n, tiles)
    lists = whole[:, 4 * bd:4 * bd + 2, :slots].astype(jnp.int32)
    counts = jnp.sum((lists[:, 0] >= 0).astype(jnp.int32), axis=1)
    lists = jnp.where(lists < 0, nb, lists)
    lists = jnp.pad(lists, ((0, 1), (0, 0), (0, 0)), constant_values=nb)
    push = pl.pallas_call(
        functools.partial(pull_kernel, bd),
        out_shape=jax.ShapeDtypeStruct((3, NBR, atoms), f32),
        in_specs=[spec(VM)] * 6,
        out_specs=spec(VM),
        scratch_shapes=[VM((DESC, atoms), f32)],
        compiler_params=small,
        name="pull",
    )(kinds, offs, hidden, w_first, w_second, wo)
    entries = nb + 2 * (n * slots - nb)
    stored = entries * BLOCK * BLOCK * 4 <= STORE_LIMIT
    charges, part = pl.pallas_call(
        functools.partial(solve_kernel, pow2, n, bd, nb, slots, stored, len(all_chi)),
        out_shape=(jax.ShapeDtypeStruct((bd, BLOCK), f32),
                   jax.ShapeDtypeStruct((n, 3 * bd, BLOCK), f32)),
        in_specs=[spec(SM)] * 4 + [spec(VM)] * (6 + len(all_chi)),
        out_specs=(spec(VM),) * 2,
        scratch_shapes=[VM((n, bd, BLOCK), f32), VM((nb + 8, BLOCK), f32),
                        VM((nb + 1, BLOCK, BLOCK), f32), VM((nb + 1, 8, BLOCK), f32),
                        VM((nb + 1, 8, BLOCK), f32),
                        VM((entries + 8 if stored else 1, BLOCK, BLOCK), f32),
                        VM((8, BLOCK, BLOCK), f32), VM((8, BLOCK, BLOCK), f32),
                        SM((3, n * (slots - bd) + 2), jnp.int32)],
        compiler_params=pltpu.CompilerParams(vmem_limit_bytes=(42 if stored else 58) << 20),
        name="solve",
    )(me[None], lists, counts, hardness, *all_chi, whole, rows, mids, left, push, nbr)
    swapped = lax.all_to_all(part, "blk", 0, 0)
    forces = jnp.sum(swapped, axis=0)
    return charges.reshape(atoms), forces.reshape(3, atoms)


def solution(mesh):
    both = ("cell", "blk")
    placed = (P(None, both), P(both), P(None, both), P(None, both)) + (P(),) * 7
    return jax.shard_map(
        on_device,
        mesh=mesh,
        in_specs=placed,
        out_specs=(P(both), P(None, both)),
        check_vma=False,
    )
```

```python
import functools
import math

import jax
import jax.numpy as jnp
import numpy as np
from jax import lax
from jax.experimental import pallas as pl
from jax.experimental.pallas import tpu as pltpu
from jax.sharding import PartitionSpec as P

ELEM = 4
RAD = 16
DESC = ELEM * RAD
BLOCK = 128
NBR = 32
ITERS = 3
PACK = 24
STORE_LIMIT = 36 << 20

coulomb_scale = 0.5
sigma_sq = 4.0
cutoff_sq = 49.0
highest = lax.Precision.HIGHEST
RATES = [0.005 * 200.0 ** (k / (RAD - 1)) for k in range(RAD)]
VM = pltpu.VMEM
SM = pltpu.SMEM
SCALE = math.log2(math.e) / (2.0 * sigma_sq)


def spec(space):
    return pl.BlockSpec(memory_space=space)


def piece_of(q, me, pow2):
    return q ^ me if pow2 else q


def dot(a, b, lhs=1):
    return lax.dot_general(a, b, (((lhs,), (0,)), ((), ())), precision=highest,
                           preferred_element_type=jnp.float32)


def column(row):
    return jnp.broadcast_to(row, (BLOCK, BLOCK)).T


def pick(kind, mats):
    out = jnp.where(kind == 0, mats[0], 0.0)
    for e in range(1, ELEM):
        out = jnp.where(kind == e, mats[e], out)
    return out


def one_hot(kind):
    ids = lax.broadcasted_iota(jnp.int32, (ELEM, kind.shape[1]), 0)
    return jnp.where(ids == kind, 1.0, 0.0)


def pack_kernel(count, *refs):
    sources = refs[:count]
    own_ref = refs[count]
    held = refs[count + 1:2 * count + 1]
    sems = refs[-1]
    copies = [pltpu.make_async_copy(sources[k], held[k], sems.at[k]) for k in range(count)]
    for copy in copies:
        copy.start()
    own_ref[...] = jnp.zeros_like(own_ref)
    for copy in copies[:3]:
        copy.wait()
    pos_ref, kind_ref, pairs_ref = held[:3]
    bd = pos_ref.shape[1] // BLOCK
    for a in range(bd):
        lanes = slice(a * BLOCK, (a + 1) * BLOCK)
        for d in range(3):
            own_ref[d * bd + a:d * bd + a + 1, :] = pos_ref[d:d + 1, lanes]
        own_ref[3 * bd + a:3 * bd + a + 1, :] = kind_ref[:, lanes].astype(jnp.float32)
    slots = pairs_ref.shape[1]
    for side in range(2):
        own_ref[4 * bd + side:4 * bd + side + 1, :slots] = (
            pairs_ref[side:side + 1, :].astype(jnp.float32))
    for copy in copies[3:]:
        copy.wait()


def join_pieces(pieces, out_ref):
    first = 0
    for piece in pieces:
        count = piece.shape[0]
        out_ref[first:first + count] = piece[...]
        first += count


def chi_kernel(pow2, nd, bd, parts, me_ref, *refs):
    pieces = refs[:parts]
    (pos_ref, nbr_ref, kind_ref, w1, b1, w2, b2, wo, bo,
     chi_ref, d_ref, h_ref, g_ref, f_ref) = refs[parts:]
    me = me_ref[0]
    chunk = min(nd, 8)
    join_pieces(pieces, g_ref)
    for a in range(bd):
        lanes = slice(a * BLOCK, (a + 1) * BLOCK)

        def group(g, carry):
            rows8 = pl.ds(pl.multiple_of(g * 8, 8), 8)
            idx = nbr_ref[rows8, lanes]
            hi = idx >> 7
            lo = idx & 127

            def look(part, vals):
                for step in range(chunk):
                    q = part * chunk + step
                    at = piece_of(q, me, pow2)
                    for r in range(bd):
                        hit = hi == q * bd + r
                        new = []
                        for d in range(4):
                            row = jnp.broadcast_to(g_ref[at, d * bd + r:d * bd + r + 1, :],
                                                   (8, BLOCK))
                            new.append(jnp.where(hit, jnp.take_along_axis(row, lo, axis=1),
                                                 vals[d]))
                        vals = tuple(new)
                return vals

            vals = (jnp.zeros((8, BLOCK), jnp.float32),) * 4
            if nd == chunk:
                vals = look(0, vals)
            else:
                vals = lax.fori_loop(0, nd // chunk, look, vals)
            live = idx >= 0
            for d in range(3):
                d_ref[d, rows8, lanes] = jnp.where(live, pos_ref[d:d + 1, lanes] - vals[d], 0.0)
            d_ref[3, rows8, lanes] = jnp.where(live, vals[3], -1.0)
            return carry

        lax.fori_loop(0, NBR // 8, group, 0, unroll=4 if nd == chunk else 1)
        offs = [d_ref[d, :, lanes] for d in range(3)]
        nk = d_ref[3, :, lanes]
        r2 = offs[0] * offs[0] + offs[1] * offs[1] + offs[2] * offs[2]
        u = 1.0 - r2 * (1.0 / cutoff_sq)
        shell = u * u * (ELEM / NBR)
        for k in range(RAD):
            val = shell * jnp.exp(-RATES[k] * r2)
            for e in range(ELEM):
                f_ref[e * RAD + k:e * RAD + k + 1, lanes] = jnp.sum(
                    jnp.where(nk == e, val, 0.0), axis=0, keepdims=True)
    kind = kind_ref[...]
    hot = one_hot(kind)
    feats = f_ref[...]
    h1 = jnp.tanh(pick(kind, [dot(w1[e], feats) for e in range(ELEM)]) + dot(b1[...], hot, 0))
    h2 = jnp.tanh(pick(kind, [dot(w2[e], h1) for e in range(ELEM)]) + dot(b2[...], hot, 0))
    h_ref[0] = h1
    h_ref[1] = h2
    chi = jnp.sum(dot(wo[...], hot, 0) * h2, axis=0, keepdims=True) + dot(bo[...], hot)
    for a in range(bd):
        chi_ref[a:a + 1, :] = chi[:, a * BLOCK:(a + 1) * BLOCK]


def fold(vals):
    tiles = vals.reshape(BLOCK // 8, 8, BLOCK)
    terms = [tiles[k] for k in range(BLOCK // 8)]
    while len(terms) > 1:
        terms = [terms[k] + terms[k + 1] for k in range(0, len(terms), 2)]
    return terms[0]


def split3(vals):
    parts = []
    for _ in range(3):
        top = vals.astype(jnp.bfloat16).astype(jnp.float32)
        parts.append(top)
        vals = vals - top
    return parts


def tile_kernel(pow2, nd, bd, nb, me_ref, g_ref, r_ref, mid_ref, a_ref):
    me = me_ref[0]
    sub8 = lax.broadcasted_iota(jnp.int32, (8, BLOCK), 0)
    r_ref[...] = jnp.zeros_like(r_ref)
    for q in range(nd):
        at = piece_of(q, me, pow2)
        for r in range(bd):
            for d in range(3):
                r_ref[q * bd + r, d:d + 1, :] = g_ref[at, d * bd + r:d * bd + r + 1, :]

    def set_block(b, carry):
        mid = jnp.broadcast_to(r_ref[b][:, 0:1], (8, BLOCK))
        mid_ref[b] = mid
        rel = r_ref[b] - mid
        size = jnp.sum(rel * rel, axis=0, keepdims=True)
        tile = jnp.where(sub8 == 3, 1.0,
                         jnp.where(sub8 == 4, size * -SCALE - 1.0, rel * (2.0 * SCALE)))
        q1, q2, q3 = split3(tile)
        gap = jnp.zeros((16, BLOCK), jnp.float32)
        half = [q1, q1, q2, q1, q3, q2, gap]
        a_ref[b] = jnp.concatenate(half + half, axis=0).T.astype(jnp.bfloat16)
        return carry

    lax.fori_loop(0, nb + 1, set_block, 0, unroll=11 if nb + 1 == 33 else 1)


def pull_kernel(bd, kind_ref, d_ref, h_ref, w1, w2, wo, push_ref, f_ref):
    kind = kind_ref[...]
    h1 = h_ref[0]
    h2 = h_ref[1]
    pre2 = dot(wo[...], one_hot(kind), 0) * (1.0 - h2 * h2)
    pre1 = sum(dot(w2[e], jnp.where(kind == e, pre2, 0.0), 0) for e in range(ELEM))
    pre1 = pre1 * (1.0 - h1 * h1)
    f_ref[...] = sum(dot(w1[e], jnp.where(kind == e, pre1, 0.0), 0)
                     for e in range(ELEM)) * (ELEM / NBR)
    for a in range(bd):
        lanes = slice(a * BLOCK, (a + 1) * BLOCK)
        offs = [d_ref[d, :, lanes] for d in range(3)]
        nk = d_ref[3, :, lanes]
        r2 = offs[0] * offs[0] + offs[1] * offs[1] + offs[2] * offs[2]
        u = 1.0 - r2 * (1.0 / cutoff_sq)
        s1 = jnp.zeros_like(r2)
        s2 = jnp.zeros_like(r2)
        for k in range(RAD):
            sel = jnp.zeros_like(r2)
            for e in range(ELEM):
                sel = jnp.where(nk == e, f_ref[e * RAD + k:e * RAD + k + 1, lanes], sel)
            term = sel * jnp.exp(-RATES[k] * r2)
            s1 = s1 + term
            s2 = s2 + RATES[k] * term
        grad = -u * ((2.0 / cutoff_sq) * s1 + u * s2)
        for d in range(3):
            push_ref[d, :, lanes] = 2.0 * grad * offs[d]


def solve_kernel(pow2, nd, bd, nb, slots, stored, parts, me_ref, pair_ref, count_ref, hard_ref,
                 *refs):
    pieces = refs[:parts]
    (g_ref, r_ref, mid_ref, a_ref, push_ref, nbr_ref, charge_ref, part_ref, x_ref, p_ref, pc_ref,
     y_ref, s_ref, t_ref, e0_ref, e1_ref, group_ref) = refs[parts:]
    me = me_ref[0]
    cross = slots - bd
    sub = lax.broadcasted_iota(jnp.int32, (BLOCK, BLOCK), 0)
    ident = sub == lax.broadcasted_iota(jnp.int32, (BLOCK, BLOCK), 1)
    sub8 = lax.broadcasted_iota(jnp.int32, (8, BLOCK), 0)

    join_pieces(pieces, x_ref)
    p_ref[...] = jnp.zeros_like(p_ref)
    hards = []
    for q in range(nd):
        at = piece_of(q, me, pow2)
        span = slice(q * bd, (q + 1) * bd)
        p_ref[span, :] = -x_ref[at]
        hards.append(pick(g_ref[at, 3 * bd:4 * bd, :], [hard_ref[e] for e in range(ELEM)]))
    hard = jnp.concatenate(hards, axis=0)

    def set_charge(b, carry):
        pc_ref[b] = column(p_ref[pl.ds(b, 1), :])
        return carry

    def set_charges():
        if nb > 64:
            lax.fori_loop(0, nb, set_charge, 0)
            return
        turned = jnp.concatenate(split3(p_ref[0:nb]), axis=0).T.astype(jnp.bfloat16)
        ids = lax.broadcasted_iota(jnp.int32, (3 * nb, BLOCK), 0) % nb
        for b in range(0, nb, 2):
            chosen = [jnp.where(ids == b + m, 1.0, 0.0).astype(jnp.bfloat16) for m in range(2)]
            cols = jnp.dot(turned, jnp.concatenate(chosen, axis=1),
                           preferred_element_type=jnp.float32)
            for m in range(2):
                pc_ref[b + m] = cols[:, m * BLOCK:(m + 1) * BLOCK]

    pc_ref[nb] = jnp.zeros((BLOCK, BLOCK), jnp.float32)
    set_charges()

    low_lanes = lax.broadcasted_iota(jnp.int32, (BLOCK, BLOCK), 1) < BLOCK // 2

    def right_side(j, i):
        rel = r_ref[i] - mid_ref[j]
        size = jnp.sum(rel * rel, axis=0, keepdims=True)
        tile = jnp.where(sub8 == 3, size * -SCALE, jnp.where(sub8 == 4, 1.0, rel))
        p1, p2, p3 = split3(tile)
        return jnp.concatenate([p1, p2, p1, p3, p1, p2], axis=0).astype(jnp.bfloat16)

    def empty(rows):
        return jnp.zeros((rows, BLOCK), jnp.bfloat16)

    def slot_of(q):
        return q ^ me if nd == 8 else q

    def power(j, i):
        right = jnp.concatenate([right_side(j, i), empty(80)], axis=0)
        return jnp.dot(a_ref[j], right, preferred_element_type=jnp.float32)

    def two_powers(j, i, j2, i2):
        left = jnp.where(low_lanes, a_ref[j].astype(jnp.float32),
                         a_ref[j2].astype(jnp.float32)).astype(jnp.bfloat16)
        right = jnp.concatenate([
            jnp.concatenate([right_side(j, i), empty(80)], axis=0),
            jnp.concatenate([empty(64), right_side(j2, i2), empty(16)], axis=0)], axis=1)
        both = jnp.dot(left, right, preferred_element_type=jnp.float32)
        return both[:, :BLOCK], both[:, BLOCK:]

    def gamma(j, i):
        return jnp.exp2(power(j, i))

    def own_gamma(b):
        return jnp.where(ident, 0.0, gamma(b, b))

    def entry(t, j, i):
        return t_ref[t] if stored else gamma(j, i)

    def own_entry(b):
        return t_ref[b] if stored else own_gamma(b)

    size = 4 if cross % 4 == 0 else 1

    def list_piece(q, groups):
        def list_group(k, g):
            group_ref[0, g] = q
            group_ref[1, g] = bd + size * k
            group_ref[2, g] = nb + 2 * (q * cross + size * k)
            return g + 1

        return lax.fori_loop(0, (count_ref[q] - bd + size - 1) // size, list_group, groups)

    groups = lax.fori_loop(0, nd, list_piece, 0)
    for extra in range(2):
        group_ref[0, groups + extra] = nd
        group_ref[1, groups + extra] = bd
        group_ref[2, groups + extra] = nb + 2 * nd * cross

    def ends_of(g):
        q, e, t = group_ref[0, g], group_ref[1, g], group_ref[2, g]
        ends = []
        for m in range(size):
            left, right = pair_ref[q, 0, e + m], pair_ref[q, 1, e + m]
            ends += [(t + 2 * m, left, right), (t + 2 * m + 1, right, left)]
        return ends

    def first_diag(k, carry):
        first = 2 * k
        for m, exponent in enumerate(two_powers(first, first, first + 1, first + 1)):
            b = first + m
            val = jnp.where(ident, 0.0, jnp.exp2(exponent))
            if stored:
                t_ref[b] = val
            s_ref[b] = fold(val)
            y_ref[b] = fold(val * pc_ref[b])
        return carry

    lax.fori_loop(0, nb // 2, first_diag, 0, unroll=4)

    def raise_powers(g, e_ref):
        ends = ends_of(g)
        for m in range(0, len(ends), 2):
            e_ref[m], e_ref[m + 1] = two_powers(*ends[m][1:], *ends[m + 1][1:])

    def first_step(g, e_ref):
        found = []
        for m, (t, j, i) in enumerate(ends_of(g)):
            val = jnp.exp2(e_ref[m])
            if stored:
                t_ref[t] = val
            found.append((i, fold(val), fold(val * pc_ref[j])))
        for i, one, two in found:
            s_ref[i] = s_ref[i] + one
            y_ref[i] = y_ref[i] + two

    def first_steps(k, carry):
        raise_powers(2 * k + 1, e1_ref)
        first_step(2 * k, e0_ref)
        raise_powers(jnp.minimum(2 * k + 2, groups), e0_ref)
        first_step(2 * k + 1, e1_ref)
        return carry

    raise_powers(0, e0_ref)
    lax.fori_loop(0, (groups + 1) // 2, first_steps, 0)

    def gathered(ref):
        return jnp.sum(ref[0:nb], axis=1)

    diag = hard + gathered(s_ref)

    def next_step(g, carry):
        found = [(i, fold(entry(t, j, i) * pc_ref[j])) for t, j, i in ends_of(g)]
        for i, one in found:
            y_ref[i] = y_ref[i] + one
        return carry

    def next_diag(b, carry):
        y_ref[b] = fold(own_entry(b) * pc_ref[b])
        return carry

    def matvec():
        set_charges()
        lax.fori_loop(0, nb, next_diag, 0, unroll=8)
        lax.fori_loop(0, groups, next_step, 0)

    def total(vals):
        return jnp.sum(jnp.sum(vals, axis=0, keepdims=True), axis=1, keepdims=True)

    res = p_ref[0:nb]
    p = res
    x = jnp.zeros_like(res)
    rho = total(res * res)
    for it in range(ITERS):
        if it:
            matvec()
        image = diag * p + gathered(y_ref)
        step = rho / total(p * image)
        x = x + step * p
        if it + 1 < ITERS:
            res = res - step * image
            rho2 = total(res * res)
            p = res + (rho2 / rho) * p
            rho = rho2
            p_ref[0:nb] = p
    p_ref[0:nb] = x
    for a in range(bd):
        charge_ref[a:a + 1, :] = p_ref[pl.ds(me * bd + a, 1), :]
        set_charge(me * bd + a, 0)
    mine = jnp.concatenate([charge_ref[a:a + 1, :] for a in range(bd)], axis=1)
    width = bd * BLOCK

    several = 4

    bf16 = jnp.bfloat16
    zero16 = jnp.zeros((16, width), bf16)
    one16 = jnp.ones((16, width), bf16)
    lines = lax.broadcasted_iota(jnp.int32, (16, width), 0).astype(jnp.float32)
    wanted = [(lines + 16.0 * k).astype(bf16) for k in range(max(BLOCK, nb) // 16)]

    def spread(row):
        return jnp.broadcast_to(row, (16, width)).astype(bf16)

    def scatter(k, acc):
        lefts = []
        rights = []
        for m in range(several):
            s = k * several + m
            idx = nbr_ref[pl.ds(s, 1), :]
            block = spread((idx >> 7).astype(jnp.float32))
            lane = spread((idx & 127).astype(jnp.float32))
            rights.append(jnp.concatenate(
                [jnp.where(wanted[r] == lane, one16, zero16) for r in range(BLOCK // 16)], axis=0))
            hits = [wanted[r] == block for r in range(nb // 16)]
            upper = []
            lower = []
            for d in range(3):
                val = push_ref[d, pl.ds(s, 1), :] * mine
                top = val.astype(bf16).astype(jnp.float32)
                top16 = spread(top)
                low16 = spread(val - top)
                upper += [jnp.where(hit, top16, zero16) for hit in hits]
                lower += [jnp.where(hit, low16, zero16) for hit in hits]
            lefts.append(jnp.concatenate(upper + lower, axis=0))
        return acc + lax.dot_general(jnp.concatenate(rights, axis=1),
                                     jnp.concatenate(lefts, axis=1), (((1,), (1,)), ((), ())),
                                     preferred_element_type=jnp.float32)

    acc = lax.fori_loop(0, NBR // several, scatter, jnp.zeros((BLOCK, 6 * nb), jnp.float32))
    acc = acc.T
    acc = acc[:3 * nb] + acc[3 * nb:]
    for q in range(nd):
        for d in range(3):
            part_ref[slot_of(q), d * bd:(d + 1) * bd, :] = acc[d * nb + q * bd:d * nb + (q + 1) * bd]

    def moments(rel, weights, side):
        tile = jnp.where(sub8 == 3, 1.0, rel)
        rows = jnp.concatenate(split3(tile) + [jnp.zeros_like(rel)], axis=0).astype(jnp.bfloat16)
        out = sum(lax.dot_general(rows, w, (((1,), (side,)), ((), ())),
                                  preferred_element_type=jnp.float32) for w in weights)
        return out[0:8] + out[8:16] + out[16:24]

    def force_of(rel, found):
        return (rel * found[3:4] - found) * (0.5 / sigma_sq)

    def weigh(val, j, i):
        both = pc_ref[j] + p_ref[pl.ds(i, 1), :]
        weight = val * (both * both)
        top = weight.astype(jnp.bfloat16)
        return top, (weight - top.astype(jnp.float32)).astype(jnp.bfloat16)

    s_ref[...] = jnp.zeros_like(s_ref)
    for a in range(bd):
        b = me * bd + a
        rel = r_ref[b] - mid_ref[b]
        force = force_of(rel, moments(rel, weigh(own_entry(b), b, b), 0))
        lanes = slice(a * BLOCK, (a + 1) * BLOCK)
        for d in range(3):
            away = jnp.sum(push_ref[d, :, lanes], axis=0, keepdims=True) * charge_ref[a:a + 1, :]
            force = jnp.where(sub8 == d, force - away, force)
        s_ref[b] = force
    piece = piece_of(me, me, pow2)
    together = 4 if cross % 4 == 0 else 1

    def pair_force(k, carry):
        found = []
        for m in range(together):
            e = k * together + m
            j, i = pair_ref[piece, 0, bd + e], pair_ref[piece, 1, bd + e]
            mid = mid_ref[j]
            rel_j = r_ref[j] - mid
            rel_i = r_ref[i] - mid
            weights = weigh(entry(nb + 2 * (piece * cross + e), j, i), j, i)
            found.append((i, force_of(rel_i, moments(rel_j, weights, 0))))
            found.append((j, force_of(rel_j, moments(rel_i, weights, 1))))
        for b, force in found:
            s_ref[b] = s_ref[b] + force
        return carry

    lax.fori_loop(0, (count_ref[piece] - bd + together - 1) // together, pair_force, 0)
    for q in range(nd):
        for d in range(3):
            for r in range(bd):
                at = slice(d * bd + r, d * bd + r + 1)
                part_ref[slot_of(q), at, :] = part_ref[slot_of(q), at, :] + s_ref[q * bd + r, d:d + 1, :]


def swap(vals, step, n):
    return lax.ppermute(vals, "blk", [(i, i ^ step) for i in range(n)])


def gather_far_first(own, n):
    if n & (n - 1):
        return [lax.all_gather(own, "blk")]
    got = own[None]
    step = n // 2
    while step:
        both = jnp.stack([got, swap(got, step, n)], axis=1)
        got = both.reshape((2 * got.shape[0],) + own.shape)
        step //= 2
    return [got]


def gather_near_first(own, n, beside):
    if n & (n - 1):
        return [lax.all_gather(own, "blk")], beside
    got = own[None]
    step = 1
    while step < n:
        got = jnp.concatenate([got, swap(got, step, n)], axis=0)
        if step == 1:
            got, beside = lax.optimization_barrier((got, beside))
            if n == 8:
                return [got] + [swap(got, k, n) for k in (2, 4, 6)], beside
        step *= 2
    return [got], beside


def reduce_parts(part, n):
    if n != 8:
        return jnp.sum(lax.all_to_all(part, "blk", 0, 0), axis=0)
    mine = part[0::2] + swap(part[1::2], 1, n)
    far = [swap(mine[k], 2 * k, n) for k in (1, 2, 3)]
    return mine[0] + far[0] + far[1] + far[2]


def on_device(positions, species, neighbors, pair_lists, hardness, w_first, b_first, w_second,
              b_second, w_out, b_out):
    n = lax.axis_size("blk")
    me = lax.axis_index("blk")
    atoms = positions.shape[1]
    bd = atoms // BLOCK
    nb = bd * n
    slots = pair_lists.shape[1]
    hid = w_first.shape[1]
    f32 = jnp.float32
    kind = species.reshape(1, atoms)
    small = pltpu.CompilerParams(vmem_limit_bytes=24 << 20)
    raw = (positions, kind, pair_lists, neighbors, b_first, b_second, w_out, b_out.reshape(1, ELEM))
    raw = tuple(pltpu.with_memory_space_constraint(r, pltpu.HBM) for r in raw)
    own, pos, kinds, _, nbr, b1, b2, wo, bo = pl.pallas_call(
        functools.partial(pack_kernel, len(raw)),
        out_shape=(jax.ShapeDtypeStruct((PACK, BLOCK), f32),)
        + tuple(jax.ShapeDtypeStruct(r.shape, r.dtype) for r in raw),
        in_specs=[spec(pltpu.HBM)] * len(raw), out_specs=(spec(VM),) * (1 + len(raw)),
        scratch_shapes=[pltpu.SemaphoreType.DMA((len(raw),))],
        compiler_params=small, name="pack",
    )(*raw)
    pow2 = n & (n - 1) == 0
    places = gather_far_first(own, n)
    chi, offs, hidden, whole = pl.pallas_call(
        functools.partial(chi_kernel, pow2, n, bd, len(places)),
        out_shape=(jax.ShapeDtypeStruct((bd, BLOCK), f32),
                   jax.ShapeDtypeStruct((4, NBR, atoms), f32),
                   jax.ShapeDtypeStruct((2, hid, atoms), f32),
                   jax.ShapeDtypeStruct((n, PACK, BLOCK), f32)),
        in_specs=[spec(SM)] + [spec(VM)] * (9 + len(places)),
        out_specs=(spec(VM),) * 4,
        scratch_shapes=[VM((DESC, atoms), f32)],
        compiler_params=small,
        name="chi",
    )(me[None], *places, pos, nbr, kinds, w_first, b1, w_second, b2, wo, bo)
    push = pl.pallas_call(
        functools.partial(pull_kernel, bd),
        out_shape=jax.ShapeDtypeStruct((3, NBR, atoms), f32),
        in_specs=[spec(VM)] * 6,
        out_specs=spec(VM),
        scratch_shapes=[VM((DESC, atoms), f32)],
        compiler_params=small,
        name="pull",
    )(kinds, offs, hidden, w_first, w_second, wo)
    all_chi, push = gather_near_first(chi, n, push)
    rows, mids, left = pl.pallas_call(
        functools.partial(tile_kernel, pow2, n, bd, nb),
        out_shape=(jax.ShapeDtypeStruct((nb + 1, 8, BLOCK), f32),
                   jax.ShapeDtypeStruct((nb + 1, 8, BLOCK), f32),
                   jax.ShapeDtypeStruct((nb + 1, BLOCK, BLOCK), jnp.bfloat16)),
        in_specs=[spec(SM), spec(VM)],
        out_specs=(spec(VM),) * 3,
        compiler_params=small,
        name="tiles",
    )(me[None], whole)
    lists = whole[:, 4 * bd:4 * bd + 2, :slots].astype(jnp.int32)
    counts = jnp.sum((lists[:, 0] >= 0).astype(jnp.int32), axis=1)
    lists = jnp.where(lists < 0, nb, lists)
    lists = jnp.pad(lists, ((0, 1), (0, 0), (0, 0)), constant_values=nb)
    entries = nb + 2 * (n * slots - nb)
    stored = entries * BLOCK * BLOCK * 4 <= STORE_LIMIT
    charges, part = pl.pallas_call(
        functools.partial(solve_kernel, pow2, n, bd, nb, slots, stored, len(all_chi)),
        out_shape=(jax.ShapeDtypeStruct((bd, BLOCK), f32),
                   jax.ShapeDtypeStruct((n, 3 * bd, BLOCK), f32)),
        in_specs=[spec(SM)] * 4 + [spec(VM)] * (6 + len(all_chi)),
        out_specs=(spec(VM),) * 2,
        scratch_shapes=[VM((n, bd, BLOCK), f32), VM((nb + 8, BLOCK), f32),
                        VM((nb + 1, BLOCK, BLOCK), f32), VM((nb + 1, 8, BLOCK), f32),
                        VM((nb + 1, 8, BLOCK), f32),
                        VM((entries + 8 if stored else 1, BLOCK, BLOCK), f32),
                        VM((8, BLOCK, BLOCK), f32), VM((8, BLOCK, BLOCK), f32),
                        SM((3, n * (slots - bd) + 2), jnp.int32)],
        compiler_params=pltpu.CompilerParams(vmem_limit_bytes=(42 if stored else 58) << 20),
        name="solve",
    )(me[None], lists, counts, hardness, *all_chi, whole, rows, mids, left, push, nbr)
    forces = reduce_parts(part, n)
    return charges.reshape(atoms), forces.reshape(3, atoms)


def solution(mesh):
    both = ("cell", "blk")
    placed = (P(None, both), P(both), P(None, both), P(None, both)) + (P(),) * 7
    return jax.shard_map(
        on_device,
        mesh=mesh,
        in_specs=placed,
        out_specs=(P(both), P(None, both)),
        check_vma=False,
    )
```

```python
import functools
import math

import jax
import jax.numpy as jnp
import numpy as np
from jax import lax
from jax.experimental import pallas as pl
from jax.experimental.pallas import tpu as pltpu
from jax.sharding import PartitionSpec as P

ELEM = 4
RAD = 16
DESC = ELEM * RAD
BLOCK = 128
NBR = 32
ITERS = 3
PACK = 24
STORE_LIMIT = 36 << 20

coulomb_scale = 0.5
sigma_sq = 4.0
cutoff_sq = 49.0
highest = lax.Precision.HIGHEST
RATES = [0.005 * 200.0 ** (k / (RAD - 1)) for k in range(RAD)]
VM = pltpu.VMEM
SM = pltpu.SMEM
SCALE = math.log2(math.e) / (2.0 * sigma_sq)


def spec(space):
    return pl.BlockSpec(memory_space=space)


def piece_of(q, me, pow2):
    return q ^ me if pow2 else q


def dot(a, b, lhs=1):
    return lax.dot_general(a, b, (((lhs,), (0,)), ((), ())), precision=highest,
                           preferred_element_type=jnp.float32)


def column(row):
    return jnp.broadcast_to(row, (BLOCK, BLOCK)).T


def pick(kind, mats):
    out = jnp.where(kind == 0, mats[0], 0.0)
    for e in range(1, ELEM):
        out = jnp.where(kind == e, mats[e], out)
    return out


def one_hot(kind):
    ids = lax.broadcasted_iota(jnp.int32, (ELEM, kind.shape[1]), 0)
    return jnp.where(ids == kind, 1.0, 0.0)


def pack_kernel(count, *refs):
    sources = refs[:count]
    own_ref = refs[count]
    held = refs[count + 1:2 * count + 1]
    sems = refs[-1]
    copies = [pltpu.make_async_copy(sources[k], held[k], sems.at[k]) for k in range(count)]
    for copy in copies:
        copy.start()
    own_ref[...] = jnp.zeros_like(own_ref)
    for copy in copies[:3]:
        copy.wait()
    pos_ref, kind_ref, pairs_ref = held[:3]
    bd = pos_ref.shape[1] // BLOCK
    for a in range(bd):
        lanes = slice(a * BLOCK, (a + 1) * BLOCK)
        for d in range(3):
            own_ref[d * bd + a:d * bd + a + 1, :] = pos_ref[d:d + 1, lanes]
        own_ref[3 * bd + a:3 * bd + a + 1, :] = kind_ref[:, lanes].astype(jnp.float32)
    slots = pairs_ref.shape[1]
    for side in range(2):
        own_ref[4 * bd + side:4 * bd + side + 1, :slots] = (
            pairs_ref[side:side + 1, :].astype(jnp.float32))
    for copy in copies[3:]:
        copy.wait()


def join_pieces(pieces, out_ref):
    first = 0
    for piece in pieces:
        count = piece.shape[0]
        out_ref[first:first + count] = piece[...]
        first += count


def chi_kernel(pow2, nd, bd, parts, me_ref, *refs):
    pieces = refs[:parts]
    (pos_ref, nbr_ref, kind_ref, v1, b1, v2, b2, wo, bo,
     chi_ref, d_ref, h_ref, g_ref, w1, w2, f_ref) = refs[parts:]
    me = me_ref[0]
    chunk = min(nd, 8)
    join_pieces(pieces, g_ref)
    for turned, kept in ((v1, w1), (v2, w2)):
        for h in range(turned.shape[0]):
            for e in range(ELEM):
                kept[e, h:h + 1, :] = turned[h, e:e + 1, :]
    for a in range(bd):
        lanes = slice(a * BLOCK, (a + 1) * BLOCK)

        def group(g, carry):
            rows8 = pl.ds(pl.multiple_of(g * 8, 8), 8)
            idx = nbr_ref[rows8, lanes]
            hi = idx >> 7
            lo = idx & 127

            def look(part, vals):
                for step in range(chunk):
                    q = part * chunk + step
                    at = piece_of(q, me, pow2)
                    for r in range(bd):
                        hit = hi == q * bd + r
                        new = []
                        for d in range(4):
                            row = jnp.broadcast_to(g_ref[at, d * bd + r:d * bd + r + 1, :],
                                                   (8, BLOCK))
                            new.append(jnp.where(hit, jnp.take_along_axis(row, lo, axis=1),
                                                 vals[d]))
                        vals = tuple(new)
                return vals

            vals = (jnp.zeros((8, BLOCK), jnp.float32),) * 4
            if nd == chunk:
                vals = look(0, vals)
            else:
                vals = lax.fori_loop(0, nd // chunk, look, vals)
            live = idx >= 0
            for d in range(3):
                d_ref[d, rows8, lanes] = jnp.where(live, pos_ref[d:d + 1, lanes] - vals[d], 0.0)
            d_ref[3, rows8, lanes] = jnp.where(live, vals[3], -1.0)
            return carry

        lax.fori_loop(0, NBR // 8, group, 0, unroll=4 if nd == chunk else 1)
        offs = [d_ref[d, :, lanes] for d in range(3)]
        nk = d_ref[3, :, lanes]
        r2 = offs[0] * offs[0] + offs[1] * offs[1] + offs[2] * offs[2]
        u = 1.0 - r2 * (1.0 / cutoff_sq)
        shell = u * u * (ELEM / NBR)
        for k in range(RAD):
            val = shell * jnp.exp(-RATES[k] * r2)
            for e in range(ELEM):
                f_ref[e * RAD + k:e * RAD + k + 1, lanes] = jnp.sum(
                    jnp.where(nk == e, val, 0.0), axis=0, keepdims=True)
    kind = kind_ref[...]
    hot = one_hot(kind)
    feats = f_ref[...]
    h1 = jnp.tanh(pick(kind, [dot(w1[e], feats) for e in range(ELEM)]) + dot(b1[...], hot, 0))
    h2 = jnp.tanh(pick(kind, [dot(w2[e], h1) for e in range(ELEM)]) + dot(b2[...], hot, 0))
    h_ref[0] = h1
    h_ref[1] = h2
    chi = jnp.sum(dot(wo[...], hot, 0) * h2, axis=0, keepdims=True) + dot(bo[...], hot)
    for a in range(bd):
        chi_ref[a:a + 1, :] = chi[:, a * BLOCK:(a + 1) * BLOCK]


def fold(vals):
    tiles = vals.reshape(BLOCK // 8, 8, BLOCK)
    terms = [tiles[k] for k in range(BLOCK // 8)]
    while len(terms) > 1:
        terms = [terms[k] + terms[k + 1] for k in range(0, len(terms), 2)]
    return terms[0]


def split3(vals):
    parts = []
    for _ in range(3):
        top = vals.astype(jnp.bfloat16).astype(jnp.float32)
        parts.append(top)
        vals = vals - top
    return parts


def tile_kernel(pow2, nd, bd, nb, me_ref, g_ref, r_ref, mid_ref, a_ref):
    me = me_ref[0]
    sub8 = lax.broadcasted_iota(jnp.int32, (8, BLOCK), 0)
    r_ref[...] = jnp.zeros_like(r_ref)
    for q in range(nd):
        at = piece_of(q, me, pow2)
        for r in range(bd):
            for d in range(3):
                r_ref[q * bd + r, d:d + 1, :] = g_ref[at, d * bd + r:d * bd + r + 1, :]

    def set_block(b, carry):
        mid = jnp.broadcast_to(r_ref[b][:, 0:1], (8, BLOCK))
        mid_ref[b] = mid
        rel = r_ref[b] - mid
        size = jnp.sum(rel * rel, axis=0, keepdims=True)
        tile = jnp.where(sub8 == 3, 1.0,
                         jnp.where(sub8 == 4, size * -SCALE - 1.0, rel * (2.0 * SCALE)))
        q1, q2, q3 = split3(tile)
        a_ref[b] = jnp.concatenate([q1, q1, q2, q1, q3, q2], axis=0).T.astype(jnp.bfloat16)
        return carry

    lax.fori_loop(0, nb + 1, set_block, 0, unroll=11 if nb + 1 == 33 else 1)


def pull_kernel(bd, kind_ref, d_ref, h_ref, w1, w2, wo, push_ref, f_ref):
    kind = kind_ref[...]
    h1 = h_ref[0]
    h2 = h_ref[1]
    pre2 = dot(wo[...], one_hot(kind), 0) * (1.0 - h2 * h2)
    pre1 = sum(dot(w2[e], jnp.where(kind == e, pre2, 0.0), 0) for e in range(ELEM))
    pre1 = pre1 * (1.0 - h1 * h1)
    f_ref[...] = sum(dot(w1[e], jnp.where(kind == e, pre1, 0.0), 0)
                     for e in range(ELEM)) * (ELEM / NBR)
    for a in range(bd):
        lanes = slice(a * BLOCK, (a + 1) * BLOCK)
        offs = [d_ref[d, :, lanes] for d in range(3)]
        nk = d_ref[3, :, lanes]
        r2 = offs[0] * offs[0] + offs[1] * offs[1] + offs[2] * offs[2]
        u = 1.0 - r2 * (1.0 / cutoff_sq)
        s1 = jnp.zeros_like(r2)
        s2 = jnp.zeros_like(r2)
        for k in range(RAD):
            sel = jnp.zeros_like(r2)
            for e in range(ELEM):
                sel = jnp.where(nk == e, f_ref[e * RAD + k:e * RAD + k + 1, lanes], sel)
            term = sel * jnp.exp(-RATES[k] * r2)
            s1 = s1 + term
            s2 = s2 + RATES[k] * term
        grad = -u * ((2.0 / cutoff_sq) * s1 + u * s2)
        for d in range(3):
            push_ref[d, :, lanes] = 2.0 * grad * offs[d]


def solve_kernel(pow2, nd, bd, nb, slots, stored, parts, me_ref, pair_ref, count_ref, hard_ref,
                 *refs):
    pieces = refs[:parts]
    (g_ref, r_ref, mid_ref, a_ref, push_ref, nbr_ref, charge_ref, part_ref, x_ref, p_ref, pc_ref,
     y_ref, s_ref, t_ref, e_ref, group_ref) = refs[parts:]
    me = me_ref[0]
    cross = slots - bd
    sub = lax.broadcasted_iota(jnp.int32, (BLOCK, BLOCK), 0)
    ident = sub == lax.broadcasted_iota(jnp.int32, (BLOCK, BLOCK), 1)
    sub8 = lax.broadcasted_iota(jnp.int32, (8, BLOCK), 0)

    join_pieces(pieces, x_ref)
    p_ref[...] = jnp.zeros_like(p_ref)
    hards = []
    for q in range(nd):
        at = piece_of(q, me, pow2)
        span = slice(q * bd, (q + 1) * bd)
        p_ref[span, :] = -x_ref[at]
        hards.append(pick(g_ref[at, 3 * bd:4 * bd, :], [hard_ref[e] for e in range(ELEM)]))
    hard = jnp.concatenate(hards, axis=0)

    def set_charge(b, carry):
        pc_ref[b] = column(p_ref[pl.ds(b, 1), :])
        return carry

    def set_charges():
        if nb > 64:
            lax.fori_loop(0, nb, set_charge, 0)
            return
        turned = jnp.concatenate(split3(p_ref[0:nb]), axis=0).T.astype(jnp.bfloat16)
        ids = lax.broadcasted_iota(jnp.int32, (3 * nb, BLOCK), 0) % nb
        for b in range(0, nb, 2):
            chosen = [jnp.where(ids == b + m, 1.0, 0.0).astype(jnp.bfloat16) for m in range(2)]
            cols = jnp.dot(turned, jnp.concatenate(chosen, axis=1),
                           preferred_element_type=jnp.float32)
            for m in range(2):
                pc_ref[b + m] = cols[:, m * BLOCK:(m + 1) * BLOCK]

    pc_ref[nb] = jnp.zeros((BLOCK, BLOCK), jnp.float32)
    set_charges()

    def slot_of(q):
        return q ^ me if nd == 8 else q

    def power(j, i):
        rel = r_ref[i] - mid_ref[j]
        size = jnp.sum(rel * rel, axis=0, keepdims=True)
        tile = jnp.where(sub8 == 3, size * -SCALE, jnp.where(sub8 == 4, 1.0, rel))
        p1, p2, p3 = split3(tile)
        right = jnp.concatenate([p1, p2, p1, p3, p1, p2], axis=0).astype(jnp.bfloat16)
        return jnp.dot(a_ref[j], right, preferred_element_type=jnp.float32)

    def gamma(j, i):
        return jnp.exp2(power(j, i))

    def own_gamma(b):
        return jnp.where(ident, 0.0, gamma(b, b))

    def entry(t, j, i):
        return t_ref[t] if stored else gamma(j, i)

    def own_entry(b):
        return t_ref[b] if stored else own_gamma(b)

    size = 4 if cross % 4 == 0 else 1

    def list_piece(q, groups):
        def list_group(k, g):
            group_ref[0, g] = q
            group_ref[1, g] = bd + size * k
            group_ref[2, g] = nb + 2 * (q * cross + size * k)
            return g + 1

        return lax.fori_loop(0, (count_ref[q] - bd + size - 1) // size, list_group, groups)

    groups = lax.fori_loop(0, nd, list_piece, 0)
    for extra in range(2):
        group_ref[0, groups + extra] = nd
        group_ref[1, groups + extra] = bd
        group_ref[2, groups + extra] = nb + 2 * nd * cross

    def ends_of(g):
        q, e, t = group_ref[0, g], group_ref[1, g], group_ref[2, g]
        ends = []
        for m in range(size):
            left, right = pair_ref[q, 0, e + m], pair_ref[q, 1, e + m]
            ends += [(t + 2 * m, left, right), (t + 2 * m + 1, right, left)]
        return ends

    def first_diag(b, carry):
        val = own_gamma(b)
        if stored:
            t_ref[b] = val
        s_ref[b] = fold(val)
        y_ref[b] = fold(val * pc_ref[b])
        return carry

    lax.fori_loop(0, nb, first_diag, 0, unroll=8)

    def raise_powers(g, half):
        for m, (_, j, i) in enumerate(ends_of(g)):
            e_ref[half, m] = power(j, i)

    def first_step(g, carry):
        half = g & 1
        found = []
        for m, (t, j, i) in enumerate(ends_of(g)):
            val = jnp.exp2(e_ref[half, m])
            if stored:
                t_ref[t] = val
            found.append((i, fold(val), fold(val * pc_ref[j])))
        raise_powers(g + 1, 1 - half)
        for i, one, two in found:
            s_ref[i] = s_ref[i] + one
            y_ref[i] = y_ref[i] + two
        return carry

    raise_powers(0, 0)
    lax.fori_loop(0, groups, first_step, 0)

    def gathered(ref):
        return jnp.sum(ref[0:nb], axis=1)

    diag = hard + gathered(s_ref)

    def next_step(g, carry):
        found = [(i, fold(entry(t, j, i) * pc_ref[j])) for t, j, i in ends_of(g)]
        for i, one in found:
            y_ref[i] = y_ref[i] + one
        return carry

    def next_diag(b, carry):
        y_ref[b] = fold(own_entry(b) * pc_ref[b])
        return carry

    def matvec():
        set_charges()
        lax.fori_loop(0, nb, next_diag, 0, unroll=8)
        lax.fori_loop(0, groups, next_step, 0)

    def total(vals):
        return jnp.sum(jnp.sum(vals, axis=0, keepdims=True), axis=1, keepdims=True)

    res = p_ref[0:nb]
    p = res
    x = jnp.zeros_like(res)
    rho = total(res * res)
    for it in range(ITERS):
        if it:
            matvec()
        image = diag * p + gathered(y_ref)
        step = rho / total(p * image)
        x = x + step * p
        if it + 1 < ITERS:
            res = res - step * image
            rho2 = total(res * res)
            p = res + (rho2 / rho) * p
            rho = rho2
            p_ref[0:nb] = p
    p_ref[0:nb] = x
    for a in range(bd):
        charge_ref[a:a + 1, :] = p_ref[pl.ds(me * bd + a, 1), :]
        set_charge(me * bd + a, 0)
    mine = jnp.concatenate([charge_ref[a:a + 1, :] for a in range(bd)], axis=1)
    width = bd * BLOCK

    several = 4

    bf16 = jnp.bfloat16
    zero16 = jnp.zeros((16, width), bf16)
    one16 = jnp.ones((16, width), bf16)
    lines = lax.broadcasted_iota(jnp.int32, (16, width), 0).astype(jnp.float32)
    wanted = [(lines + 16.0 * k).astype(bf16) for k in range(max(BLOCK, nb) // 16)]

    def spread(row):
        return jnp.broadcast_to(row, (16, width)).astype(bf16)

    def scatter(k, acc):
        lefts = []
        rights = []
        for m in range(several):
            s = k * several + m
            idx = nbr_ref[pl.ds(s, 1), :]
            block = spread((idx >> 7).astype(jnp.float32))
            lane = spread((idx & 127).astype(jnp.float32))
            rights.append(jnp.concatenate(
                [jnp.where(wanted[r] == lane, one16, zero16) for r in range(BLOCK // 16)], axis=0))
            hits = [wanted[r] == block for r in range(nb // 16)]
            upper = []
            lower = []
            for d in range(3):
                val = push_ref[d, pl.ds(s, 1), :] * mine
                top = val.astype(bf16).astype(jnp.float32)
                top16 = spread(top)
                low16 = spread(val - top)
                upper += [jnp.where(hit, top16, zero16) for hit in hits]
                lower += [jnp.where(hit, low16, zero16) for hit in hits]
            lefts.append(jnp.concatenate(upper + lower, axis=0))
        return acc + lax.dot_general(jnp.concatenate(rights, axis=1),
                                     jnp.concatenate(lefts, axis=1), (((1,), (1,)), ((), ())),
                                     preferred_element_type=jnp.float32)

    acc = lax.fori_loop(0, NBR // several, scatter, jnp.zeros((BLOCK, 6 * nb), jnp.float32))
    acc = acc.T
    acc = acc[:3 * nb] + acc[3 * nb:]
    for q in range(nd):
        for d in range(3):
            part_ref[slot_of(q), d * bd:(d + 1) * bd, :] = acc[d * nb + q * bd:d * nb + (q + 1) * bd]

    def moments(rel, weights, side):
        tile = jnp.where(sub8 == 3, 1.0, rel)
        rows = jnp.concatenate(split3(tile) + [jnp.zeros_like(rel)], axis=0).astype(jnp.bfloat16)
        out = sum(lax.dot_general(rows, w, (((1,), (side,)), ((), ())),
                                  preferred_element_type=jnp.float32) for w in weights)
        return out[0:8] + out[8:16] + out[16:24]

    def force_of(rel, found):
        return (rel * found[3:4] - found) * (0.5 / sigma_sq)

    def weigh(val, j, i):
        both = pc_ref[j] + p_ref[pl.ds(i, 1), :]
        weight = val * (both * both)
        top = weight.astype(jnp.bfloat16)
        return top, (weight - top.astype(jnp.float32)).astype(jnp.bfloat16)

    s_ref[...] = jnp.zeros_like(s_ref)
    for a in range(bd):
        b = me * bd + a
        rel = r_ref[b] - mid_ref[b]
        force = force_of(rel, moments(rel, weigh(own_entry(b), b, b), 0))
        lanes = slice(a * BLOCK, (a + 1) * BLOCK)
        for d in range(3):
            away = jnp.sum(push_ref[d, :, lanes], axis=0, keepdims=True) * charge_ref[a:a + 1, :]
            force = jnp.where(sub8 == d, force - away, force)
        s_ref[b] = force
    piece = piece_of(me, me, pow2)
    together = 4 if cross % 4 == 0 else 1

    def pair_force(k, carry):
        found = []
        for m in range(together):
            e = k * together + m
            j, i = pair_ref[piece, 0, bd + e], pair_ref[piece, 1, bd + e]
            mid = mid_ref[j]
            rel_j = r_ref[j] - mid
            rel_i = r_ref[i] - mid
            weights = weigh(entry(nb + 2 * (piece * cross + e), j, i), j, i)
            found.append((i, force_of(rel_i, moments(rel_j, weights, 0))))
            found.append((j, force_of(rel_j, moments(rel_i, weights, 1))))
        for b, force in found:
            s_ref[b] = s_ref[b] + force
        return carry

    lax.fori_loop(0, (count_ref[piece] - bd + together - 1) // together, pair_force, 0)
    for q in range(nd):
        for d in range(3):
            for r in range(bd):
                at = slice(d * bd + r, d * bd + r + 1)
                part_ref[slot_of(q), at, :] = part_ref[slot_of(q), at, :] + s_ref[q * bd + r, d:d + 1, :]


def swap(vals, step, n):
    return lax.ppermute(vals, "blk", [(i, i ^ step) for i in range(n)])


def gather_far_first(own, n):
    if n & (n - 1):
        return [lax.all_gather(own, "blk")]
    got = own[None]
    step = n // 2
    while step:
        both = jnp.stack([got, swap(got, step, n)], axis=1)
        got = both.reshape((2 * got.shape[0],) + own.shape)
        step //= 2
    return [got]


def gather_near_first(own, n, beside):
    if n & (n - 1):
        return [lax.all_gather(own, "blk")], beside
    got = own[None]
    step = 1
    while step < n:
        got = jnp.concatenate([got, swap(got, step, n)], axis=0)
        if step == n // 4:
            got, beside = lax.optimization_barrier((got, beside))
        step *= 2
    return [got], beside


def reduce_parts(part, n):
    if n != 8:
        return jnp.sum(lax.all_to_all(part, "blk", 0, 0), axis=0)
    mine = part[0::2] + swap(part[1::2], 1, n)
    far = [swap(mine[k], 2 * k, n) for k in (1, 2, 3)]
    return mine[0] + far[0] + far[1] + far[2]


def on_device(positions, species, neighbors, pair_lists, hardness, w_first, b_first, w_second,
              b_second, w_out, b_out):
    n = lax.axis_size("blk")
    me = lax.axis_index("blk")
    atoms = positions.shape[1]
    bd = atoms // BLOCK
    nb = bd * n
    slots = pair_lists.shape[1]
    hid = w_first.shape[1]
    f32 = jnp.float32
    kind = species.reshape(1, atoms)
    small = pltpu.CompilerParams(vmem_limit_bytes=24 << 20)
    raw = (positions, kind, pair_lists, neighbors, w_first.transpose(1, 0, 2), b_first,
           w_second.transpose(1, 0, 2), b_second, w_out, b_out.reshape(1, ELEM))
    raw = tuple(pltpu.with_memory_space_constraint(r, pltpu.HBM) for r in raw)
    own, pos, kinds, _, nbr, v1, b1, v2, b2, wo, bo = pl.pallas_call(
        functools.partial(pack_kernel, len(raw)),
        out_shape=(jax.ShapeDtypeStruct((PACK, BLOCK), f32),)
        + tuple(jax.ShapeDtypeStruct(r.shape, r.dtype) for r in raw),
        in_specs=[spec(pltpu.HBM)] * len(raw), out_specs=(spec(VM),) * (1 + len(raw)),
        scratch_shapes=[pltpu.SemaphoreType.DMA((len(raw),))],
        compiler_params=small, name="pack",
    )(*raw)
    pow2 = n & (n - 1) == 0
    places = gather_far_first(own, n)
    chi, offs, hidden, whole, w1, w2 = pl.pallas_call(
        functools.partial(chi_kernel, pow2, n, bd, len(places)),
        out_shape=(jax.ShapeDtypeStruct((bd, BLOCK), f32),
                   jax.ShapeDtypeStruct((4, NBR, atoms), f32),
                   jax.ShapeDtypeStruct((2, hid, atoms), f32),
                   jax.ShapeDtypeStruct((n, PACK, BLOCK), f32),
                   jax.ShapeDtypeStruct(w_first.shape, f32),
                   jax.ShapeDtypeStruct(w_second.shape, f32)),
        in_specs=[spec(SM)] + [spec(VM)] * (9 + len(places)),
        out_specs=(spec(VM),) * 6,
        scratch_shapes=[VM((DESC, atoms), f32)],
        compiler_params=small,
        name="chi",
    )(me[None], *places, pos, nbr, kinds, v1, b1, v2, b2, wo, bo)
    tiles = pl.pallas_call(
        functools.partial(tile_kernel, pow2, n, bd, nb),
        out_shape=(jax.ShapeDtypeStruct((nb + 1, 8, BLOCK), f32),
                   jax.ShapeDtypeStruct((nb + 1, 8, BLOCK), f32),
                   jax.ShapeDtypeStruct((nb + 1, BLOCK, 48), jnp.bfloat16)),
        in_specs=[spec(SM), spec(VM)],
        out_specs=(spec(VM),) * 3,
        compiler_params=small,
        name="tiles",
    )(me[None], whole)
    all_chi, (rows, mids, left) = gather_near_first(chi, n, tiles)
    push = pl.pallas_call(
        functools.partial(pull_kernel, bd),
        out_shape=jax.ShapeDtypeStruct((3, NBR, atoms), f32),
        in_specs=[spec(VM)] * 6,
        out_specs=spec(VM),
        scratch_shapes=[VM((DESC, atoms), f32)],
        compiler_params=small,
        name="pull",
    )(kinds, offs, hidden, w1, w2, wo)
    lists = whole[:, 4 * bd:4 * bd + 2, :slots].astype(jnp.int32)
    counts = jnp.sum((lists[:, 0] >= 0).astype(jnp.int32), axis=1)
    lists = jnp.where(lists < 0, nb, lists)
    lists = jnp.pad(lists, ((0, 1), (0, 0), (0, 0)), constant_values=nb)
    entries = nb + 2 * (n * slots - nb)
    stored = entries * BLOCK * BLOCK * 4 <= STORE_LIMIT
    charges, part = pl.pallas_call(
        functools.partial(solve_kernel, pow2, n, bd, nb, slots, stored, len(all_chi)),
        out_shape=(jax.ShapeDtypeStruct((bd, BLOCK), f32),
                   jax.ShapeDtypeStruct((n, 3 * bd, BLOCK), f32)),
        in_specs=[spec(SM)] * 4 + [spec(VM)] * (6 + len(all_chi)),
        out_specs=(spec(VM),) * 2,
        scratch_shapes=[VM((n, bd, BLOCK), f32), VM((nb + 8, BLOCK), f32),
                        VM((nb + 1, BLOCK, BLOCK), f32), VM((nb + 1, 8, BLOCK), f32),
                        VM((nb + 1, 8, BLOCK), f32),
                        VM((entries + 8 if stored else 1, BLOCK, BLOCK), f32),
                        VM((2, 8, BLOCK, BLOCK), f32),
                        SM((3, n * (slots - bd) + 2), jnp.int32)],
        compiler_params=pltpu.CompilerParams(vmem_limit_bytes=(42 if stored else 58) << 20),
        name="solve",
    )(me[None], lists, counts, hardness, *all_chi, whole, rows, mids, left, push, nbr)
    forces = reduce_parts(part, n)
    return charges.reshape(atoms), forces.reshape(3, atoms)


def solution(mesh):
    both = ("cell", "blk")
    placed = (P(None, both), P(both), P(None, both), P(None, both)) + (P(),) * 7
    return jax.shard_map(
        on_device,
        mesh=mesh,
        in_specs=placed,
        out_specs=(P(both), P(None, both)),
        check_vma=False,
    )
```

```python
import functools
import math

import jax
import jax.numpy as jnp
import numpy as np
from jax import lax
from jax.experimental import pallas as pl
from jax.experimental.pallas import tpu as pltpu
from jax.sharding import PartitionSpec as P

ELEM = 4
RAD = 16
DESC = ELEM * RAD
BLOCK = 128
NBR = 32
ITERS = 3
PACK = 24
STORE_LIMIT = 36 << 20

coulomb_scale = 0.5
sigma_sq = 4.0
cutoff_sq = 49.0
highest = lax.Precision.HIGHEST
RATES = [0.005 * 200.0 ** (k / (RAD - 1)) for k in range(RAD)]
VM = pltpu.VMEM
SM = pltpu.SMEM
SCALE = math.log2(math.e) / (2.0 * sigma_sq)


def spec(space):
    return pl.BlockSpec(memory_space=space)


def piece_of(q, me, pow2):
    return q ^ me if pow2 else q


def dot(a, b, lhs=1):
    return lax.dot_general(a, b, (((lhs,), (0,)), ((), ())), precision=highest,
                           preferred_element_type=jnp.float32)


def column(row):
    return jnp.broadcast_to(row, (BLOCK, BLOCK)).T


def pick(kind, mats):
    out = jnp.where(kind == 0, mats[0], 0.0)
    for e in range(1, ELEM):
        out = jnp.where(kind == e, mats[e], out)
    return out


def one_hot(kind):
    ids = lax.broadcasted_iota(jnp.int32, (ELEM, kind.shape[1]), 0)
    return jnp.where(ids == kind, 1.0, 0.0)


def pack_kernel(count, *refs):
    sources = refs[:count]
    own_ref = refs[count]
    held = refs[count + 1:2 * count + 1]
    sems = refs[-1]
    copies = [pltpu.make_async_copy(sources[k], held[k], sems.at[k]) for k in range(count)]
    for copy in copies:
        copy.start()
    own_ref[...] = jnp.zeros_like(own_ref)
    for copy in copies[:3]:
        copy.wait()
    pos_ref, kind_ref, pairs_ref = held[:3]
    bd = pos_ref.shape[1] // BLOCK
    for a in range(bd):
        lanes = slice(a * BLOCK, (a + 1) * BLOCK)
        for d in range(3):
            own_ref[d * bd + a:d * bd + a + 1, :] = pos_ref[d:d + 1, lanes]
        own_ref[3 * bd + a:3 * bd + a + 1, :] = kind_ref[:, lanes].astype(jnp.float32)
    slots = pairs_ref.shape[1]
    for side in range(2):
        own_ref[4 * bd + side:4 * bd + side + 1, :slots] = (
            pairs_ref[side:side + 1, :].astype(jnp.float32))
    for copy in copies[3:]:
        copy.wait()


def join_pieces(pieces, out_ref):
    first = 0
    for piece in pieces:
        count = piece.shape[0]
        out_ref[first:first + count] = piece[...]
        first += count


def chi_kernel(pow2, nd, bd, parts, me_ref, *refs):
    pieces = refs[:parts]
    (pos_ref, nbr_ref, kind_ref, v1, b1, v2, b2, wo, bo,
     chi_ref, d_ref, h_ref, g_ref, w1, w2, f_ref) = refs[parts:]
    me = me_ref[0]
    chunk = min(nd, 8)
    join_pieces(pieces, g_ref)
    for turned, kept in ((v1, w1), (v2, w2)):
        for h in range(turned.shape[0]):
            for e in range(ELEM):
                kept[e, h:h + 1, :] = turned[h, e:e + 1, :]
    for a in range(bd):
        lanes = slice(a * BLOCK, (a + 1) * BLOCK)

        def group(g, carry):
            rows8 = pl.ds(pl.multiple_of(g * 8, 8), 8)
            idx = nbr_ref[rows8, lanes]
            hi = idx >> 7
            lo = idx & 127

            def look(part, vals):
                for step in range(chunk):
                    q = part * chunk + step
                    at = piece_of(q, me, pow2)
                    for r in range(bd):
                        hit = hi == q * bd + r
                        new = []
                        for d in range(4):
                            row = jnp.broadcast_to(g_ref[at, d * bd + r:d * bd + r + 1, :],
                                                   (8, BLOCK))
                            new.append(jnp.where(hit, jnp.take_along_axis(row, lo, axis=1),
                                                 vals[d]))
                        vals = tuple(new)
                return vals

            vals = (jnp.zeros((8, BLOCK), jnp.float32),) * 4
            if nd == chunk:
                vals = look(0, vals)
            else:
                vals = lax.fori_loop(0, nd // chunk, look, vals)
            live = idx >= 0
            for d in range(3):
                d_ref[d, rows8, lanes] = jnp.where(live, pos_ref[d:d + 1, lanes] - vals[d], 0.0)
            d_ref[3, rows8, lanes] = jnp.where(live, vals[3], -1.0)
            return carry

        lax.fori_loop(0, NBR // 8, group, 0, unroll=4 if nd == chunk else 1)
        offs = [d_ref[d, :, lanes] for d in range(3)]
        nk = d_ref[3, :, lanes]
        r2 = offs[0] * offs[0] + offs[1] * offs[1] + offs[2] * offs[2]
        u = 1.0 - r2 * (1.0 / cutoff_sq)
        shell = u * u * (ELEM / NBR)
        for k in range(RAD):
            val = shell * jnp.exp(-RATES[k] * r2)
            for e in range(ELEM):
                f_ref[e * RAD + k:e * RAD + k + 1, lanes] = jnp.sum(
                    jnp.where(nk == e, val, 0.0), axis=0, keepdims=True)
    kind = kind_ref[...]
    hot = one_hot(kind)
    feats = f_ref[...]
    h1 = jnp.tanh(pick(kind, [dot(w1[e], feats) for e in range(ELEM)]) + dot(b1[...], hot, 0))
    h2 = jnp.tanh(pick(kind, [dot(w2[e], h1) for e in range(ELEM)]) + dot(b2[...], hot, 0))
    h_ref[0] = h1
    h_ref[1] = h2
    chi = jnp.sum(dot(wo[...], hot, 0) * h2, axis=0, keepdims=True) + dot(bo[...], hot)
    for a in range(bd):
        chi_ref[a:a + 1, :] = chi[:, a * BLOCK:(a + 1) * BLOCK]


def fold(vals):
    tiles = vals.reshape(BLOCK // 8, 8, BLOCK)
    terms = [tiles[k] for k in range(BLOCK // 8)]
    while len(terms) > 1:
        terms = [terms[k] + terms[k + 1] for k in range(0, len(terms), 2)]
    return terms[0]


def split3(vals):
    parts = []
    for _ in range(3):
        top = vals.astype(jnp.bfloat16).astype(jnp.float32)
        parts.append(top)
        vals = vals - top
    return parts


def tile_kernel(pow2, nd, bd, nb, me_ref, g_ref, r_ref, mid_ref, a_ref):
    me = me_ref[0]
    sub8 = lax.broadcasted_iota(jnp.int32, (8, BLOCK), 0)
    r_ref[...] = jnp.zeros_like(r_ref)
    for q in range(nd):
        at = piece_of(q, me, pow2)
        for r in range(bd):
            for d in range(3):
                r_ref[q * bd + r, d:d + 1, :] = g_ref[at, d * bd + r:d * bd + r + 1, :]

    def set_block(b, carry):
        mid = jnp.broadcast_to(r_ref[b][:, 0:1], (8, BLOCK))
        mid_ref[b] = mid
        rel = r_ref[b] - mid
        size = jnp.sum(rel * rel, axis=0, keepdims=True)
        tile = jnp.where(sub8 == 3, 1.0,
                         jnp.where(sub8 == 4, size * -SCALE - 1.0, rel * (2.0 * SCALE)))
        q1, q2, q3 = split3(tile)
        a_ref[b] = jnp.concatenate([q1, q1, q2, q1, q3, q2], axis=0).T.astype(jnp.bfloat16)
        return carry

    lax.fori_loop(0, nb + 1, set_block, 0, unroll=11 if nb + 1 == 33 else 1)


def pull_kernel(bd, kind_ref, d_ref, h_ref, w1, w2, wo, push_ref, f_ref):
    kind = kind_ref[...]
    h1 = h_ref[0]
    h2 = h_ref[1]
    pre2 = dot(wo[...], one_hot(kind), 0) * (1.0 - h2 * h2)
    pre1 = sum(dot(w2[e], jnp.where(kind == e, pre2, 0.0), 0) for e in range(ELEM))
    pre1 = pre1 * (1.0 - h1 * h1)
    f_ref[...] = sum(dot(w1[e], jnp.where(kind == e, pre1, 0.0), 0)
                     for e in range(ELEM)) * (ELEM / NBR)
    for a in range(bd):
        lanes = slice(a * BLOCK, (a + 1) * BLOCK)
        offs = [d_ref[d, :, lanes] for d in range(3)]
        nk = d_ref[3, :, lanes]
        r2 = offs[0] * offs[0] + offs[1] * offs[1] + offs[2] * offs[2]
        u = 1.0 - r2 * (1.0 / cutoff_sq)
        s1 = jnp.zeros_like(r2)
        s2 = jnp.zeros_like(r2)
        for k in range(RAD):
            sel = jnp.zeros_like(r2)
            for e in range(ELEM):
                sel = jnp.where(nk == e, f_ref[e * RAD + k:e * RAD + k + 1, lanes], sel)
            term = sel * jnp.exp(-RATES[k] * r2)
            s1 = s1 + term
            s2 = s2 + RATES[k] * term
        grad = -u * ((2.0 / cutoff_sq) * s1 + u * s2)
        for d in range(3):
            push_ref[d, :, lanes] = 2.0 * grad * offs[d]


def solve_kernel(pow2, nd, bd, nb, slots, stored, parts, me_ref, pair_ref, count_ref, hard_ref,
                 *refs):
    pieces = refs[:parts]
    (g_ref, r_ref, mid_ref, a_ref, push_ref, nbr_ref, charge_ref, part_ref, x_ref, p_ref, pc_ref,
     y_ref, s_ref, t_ref, flat_ref) = refs[parts:]
    me = me_ref[0]
    cross = slots - bd
    sub = lax.broadcasted_iota(jnp.int32, (BLOCK, BLOCK), 0)
    ident = sub == lax.broadcasted_iota(jnp.int32, (BLOCK, BLOCK), 1)
    sub8 = lax.broadcasted_iota(jnp.int32, (8, BLOCK), 0)

    join_pieces(pieces, x_ref)
    p_ref[...] = jnp.zeros_like(p_ref)
    hards = []
    for q in range(nd):
        at = piece_of(q, me, pow2)
        span = slice(q * bd, (q + 1) * bd)
        p_ref[span, :] = -x_ref[at]
        hards.append(pick(g_ref[at, 3 * bd:4 * bd, :], [hard_ref[e] for e in range(ELEM)]))
    hard = jnp.concatenate(hards, axis=0)

    def set_charge(b, carry):
        pc_ref[b] = column(p_ref[pl.ds(b, 1), :])
        return carry

    def set_charges():
        if nb > 64:
            lax.fori_loop(0, nb, set_charge, 0)
            return
        turned = jnp.concatenate(split3(p_ref[0:nb]), axis=0).T.astype(jnp.bfloat16)
        ids = lax.broadcasted_iota(jnp.int32, (3 * nb, BLOCK), 0) % nb
        for b in range(0, nb, 2):
            chosen = [jnp.where(ids == b + m, 1.0, 0.0).astype(jnp.bfloat16) for m in range(2)]
            cols = jnp.dot(turned, jnp.concatenate(chosen, axis=1),
                           preferred_element_type=jnp.float32)
            for m in range(2):
                pc_ref[b + m] = cols[:, m * BLOCK:(m + 1) * BLOCK]

    pc_ref[nb] = jnp.zeros((BLOCK, BLOCK), jnp.float32)
    set_charges()

    def slot_of(q):
        return q ^ me if nd == 8 else q

    def power(j, i):
        rel = r_ref[i] - mid_ref[j]
        size = jnp.sum(rel * rel, axis=0, keepdims=True)
        tile = jnp.where(sub8 == 3, size * -SCALE, jnp.where(sub8 == 4, 1.0, rel))
        p1, p2, p3 = split3(tile)
        right = jnp.concatenate([p1, p2, p1, p3, p1, p2], axis=0).astype(jnp.bfloat16)
        return jnp.dot(a_ref[j], right, preferred_element_type=jnp.float32)

    def gamma(j, i):
        return jnp.exp2(power(j, i))

    def own_gamma(b):
        return jnp.where(ident, 0.0, gamma(b, b))

    def entry(t, j, i):
        return t_ref[t] if stored else gamma(j, i)

    def own_entry(b):
        return t_ref[b] if stored else own_gamma(b)

    size = 4 if cross % 4 == 0 else 1
    wide = 8
    piece = piece_of(me, me, pow2)

    def list_piece(q, carry):
        place, own_place = carry
        number = count_ref[q] - bd

        def list_group(k, inner):
            spots = [(side, m) for side in range(2) for m in range(size)]
            found = [pair_ref[q, side, bd + size * k + m] for side, m in spots]
            for (side, m), block in zip(spots, found):
                flat_ref[side, place + size * k + m] = block
            return inner

        lax.fori_loop(0, (number + size - 1) // size, list_group, 0)
        return place + number, jnp.where(q == piece, place, own_place)

    pairs, own_place = lax.fori_loop(0, nd, list_piece, (jnp.int32(0), jnp.int32(0)))
    for m in range(wide):
        for side in range(2):
            flat_ref[side, pairs + m] = nb

    def ends_of(g, width):
        ends = []
        for m in range(width):
            e = g * width + m
            left, right = flat_ref[0, e], flat_ref[1, e]
            ends += [(nb + 2 * e, left, right), (nb + 2 * e + 1, right, left)]
        return ends

    def first_diag(b, carry):
        val = own_gamma(b)
        if stored:
            t_ref[b] = val
        s_ref[b] = fold(val)
        y_ref[b] = fold(val * pc_ref[b])
        return carry

    lax.fori_loop(0, nb, first_diag, 0, unroll=16)

    def first_step(g, carry):
        found = []
        for t, j, i in ends_of(g, wide):
            val = gamma(j, i)
            if stored:
                t_ref[t] = val
            found.append((i, fold(val), fold(val * pc_ref[j])))
        for i, one, two in found:
            s_ref[i] = s_ref[i] + one
            y_ref[i] = y_ref[i] + two
        return carry

    lax.fori_loop(0, (pairs + wide - 1) // wide, first_step, 0)

    def gathered(ref):
        return jnp.sum(ref[0:nb], axis=1)

    diag = hard + gathered(s_ref)

    def next_step(g, carry):
        found = [(i, fold(entry(t, j, i) * pc_ref[j])) for t, j, i in ends_of(g, 4)]
        for i, one in found:
            y_ref[i] = y_ref[i] + one
        return carry

    def next_diag(b, carry):
        y_ref[b] = fold(own_entry(b) * pc_ref[b])
        return carry

    def matvec():
        set_charges()
        lax.fori_loop(0, nb, next_diag, 0, unroll=8)
        lax.fori_loop(0, (pairs + 3) // 4, next_step, 0)

    def total(vals):
        return jnp.sum(jnp.sum(vals, axis=0, keepdims=True), axis=1, keepdims=True)

    res = p_ref[0:nb]
    p = res
    x = jnp.zeros_like(res)
    rho = total(res * res)
    for it in range(ITERS):
        if it:
            matvec()
        image = diag * p + gathered(y_ref)
        step = rho / total(p * image)
        x = x + step * p
        if it + 1 < ITERS:
            res = res - step * image
            rho2 = total(res * res)
            p = res + (rho2 / rho) * p
            rho = rho2
            p_ref[0:nb] = p
    p_ref[0:nb] = x
    for a in range(bd):
        charge_ref[a:a + 1, :] = p_ref[pl.ds(me * bd + a, 1), :]
        set_charge(me * bd + a, 0)
    mine = jnp.concatenate([charge_ref[a:a + 1, :] for a in range(bd)], axis=1)
    width = bd * BLOCK

    several = 4

    bf16 = jnp.bfloat16
    zero16 = jnp.zeros((16, width), bf16)
    one16 = jnp.ones((16, width), bf16)
    lines = lax.broadcasted_iota(jnp.int32, (16, width), 0).astype(jnp.float32)
    wanted = [(lines + 16.0 * k).astype(bf16) for k in range(max(BLOCK, nb) // 16)]

    def spread(row):
        return jnp.broadcast_to(row, (16, width)).astype(bf16)

    def scatter(k, acc):
        lefts = []
        rights = []
        for m in range(several):
            s = k * several + m
            idx = nbr_ref[pl.ds(s, 1), :]
            block = spread((idx >> 7).astype(jnp.float32))
            lane = spread((idx & 127).astype(jnp.float32))
            rights.append(jnp.concatenate(
                [jnp.where(wanted[r] == lane, one16, zero16) for r in range(BLOCK // 16)], axis=0))
            hits = [wanted[r] == block for r in range(nb // 16)]
            upper = []
            lower = []
            for d in range(3):
                val = push_ref[d, pl.ds(s, 1), :] * mine
                top = val.astype(bf16).astype(jnp.float32)
                top16 = spread(top)
                low16 = spread(val - top)
                upper += [jnp.where(hit, top16, zero16) for hit in hits]
                lower += [jnp.where(hit, low16, zero16) for hit in hits]
            lefts.append(jnp.concatenate(upper + lower, axis=0))
        return acc + lax.dot_general(jnp.concatenate(rights, axis=1),
                                     jnp.concatenate(lefts, axis=1), (((1,), (1,)), ((), ())),
                                     preferred_element_type=jnp.float32)

    acc = lax.fori_loop(0, NBR // several, scatter, jnp.zeros((BLOCK, 6 * nb), jnp.float32))
    acc = acc.T
    acc = acc[:3 * nb] + acc[3 * nb:]
    for q in range(nd):
        for d in range(3):
            part_ref[slot_of(q), d * bd:(d + 1) * bd, :] = acc[d * nb + q * bd:d * nb + (q + 1) * bd]

    def moments(rel, weights, side):
        tile = jnp.where(sub8 == 3, 1.0, rel)
        rows = jnp.concatenate(split3(tile) + [jnp.zeros_like(rel)], axis=0).astype(jnp.bfloat16)
        out = sum(lax.dot_general(rows, w, (((1,), (side,)), ((), ())),
                                  preferred_element_type=jnp.float32) for w in weights)
        return out[0:8] + out[8:16] + out[16:24]

    def force_of(rel, found):
        return (rel * found[3:4] - found) * (0.5 / sigma_sq)

    def weigh(val, j, i):
        both = pc_ref[j] + p_ref[pl.ds(i, 1), :]
        weight = val * (both * both)
        top = weight.astype(jnp.bfloat16)
        return top, (weight - top.astype(jnp.float32)).astype(jnp.bfloat16)

    s_ref[...] = jnp.zeros_like(s_ref)
    for a in range(bd):
        b = me * bd + a
        rel = r_ref[b] - mid_ref[b]
        force = force_of(rel, moments(rel, weigh(own_entry(b), b, b), 0))
        lanes = slice(a * BLOCK, (a + 1) * BLOCK)
        for d in range(3):
            away = jnp.sum(push_ref[d, :, lanes], axis=0, keepdims=True) * charge_ref[a:a + 1, :]
            force = jnp.where(sub8 == d, force - away, force)
        s_ref[b] = force
    together = 4 if cross % 4 == 0 else 1

    def pair_force(k, carry):
        found = []
        for m in range(together):
            e = k * together + m
            j, i = pair_ref[piece, 0, bd + e], pair_ref[piece, 1, bd + e]
            mid = mid_ref[j]
            rel_j = r_ref[j] - mid
            rel_i = r_ref[i] - mid
            weights = weigh(entry(nb + 2 * (own_place + e), j, i), j, i)
            found.append((i, force_of(rel_i, moments(rel_j, weights, 0))))
            found.append((j, force_of(rel_j, moments(rel_i, weights, 1))))
        for b, force in found:
            s_ref[b] = s_ref[b] + force
        return carry

    lax.fori_loop(0, (count_ref[piece] - bd + together - 1) // together, pair_force, 0)
    for q in range(nd):
        for d in range(3):
            for r in range(bd):
                at = slice(d * bd + r, d * bd + r + 1)
                part_ref[slot_of(q), at, :] = part_ref[slot_of(q), at, :] + s_ref[q * bd + r, d:d + 1, :]


def swap(vals, step, n):
    return lax.ppermute(vals, "blk", [(i, i ^ step) for i in range(n)])


def gather_far_first(own, n):
    if n & (n - 1):
        return [lax.all_gather(own, "blk")]
    got = own[None]
    step = n // 2
    while step:
        both = jnp.stack([got, swap(got, step, n)], axis=1)
        got = both.reshape((2 * got.shape[0],) + own.shape)
        step //= 2
    return [got]


def gather_near_first(own, n, beside):
    if n & (n - 1):
        return [lax.all_gather(own, "blk")], beside
    got = own[None]
    step = 1
    while step < n:
        got = jnp.concatenate([got, swap(got, step, n)], axis=0)
        if step == n // 4:
            got, beside = lax.optimization_barrier((got, beside))
        step *= 2
    return [got], beside


def reduce_parts(part, n):
    if n != 8:
        return jnp.sum(lax.all_to_all(part, "blk", 0, 0), axis=0)
    mine = part[0::2] + swap(part[1::2], 1, n)
    far = [swap(mine[k], 2 * k, n) for k in (1, 2, 3)]
    return mine[0] + far[0] + far[1] + far[2]


def on_device(positions, species, neighbors, pair_lists, hardness, w_first, b_first, w_second,
              b_second, w_out, b_out):
    n = lax.axis_size("blk")
    me = lax.axis_index("blk")
    atoms = positions.shape[1]
    bd = atoms // BLOCK
    nb = bd * n
    slots = pair_lists.shape[1]
    hid = w_first.shape[1]
    f32 = jnp.float32
    kind = species.reshape(1, atoms)
    small = pltpu.CompilerParams(vmem_limit_bytes=24 << 20)
    raw = (positions, kind, pair_lists, neighbors, w_first.transpose(1, 0, 2), b_first,
           w_second.transpose(1, 0, 2), b_second, w_out, b_out.reshape(1, ELEM))
    raw = tuple(pltpu.with_memory_space_constraint(r, pltpu.HBM) for r in raw)
    own, pos, kinds, _, nbr, v1, b1, v2, b2, wo, bo = pl.pallas_call(
        functools.partial(pack_kernel, len(raw)),
        out_shape=(jax.ShapeDtypeStruct((PACK, BLOCK), f32),)
        + tuple(jax.ShapeDtypeStruct(r.shape, r.dtype) for r in raw),
        in_specs=[spec(pltpu.HBM)] * len(raw), out_specs=(spec(VM),) * (1 + len(raw)),
        scratch_shapes=[pltpu.SemaphoreType.DMA((len(raw),))],
        compiler_params=small, name="pack",
    )(*raw)
    pow2 = n & (n - 1) == 0
    places = gather_far_first(own, n)
    chi, offs, hidden, whole, w1, w2 = pl.pallas_call(
        functools.partial(chi_kernel, pow2, n, bd, len(places)),
        out_shape=(jax.ShapeDtypeStruct((bd, BLOCK), f32),
                   jax.ShapeDtypeStruct((4, NBR, atoms), f32),
                   jax.ShapeDtypeStruct((2, hid, atoms), f32),
                   jax.ShapeDtypeStruct((n, PACK, BLOCK), f32),
                   jax.ShapeDtypeStruct(w_first.shape, f32),
                   jax.ShapeDtypeStruct(w_second.shape, f32)),
        in_specs=[spec(SM)] + [spec(VM)] * (9 + len(places)),
        out_specs=(spec(VM),) * 6,
        scratch_shapes=[VM((DESC, atoms), f32)],
        compiler_params=small,
        name="chi",
    )(me[None], *places, pos, nbr, kinds, v1, b1, v2, b2, wo, bo)
    tiles = pl.pallas_call(
        functools.partial(tile_kernel, pow2, n, bd, nb),
        out_shape=(jax.ShapeDtypeStruct((nb + 1, 8, BLOCK), f32),
                   jax.ShapeDtypeStruct((nb + 1, 8, BLOCK), f32),
                   jax.ShapeDtypeStruct((nb + 1, BLOCK, 48), jnp.bfloat16)),
        in_specs=[spec(SM), spec(VM)],
        out_specs=(spec(VM),) * 3,
        compiler_params=small,
        name="tiles",
    )(me[None], whole)
    all_chi, (rows, mids, left) = gather_near_first(chi, n, tiles)
    push = pl.pallas_call(
        functools.partial(pull_kernel, bd),
        out_shape=jax.ShapeDtypeStruct((3, NBR, atoms), f32),
        in_specs=[spec(VM)] * 6,
        out_specs=spec(VM),
        scratch_shapes=[VM((DESC, atoms), f32)],
        compiler_params=small,
        name="pull",
    )(kinds, offs, hidden, w1, w2, wo)
    lists = whole[:, 4 * bd:4 * bd + 2, :slots].astype(jnp.int32)
    counts = jnp.sum((lists[:, 0] >= 0).astype(jnp.int32), axis=1)
    lists = jnp.where(lists < 0, nb, lists)
    lists = jnp.pad(lists, ((0, 1), (0, 0), (0, 0)), constant_values=nb)
    entries = nb + 2 * (n * slots - nb)
    stored = entries * BLOCK * BLOCK * 4 <= STORE_LIMIT
    charges, part = pl.pallas_call(
        functools.partial(solve_kernel, pow2, n, bd, nb, slots, stored, len(all_chi)),
        out_shape=(jax.ShapeDtypeStruct((bd, BLOCK), f32),
                   jax.ShapeDtypeStruct((n, 3 * bd, BLOCK), f32)),
        in_specs=[spec(SM)] * 4 + [spec(VM)] * (6 + len(all_chi)),
        out_specs=(spec(VM),) * 2,
        scratch_shapes=[VM((n, bd, BLOCK), f32), VM((nb + 8, BLOCK), f32),
                        VM((nb + 1, BLOCK, BLOCK), f32), VM((nb + 1, 8, BLOCK), f32),
                        VM((nb + 1, 8, BLOCK), f32),
                        VM((entries + 16 if stored else 1, BLOCK, BLOCK), f32),
                        SM((2, n * (slots - bd) + 12), jnp.int32)],
        compiler_params=pltpu.CompilerParams(vmem_limit_bytes=(42 if stored else 58) << 20),
        name="solve",
    )(me[None], lists, counts, hardness, *all_chi, whole, rows, mids, left, push, nbr)
    forces = reduce_parts(part, n)
    return charges.reshape(atoms), forces.reshape(3, atoms)


def solution(mesh):
    both = ("cell", "blk")
    placed = (P(None, both), P(both), P(None, both), P(None, both)) + (P(),) * 7
    return jax.shard_map(
        on_device,
        mesh=mesh,
        in_specs=placed,
        out_specs=(P(both), P(None, both)),
        check_vma=False,
    )
```

```python
import functools
import math

import jax
import jax.numpy as jnp
import numpy as np
from jax import lax
from jax.experimental import pallas as pl
from jax.experimental.pallas import tpu as pltpu
from jax.sharding import PartitionSpec as P

ELEM = 4
RAD = 16
DESC = ELEM * RAD
BLOCK = 128
NBR = 32
ITERS = 3
PACK = 24
STORE_LIMIT = 36 << 20
WIDE = 8

coulomb_scale = 0.5
sigma_sq = 4.0
cutoff_sq = 49.0
highest = lax.Precision.HIGHEST
RATES = [0.005 * 200.0 ** (k / (RAD - 1)) for k in range(RAD)]
VM = pltpu.VMEM
SM = pltpu.SMEM
SCALE = math.log2(math.e) / (2.0 * sigma_sq)


def spec(space):
    return pl.BlockSpec(memory_space=space)


def piece_of(q, me, pow2):
    return q ^ me if pow2 else q


def dot(a, b, lhs=1):
    return lax.dot_general(a, b, (((lhs,), (0,)), ((), ())), precision=highest,
                           preferred_element_type=jnp.float32)


def column(row):
    return jnp.broadcast_to(row, (BLOCK, BLOCK)).T


def pick(kind, mats):
    out = jnp.where(kind == 0, mats[0], 0.0)
    for e in range(1, ELEM):
        out = jnp.where(kind == e, mats[e], out)
    return out


def one_hot(kind):
    ids = lax.broadcasted_iota(jnp.int32, (ELEM, kind.shape[1]), 0)
    return jnp.where(ids == kind, 1.0, 0.0)


def pack_kernel(count, *refs):
    sources = refs[:count]
    own_ref = refs[count]
    held = refs[count + 1:2 * count + 1]
    sems = refs[-1]
    copies = [pltpu.make_async_copy(sources[k], held[k], sems.at[k]) for k in range(count)]
    for copy in copies:
        copy.start()
    own_ref[...] = jnp.zeros_like(own_ref)
    for copy in copies[:3]:
        copy.wait()
    pos_ref, kind_ref, pairs_ref = held[:3]
    bd = pos_ref.shape[1] // BLOCK
    for a in range(bd):
        lanes = slice(a * BLOCK, (a + 1) * BLOCK)
        for d in range(3):
            own_ref[d * bd + a:d * bd + a + 1, :] = pos_ref[d:d + 1, lanes]
        own_ref[3 * bd + a:3 * bd + a + 1, :] = kind_ref[:, lanes].astype(jnp.float32)
    slots = pairs_ref.shape[1]
    for side in range(2):
        own_ref[4 * bd + side:4 * bd + side + 1, :slots] = (
            pairs_ref[side:side + 1, :].astype(jnp.float32))
    for copy in copies[3:]:
        copy.wait()


def join_pieces(pieces, out_ref):
    first = 0
    for piece in pieces:
        count = piece.shape[0]
        out_ref[first:first + count] = piece[...]
        first += count


def chi_kernel(pow2, nd, bd, parts, me_ref, *refs):
    pieces = refs[:parts]
    (pos_ref, nbr_ref, kind_ref, v1, b1, v2, b2, wo, bo,
     chi_ref, d_ref, h_ref, g_ref, w1, w2, f_ref) = refs[parts:]
    me = me_ref[0]
    chunk = min(nd, 8)
    join_pieces(pieces, g_ref)
    for turned, kept in ((v1, w1), (v2, w2)):
        for h in range(turned.shape[0]):
            for e in range(ELEM):
                kept[e, h:h + 1, :] = turned[h, e:e + 1, :]
    for a in range(bd):
        lanes = slice(a * BLOCK, (a + 1) * BLOCK)

        def group(g, carry):
            rows8 = pl.ds(pl.multiple_of(g * 8, 8), 8)
            idx = nbr_ref[rows8, lanes]
            hi = idx >> 7
            lo = idx & 127

            def look(part, vals):
                for step in range(chunk):
                    q = part * chunk + step
                    at = piece_of(q, me, pow2)
                    for r in range(bd):
                        hit = hi == q * bd + r
                        new = []
                        for d in range(4):
                            row = jnp.broadcast_to(g_ref[at, d * bd + r:d * bd + r + 1, :],
                                                   (8, BLOCK))
                            new.append(jnp.where(hit, jnp.take_along_axis(row, lo, axis=1),
                                                 vals[d]))
                        vals = tuple(new)
                return vals

            vals = (jnp.zeros((8, BLOCK), jnp.float32),) * 4
            if nd == chunk:
                vals = look(0, vals)
            else:
                vals = lax.fori_loop(0, nd // chunk, look, vals)
            live = idx >= 0
            for d in range(3):
                d_ref[d, rows8, lanes] = jnp.where(live, pos_ref[d:d + 1, lanes] - vals[d], 0.0)
            d_ref[3, rows8, lanes] = jnp.where(live, vals[3], -1.0)
            return carry

        lax.fori_loop(0, NBR // 8, group, 0, unroll=4 if nd == chunk else 1)
        offs = [d_ref[d, :, lanes] for d in range(3)]
        nk = d_ref[3, :, lanes]
        r2 = offs[0] * offs[0] + offs[1] * offs[1] + offs[2] * offs[2]
        u = 1.0 - r2 * (1.0 / cutoff_sq)
        shell = u * u * (ELEM / NBR)
        for k in range(RAD):
            val = shell * jnp.exp(-RATES[k] * r2)
            for e in range(ELEM):
                f_ref[e * RAD + k:e * RAD + k + 1, lanes] = jnp.sum(
                    jnp.where(nk == e, val, 0.0), axis=0, keepdims=True)
    kind = kind_ref[...]
    hot = one_hot(kind)
    feats = f_ref[...]
    h1 = jnp.tanh(pick(kind, [dot(w1[e], feats) for e in range(ELEM)]) + dot(b1[...], hot, 0))
    h2 = jnp.tanh(pick(kind, [dot(w2[e], h1) for e in range(ELEM)]) + dot(b2[...], hot, 0))
    h_ref[0] = h1
    h_ref[1] = h2
    chi = jnp.sum(dot(wo[...], hot, 0) * h2, axis=0, keepdims=True) + dot(bo[...], hot)
    for a in range(bd):
        chi_ref[a:a + 1, :] = chi[:, a * BLOCK:(a + 1) * BLOCK]


def fold(vals):
    tiles = vals.reshape(BLOCK // 8, 8, BLOCK)
    terms = [tiles[k] for k in range(BLOCK // 8)]
    while len(terms) > 1:
        terms = [terms[k] + terms[k + 1] for k in range(0, len(terms), 2)]
    return terms[0]


def split3(vals):
    parts = []
    for _ in range(3):
        top = vals.astype(jnp.bfloat16).astype(jnp.float32)
        parts.append(top)
        vals = vals - top
    return parts


def tile_kernel(pow2, nd, bd, nb, me_ref, g_ref, r_ref, mid_ref, a_ref):
    me = me_ref[0]
    sub8 = lax.broadcasted_iota(jnp.int32, (8, BLOCK), 0)
    r_ref[...] = jnp.zeros_like(r_ref)
    for q in range(nd):
        at = piece_of(q, me, pow2)
        for r in range(bd):
            for d in range(3):
                r_ref[q * bd + r, d:d + 1, :] = g_ref[at, d * bd + r:d * bd + r + 1, :]

    def set_block(b, carry):
        mid = jnp.broadcast_to(r_ref[b][:, 0:1], (8, BLOCK))
        mid_ref[b] = mid
        rel = r_ref[b] - mid
        size = jnp.sum(rel * rel, axis=0, keepdims=True)
        tile = jnp.where(sub8 == 3, 1.0,
                         jnp.where(sub8 == 4, size * -SCALE - 1.0, rel * (2.0 * SCALE)))
        q1, q2, q3 = split3(tile)
        a_ref[b] = jnp.concatenate([q1, q1, q2, q1, q3, q2], axis=0).T.astype(jnp.bfloat16)
        return carry

    lax.fori_loop(0, nb + 1, set_block, 0, unroll=11 if nb + 1 == 33 else 1)


def pull_kernel(bd, kind_ref, d_ref, h_ref, w1, w2, wo, push_ref, f_ref):
    kind = kind_ref[...]
    h1 = h_ref[0]
    h2 = h_ref[1]
    pre2 = dot(wo[...], one_hot(kind), 0) * (1.0 - h2 * h2)
    pre1 = sum(dot(w2[e], jnp.where(kind == e, pre2, 0.0), 0) for e in range(ELEM))
    pre1 = pre1 * (1.0 - h1 * h1)
    f_ref[...] = sum(dot(w1[e], jnp.where(kind == e, pre1, 0.0), 0)
                     for e in range(ELEM)) * (ELEM / NBR)
    for a in range(bd):
        lanes = slice(a * BLOCK, (a + 1) * BLOCK)
        offs = [d_ref[d, :, lanes] for d in range(3)]
        nk = d_ref[3, :, lanes]
        r2 = offs[0] * offs[0] + offs[1] * offs[1] + offs[2] * offs[2]
        u = 1.0 - r2 * (1.0 / cutoff_sq)
        s1 = jnp.zeros_like(r2)
        s2 = jnp.zeros_like(r2)
        for k in range(RAD):
            sel = jnp.zeros_like(r2)
            for e in range(ELEM):
                sel = jnp.where(nk == e, f_ref[e * RAD + k:e * RAD + k + 1, lanes], sel)
            term = sel * jnp.exp(-RATES[k] * r2)
            s1 = s1 + term
            s2 = s2 + RATES[k] * term
        grad = -u * ((2.0 / cutoff_sq) * s1 + u * s2)
        for d in range(3):
            push_ref[d, :, lanes] = 2.0 * grad * offs[d]


def list_kernel(pow2, nd, bd, nb, slots, me_ref, pair_ref, count_ref, flat_ref, meta_ref):
    me = me_ref[0]
    cross = slots - bd
    size = 4 if cross % 4 == 0 else 1
    piece = piece_of(me, me, pow2)

    def list_piece(q, carry):
        place, own_place = carry
        number = count_ref[q] - bd

        def list_group(k, inner):
            spots = [(side, m) for side in range(2) for m in range(size)]
            found = [pair_ref[q, side, bd + size * k + m] for side, m in spots]
            for (side, m), block in zip(spots, found):
                flat_ref[side, place + size * k + m] = block
            return inner

        lax.fori_loop(0, (number + size - 1) // size, list_group, 0)
        return place + number, jnp.where(q == piece, place, own_place)

    pairs, own_place = lax.fori_loop(0, nd, list_piece, (jnp.int32(0), jnp.int32(0)))
    for m in range(WIDE):
        for side in range(2):
            flat_ref[side, pairs + m] = nb
    meta_ref[0] = pairs
    meta_ref[1] = own_place


def solve_kernel(pow2, nd, bd, nb, slots, stored, parts, me_ref, flat_ref, meta_ref, counts_ref, hard_ref,
                 *refs):
    pieces = refs[:parts]
    (g_ref, r_ref, mid_ref, a_ref, push_ref, nbr_ref, charge_ref, part_ref, x_ref, p_ref, pc_ref,
     y_ref, s_ref, t_ref) = refs[parts:]
    me = me_ref[0]
    cross = slots - bd
    sub = lax.broadcasted_iota(jnp.int32, (BLOCK, BLOCK), 0)
    ident = sub == lax.broadcasted_iota(jnp.int32, (BLOCK, BLOCK), 1)
    sub8 = lax.broadcasted_iota(jnp.int32, (8, BLOCK), 0)

    join_pieces(pieces, x_ref)
    p_ref[...] = jnp.zeros_like(p_ref)
    hards = []
    for q in range(nd):
        at = piece_of(q, me, pow2)
        span = slice(q * bd, (q + 1) * bd)
        p_ref[span, :] = -x_ref[at]
        hards.append(pick(g_ref[at, 3 * bd:4 * bd, :], [hard_ref[e] for e in range(ELEM)]))
    hard = jnp.concatenate(hards, axis=0)

    def set_charge(b, carry):
        pc_ref[b] = column(p_ref[pl.ds(b, 1), :])
        return carry

    def set_charges():
        if nb > 64:
            lax.fori_loop(0, nb, set_charge, 0)
            return
        turned = jnp.concatenate(split3(p_ref[0:nb]), axis=0).T.astype(jnp.bfloat16)
        ids = lax.broadcasted_iota(jnp.int32, (3 * nb, BLOCK), 0) % nb
        for b in range(0, nb, 2):
            chosen = [jnp.where(ids == b + m, 1.0, 0.0).astype(jnp.bfloat16) for m in range(2)]
            cols = jnp.dot(turned, jnp.concatenate(chosen, axis=1),
                           preferred_element_type=jnp.float32)
            for m in range(2):
                pc_ref[b + m] = cols[:, m * BLOCK:(m + 1) * BLOCK]

    pc_ref[nb] = jnp.zeros((BLOCK, BLOCK), jnp.float32)
    set_charges()

    def slot_of(q):
        return q ^ me if nd == 8 else q

    def power(j, i):
        rel = r_ref[i] - mid_ref[j]
        size = jnp.sum(rel * rel, axis=0, keepdims=True)
        tile = jnp.where(sub8 == 3, size * -SCALE, jnp.where(sub8 == 4, 1.0, rel))
        p1, p2, p3 = split3(tile)
        right = jnp.concatenate([p1, p2, p1, p3, p1, p2], axis=0).astype(jnp.bfloat16)
        return jnp.dot(a_ref[j], right, preferred_element_type=jnp.float32)

    def gamma(j, i):
        return jnp.exp2(power(j, i))

    def own_gamma(b):
        return jnp.where(ident, 0.0, gamma(b, b))

    def entry(t, j, i):
        return t_ref[t] if stored else gamma(j, i)

    def own_entry(b):
        return t_ref[b] if stored else own_gamma(b)

    wide = WIDE
    pairs, own_place = meta_ref[0], meta_ref[1]

    def ends_of(g, width):
        ends = []
        for m in range(width):
            e = g * width + m
            left, right = flat_ref[0, e], flat_ref[1, e]
            ends += [(nb + 2 * e, left, right), (nb + 2 * e + 1, right, left)]
        return ends

    def first_diag(b, carry):
        val = own_gamma(b)
        if stored:
            t_ref[b] = val
        s_ref[b] = fold(val)
        y_ref[b] = fold(val * pc_ref[b])
        return carry

    lax.fori_loop(0, nb, first_diag, 0, unroll=16)

    def first_step(g, carry):
        found = []
        for t, j, i in ends_of(g, wide):
            val = gamma(j, i)
            if stored:
                t_ref[t] = val
            found.append((i, fold(val), fold(val * pc_ref[j])))
        for i, one, two in found:
            s_ref[i] = s_ref[i] + one
            y_ref[i] = y_ref[i] + two
        return carry

    lax.fori_loop(0, (pairs + wide - 1) // wide, first_step, 0)

    def gathered(ref):
        return jnp.sum(ref[0:nb], axis=1)

    diag = hard + gathered(s_ref)

    def next_step(g, carry):
        found = [(i, fold(entry(t, j, i) * pc_ref[j])) for t, j, i in ends_of(g, wide)]
        for i, one in found:
            y_ref[i] = y_ref[i] + one
        return carry

    def next_diag(b, carry):
        y_ref[b] = fold(own_entry(b) * pc_ref[b])
        return carry

    def matvec():
        set_charges()
        lax.fori_loop(0, nb, next_diag, 0, unroll=8)
        lax.fori_loop(0, (pairs + wide - 1) // wide, next_step, 0)

    def total(vals):
        return jnp.sum(jnp.sum(vals, axis=0, keepdims=True), axis=1, keepdims=True)

    res = p_ref[0:nb]
    p = res
    x = jnp.zeros_like(res)
    rho = total(res * res)
    for it in range(ITERS):
        if it:
            matvec()
        image = diag * p + gathered(y_ref)
        step = rho / total(p * image)
        x = x + step * p
        if it + 1 < ITERS:
            res = res - step * image
            rho2 = total(res * res)
            p = res + (rho2 / rho) * p
            rho = rho2
            p_ref[0:nb] = p
    p_ref[0:nb] = x
    for a in range(bd):
        charge_ref[a:a + 1, :] = p_ref[pl.ds(me * bd + a, 1), :]
        set_charge(me * bd + a, 0)
    mine = jnp.concatenate([charge_ref[a:a + 1, :] for a in range(bd)], axis=1)
    width = bd * BLOCK

    several = 4

    bf16 = jnp.bfloat16
    zero16 = jnp.zeros((16, width), bf16)
    one16 = jnp.ones((16, width), bf16)
    lines = lax.broadcasted_iota(jnp.int32, (16, width), 0).astype(jnp.float32)
    wanted = [(lines + 16.0 * k).astype(bf16) for k in range(max(BLOCK, nb) // 16)]

    def spread(row):
        return jnp.broadcast_to(row, (16, width)).astype(bf16)

    def scatter(k, acc):
        lefts = []
        rights = []
        for m in range(several):
            s = k * several + m
            idx = nbr_ref[pl.ds(s, 1), :]
            block = spread((idx >> 7).astype(jnp.float32))
            lane = spread((idx & 127).astype(jnp.float32))
            rights.append(jnp.concatenate(
                [jnp.where(wanted[r] == lane, one16, zero16) for r in range(BLOCK // 16)], axis=0))
            hits = [wanted[r] == block for r in range(nb // 16)]
            upper = []
            lower = []
            for d in range(3):
                val = push_ref[d, pl.ds(s, 1), :] * mine
                top = val.astype(bf16).astype(jnp.float32)
                top16 = spread(top)
                low16 = spread(val - top)
                upper += [jnp.where(hit, top16, zero16) for hit in hits]
                lower += [jnp.where(hit, low16, zero16) for hit in hits]
            lefts.append(jnp.concatenate(upper + lower, axis=0))
        return acc + lax.dot_general(jnp.concatenate(rights, axis=1),
                                     jnp.concatenate(lefts, axis=1), (((1,), (1,)), ((), ())),
                                     preferred_element_type=jnp.float32)

    acc = lax.fori_loop(0, NBR // several, scatter, jnp.zeros((BLOCK, 6 * nb), jnp.float32))
    acc = acc.T
    acc = acc[:3 * nb] + acc[3 * nb:]
    for q in range(nd):
        for d in range(3):
            part_ref[slot_of(q), d * bd:(d + 1) * bd, :] = acc[d * nb + q * bd:d * nb + (q + 1) * bd]

    def moments(rel, weights, side):
        tile = jnp.where(sub8 == 3, 1.0, rel)
        rows = jnp.concatenate(split3(tile) + [jnp.zeros_like(rel)], axis=0).astype(jnp.bfloat16)
        out = lax.dot_general(jnp.concatenate([rows, rows], axis=1),
                              jnp.concatenate(weights, axis=side), (((1,), (side,)), ((), ())),
                              preferred_element_type=jnp.float32)
        return out[0:8] + out[8:16] + out[16:24]

    def force_of(rel, found):
        return (rel * found[3:4] - found) * (0.5 / sigma_sq)

    def weigh(val, j, i):
        both = pc_ref[j] + p_ref[pl.ds(i, 1), :]
        weight = val * (both * both)
        top = weight.astype(jnp.bfloat16)
        return top, (weight - top.astype(jnp.float32)).astype(jnp.bfloat16)

    s_ref[...] = jnp.zeros_like(s_ref)
    for a in range(bd):
        b = me * bd + a
        rel = r_ref[b] - mid_ref[b]
        force = force_of(rel, moments(rel, weigh(own_entry(b), b, b), 0))
        lanes = slice(a * BLOCK, (a + 1) * BLOCK)
        for d in range(3):
            away = jnp.sum(push_ref[d, :, lanes], axis=0, keepdims=True) * charge_ref[a:a + 1, :]
            force = jnp.where(sub8 == d, force - away, force)
        s_ref[b] = force
    together = 4 if cross % 4 == 0 else 1
    own_count = counts_ref[piece_of(me, me, pow2)] - bd

    def own_ends(e):
        real = e < own_count
        return [jnp.where(real, flat_ref[side, own_place + e], nb) for side in range(2)]

    def pair_force(k, carry):
        found = []
        for m in range(together):
            e = k * together + m
            j, i = own_ends(e)
            mid = mid_ref[j]
            rel_j = r_ref[j] - mid
            rel_i = r_ref[i] - mid
            weights = weigh(entry(nb + 2 * (own_place + e), j, i), j, i)
            found.append((i, force_of(rel_i, moments(rel_j, weights, 0))))
            found.append((j, force_of(rel_j, moments(rel_i, weights, 1))))
        for b, force in found:
            s_ref[b] = s_ref[b] + force
        return carry

    lax.fori_loop(0, (own_count + together - 1) // together, pair_force, 0)
    for q in range(nd):
        for d in range(3):
            for r in range(bd):
                at = slice(d * bd + r, d * bd + r + 1)
                part_ref[slot_of(q), at, :] = part_ref[slot_of(q), at, :] + s_ref[q * bd + r, d:d + 1, :]


def swap(vals, step, n):
    return lax.ppermute(vals, "blk", [(i, i ^ step) for i in range(n)])


def gather_far_first(own, n):
    if n & (n - 1):
        return [lax.all_gather(own, "blk")]
    got = own[None]
    step = n // 2
    while step:
        both = jnp.stack([got, swap(got, step, n)], axis=1)
        got = both.reshape((2 * got.shape[0],) + own.shape)
        step //= 2
    return [got]


def gather_near_first(own, n, beside):
    if n & (n - 1):
        return [lax.all_gather(own, "blk")], beside
    got = own[None]
    step = 1
    while step < n:
        got = jnp.concatenate([got, swap(got, step, n)], axis=0)
        if step in (1, 2):
            got, held = lax.optimization_barrier((got, beside[step - 1]))
            beside = (held, beside[1]) if step == 1 else (beside[0], held)
        step *= 2
    return [got], beside


def reduce_parts(part, n):
    if n != 8:
        return jnp.sum(lax.all_to_all(part, "blk", 0, 0), axis=0)
    mine = part[0::2] + swap(part[1::2], 1, n)
    far = [swap(mine[k], 2 * k, n) for k in (1, 2, 3)]
    return mine[0] + far[0] + far[1] + far[2]


def on_device(positions, species, neighbors, pair_lists, hardness, w_first, b_first, w_second,
              b_second, w_out, b_out):
    n = lax.axis_size("blk")
    me = lax.axis_index("blk")
    atoms = positions.shape[1]
    bd = atoms // BLOCK
    nb = bd * n
    slots = pair_lists.shape[1]
    hid = w_first.shape[1]
    f32 = jnp.float32
    kind = species.reshape(1, atoms)
    small = pltpu.CompilerParams(vmem_limit_bytes=24 << 20)
    raw = (positions, kind, pair_lists, neighbors, w_first.transpose(1, 0, 2), b_first,
           w_second.transpose(1, 0, 2), b_second, w_out, b_out.reshape(1, ELEM))
    raw = tuple(pltpu.with_memory_space_constraint(r, pltpu.HBM) for r in raw)
    own, pos, kinds, _, nbr, v1, b1, v2, b2, wo, bo = pl.pallas_call(
        functools.partial(pack_kernel, len(raw)),
        out_shape=(jax.ShapeDtypeStruct((PACK, BLOCK), f32),)
        + tuple(jax.ShapeDtypeStruct(r.shape, r.dtype) for r in raw),
        in_specs=[spec(pltpu.HBM)] * len(raw), out_specs=(spec(VM),) * (1 + len(raw)),
        scratch_shapes=[pltpu.SemaphoreType.DMA((len(raw),))],
        compiler_params=small, name="pack",
    )(*raw)
    pow2 = n & (n - 1) == 0
    places = gather_far_first(own, n)
    chi, offs, hidden, whole, w1, w2 = pl.pallas_call(
        functools.partial(chi_kernel, pow2, n, bd, len(places)),
        out_shape=(jax.ShapeDtypeStruct((bd, BLOCK), f32),
                   jax.ShapeDtypeStruct((4, NBR, atoms), f32),
                   jax.ShapeDtypeStruct((2, hid, atoms), f32),
                   jax.ShapeDtypeStruct((n, PACK, BLOCK), f32),
                   jax.ShapeDtypeStruct(w_first.shape, f32),
                   jax.ShapeDtypeStruct(w_second.shape, f32)),
        in_specs=[spec(SM)] + [spec(VM)] * (9 + len(places)),
        out_specs=(spec(VM),) * 6,
        scratch_shapes=[VM((DESC, atoms), f32)],
        compiler_params=small,
        name="chi",
    )(me[None], *places, pos, nbr, kinds, v1, b1, v2, b2, wo, bo)
    lists = whole[:, 4 * bd:4 * bd + 2, :slots].astype(jnp.int32)
    counts = jnp.sum((lists[:, 0] >= 0).astype(jnp.int32), axis=1)
    lists = jnp.where(lists < 0, nb, lists)
    compact = pl.pallas_call(
        functools.partial(list_kernel, pow2, n, bd, nb, slots),
        out_shape=(jax.ShapeDtypeStruct((2, n * (slots - bd) + 12), jnp.int32),
                   jax.ShapeDtypeStruct((2,), jnp.int32)),
        in_specs=[spec(SM)] * 3,
        out_specs=(spec(SM),) * 2,
        compiler_params=small,
        name="lists",
    )(me[None], lists, counts)
    tiles = pl.pallas_call(
        functools.partial(tile_kernel, pow2, n, bd, nb),
        out_shape=(jax.ShapeDtypeStruct((nb + 1, 8, BLOCK), f32),
                   jax.ShapeDtypeStruct((nb + 1, 8, BLOCK), f32),
                   jax.ShapeDtypeStruct((nb + 1, BLOCK, 48), jnp.bfloat16)),
        in_specs=[spec(SM), spec(VM)],
        out_specs=(spec(VM),) * 3,
        compiler_params=small,
        name="tiles",
    )(me[None], whole)
    all_chi, ((flat, meta), (rows, mids, left)) = gather_near_first(chi, n, (compact, tiles))
    push = pl.pallas_call(
        functools.partial(pull_kernel, bd),
        out_shape=jax.ShapeDtypeStruct((3, NBR, atoms), f32),
        in_specs=[spec(VM)] * 6,
        out_specs=spec(VM),
        scratch_shapes=[VM((DESC, atoms), f32)],
        compiler_params=small,
        name="pull",
    )(kinds, offs, hidden, w1, w2, wo)
    entries = nb + 2 * (n * slots - nb)
    stored = entries * BLOCK * BLOCK * 4 <= STORE_LIMIT
    charges, part = pl.pallas_call(
        functools.partial(solve_kernel, pow2, n, bd, nb, slots, stored, len(all_chi)),
        out_shape=(jax.ShapeDtypeStruct((bd, BLOCK), f32),
                   jax.ShapeDtypeStruct((n, 3 * bd, BLOCK), f32)),
        in_specs=[spec(SM)] * 5 + [spec(VM)] * (6 + len(all_chi)),
        out_specs=(spec(VM),) * 2,
        scratch_shapes=[VM((n, bd, BLOCK), f32), VM((nb + 8, BLOCK), f32),
                        VM((nb + 1, BLOCK, BLOCK), f32), VM((nb + 1, 8, BLOCK), f32),
                        VM((nb + 1, 8, BLOCK), f32),
                        VM((entries + 16 if stored else 1, BLOCK, BLOCK), f32)],
        compiler_params=pltpu.CompilerParams(vmem_limit_bytes=(42 if stored else 58) << 20),
        name="solve",
    )(me[None], flat, meta, counts, hardness, *all_chi, whole, rows, mids, left, push, nbr)
    forces = reduce_parts(part, n)
    return charges.reshape(atoms), forces.reshape(3, atoms)


def solution(mesh):
    both = ("cell", "blk")
    placed = (P(None, both), P(both), P(None, both), P(None, both)) + (P(),) * 7
    return jax.shard_map(
        on_device,
        mesh=mesh,
        in_specs=placed,
        out_specs=(P(both), P(None, both)),
        check_vma=False,
    )
```

```python
import functools
import math

import jax
import jax.numpy as jnp
import numpy as np
from jax import lax
from jax.experimental import pallas as pl
from jax.experimental.pallas import tpu as pltpu
from jax.sharding import PartitionSpec as P

ELEM = 4
RAD = 16
DESC = ELEM * RAD
BLOCK = 128
NBR = 32
ITERS = 3
PACK = 24
STORE_LIMIT = 36 << 20

coulomb_scale = 0.5
sigma_sq = 4.0
cutoff_sq = 49.0
highest = lax.Precision.HIGHEST
RATES = [0.005 * 200.0 ** (k / (RAD - 1)) for k in range(RAD)]
VM = pltpu.VMEM
SM = pltpu.SMEM
SCALE = math.log2(math.e) / (2.0 * sigma_sq)


def spec(space):
    return pl.BlockSpec(memory_space=space)


def piece_of(q, me, pow2):
    return q ^ me if pow2 else q


def dot(a, b, lhs=1):
    return lax.dot_general(a, b, (((lhs,), (0,)), ((), ())), precision=highest,
                           preferred_element_type=jnp.float32)


def column(row):
    return jnp.broadcast_to(row, (BLOCK, BLOCK)).T


def pick(kind, mats):
    out = jnp.where(kind == 0, mats[0], 0.0)
    for e in range(1, ELEM):
        out = jnp.where(kind == e, mats[e], out)
    return out


def one_hot(kind):
    ids = lax.broadcasted_iota(jnp.int32, (ELEM, kind.shape[1]), 0)
    return jnp.where(ids == kind, 1.0, 0.0)


def pack_kernel(count, *refs):
    sources = refs[:count]
    own_ref = refs[count]
    held = refs[count + 1:2 * count + 1]
    sems = refs[-1]
    copies = [pltpu.make_async_copy(sources[k], held[k], sems.at[k]) for k in range(count)]
    for copy in copies:
        copy.start()
    own_ref[...] = jnp.zeros_like(own_ref)
    for copy in copies[:3]:
        copy.wait()
    pos_ref, kind_ref, pairs_ref = held[:3]
    bd = pos_ref.shape[1] // BLOCK
    for a in range(bd):
        lanes = slice(a * BLOCK, (a + 1) * BLOCK)
        for d in range(3):
            own_ref[d * bd + a:d * bd + a + 1, :] = pos_ref[d:d + 1, lanes]
        own_ref[3 * bd + a:3 * bd + a + 1, :] = kind_ref[:, lanes].astype(jnp.float32)
    slots = pairs_ref.shape[1]
    for side in range(2):
        own_ref[4 * bd + side:4 * bd + side + 1, :slots] = (
            pairs_ref[side:side + 1, :].astype(jnp.float32))
    for copy in copies[3:]:
        copy.wait()


def join_pieces(pieces, out_ref):
    first = 0
    for piece in pieces:
        count = piece.shape[0]
        out_ref[first:first + count] = piece[...]
        first += count


def chi_kernel(pow2, nd, bd, parts, me_ref, *refs):
    pieces = refs[:parts]
    (pos_ref, nbr_ref, kind_ref, v1, b1, v2, b2, wo, bo,
     chi_ref, d_ref, h_ref, g_ref, w1, w2, f_ref) = refs[parts:]
    me = me_ref[0]
    chunk = min(nd, 8)
    join_pieces(pieces, g_ref)
    for turned, kept in ((v1, w1), (v2, w2)):
        for h in range(turned.shape[0]):
            for e in range(ELEM):
                kept[e, h:h + 1, :] = turned[h, e:e + 1, :]
    for a in range(bd):
        lanes = slice(a * BLOCK, (a + 1) * BLOCK)

        def group(g, carry):
            rows8 = pl.ds(pl.multiple_of(g * 8, 8), 8)
            idx = nbr_ref[rows8, lanes]
            hi = idx >> 7
            lo = idx & 127

            def look(part, vals):
                for step in range(chunk):
                    q = part * chunk + step
                    at = piece_of(q, me, pow2)
                    for r in range(bd):
                        hit = hi == q * bd + r
                        new = []
                        for d in range(4):
                            row = jnp.broadcast_to(g_ref[at, d * bd + r:d * bd + r + 1, :],
                                                   (8, BLOCK))
                            new.append(jnp.where(hit, jnp.take_along_axis(row, lo, axis=1),
                                                 vals[d]))
                        vals = tuple(new)
                return vals

            vals = (jnp.zeros((8, BLOCK), jnp.float32),) * 4
            if nd == chunk:
                vals = look(0, vals)
            else:
                vals = lax.fori_loop(0, nd // chunk, look, vals)
            live = idx >= 0
            for d in range(3):
                d_ref[d, rows8, lanes] = jnp.where(live, pos_ref[d:d + 1, lanes] - vals[d], 0.0)
            d_ref[3, rows8, lanes] = jnp.where(live, vals[3], -1.0)
            return carry

        lax.fori_loop(0, NBR // 8, group, 0, unroll=4 if nd == chunk else 1)
        offs = [d_ref[d, :, lanes] for d in range(3)]
        nk = d_ref[3, :, lanes]
        r2 = offs[0] * offs[0] + offs[1] * offs[1] + offs[2] * offs[2]
        u = 1.0 - r2 * (1.0 / cutoff_sq)
        shell = u * u * (ELEM / NBR)
        for k in range(RAD):
            val = shell * jnp.exp(-RATES[k] * r2)
            for e in range(ELEM):
                f_ref[e * RAD + k:e * RAD + k + 1, lanes] = jnp.sum(
                    jnp.where(nk == e, val, 0.0), axis=0, keepdims=True)
    kind = kind_ref[...]
    hot = one_hot(kind)
    feats = f_ref[...]
    h1 = jnp.tanh(pick(kind, [dot(w1[e], feats) for e in range(ELEM)]) + dot(b1[...], hot, 0))
    h2 = jnp.tanh(pick(kind, [dot(w2[e], h1) for e in range(ELEM)]) + dot(b2[...], hot, 0))
    h_ref[0] = h1
    h_ref[1] = h2
    chi = jnp.sum(dot(wo[...], hot, 0) * h2, axis=0, keepdims=True) + dot(bo[...], hot)
    for a in range(bd):
        chi_ref[a:a + 1, :] = chi[:, a * BLOCK:(a + 1) * BLOCK]


def fold(vals):
    tiles = vals.reshape(BLOCK // 8, 8, BLOCK)
    terms = [tiles[k] for k in range(BLOCK // 8)]
    while len(terms) > 1:
        terms = [terms[k] + terms[k + 1] for k in range(0, len(terms), 2)]
    return terms[0]


def split3(vals):
    parts = []
    for _ in range(3):
        top = vals.astype(jnp.bfloat16).astype(jnp.float32)
        parts.append(top)
        vals = vals - top
    return parts


def tile_kernel(pow2, nd, bd, nb, me_ref, g_ref, r_ref, mid_ref, a_ref):
    me = me_ref[0]
    sub8 = lax.broadcasted_iota(jnp.int32, (8, BLOCK), 0)
    r_ref[...] = jnp.zeros_like(r_ref)
    for q in range(nd):
        at = piece_of(q, me, pow2)
        for r in range(bd):
            for d in range(3):
                r_ref[q * bd + r, d:d + 1, :] = g_ref[at, d * bd + r:d * bd + r + 1, :]

    def set_block(b, carry):
        mid = jnp.broadcast_to(r_ref[b][:, 0:1], (8, BLOCK))
        mid_ref[b] = mid
        rel = r_ref[b] - mid
        size = jnp.sum(rel * rel, axis=0, keepdims=True)
        tile = jnp.where(sub8 == 3, 1.0,
                         jnp.where(sub8 == 4, size * -SCALE - 1.0, rel * (2.0 * SCALE)))
        q1, q2, q3 = split3(tile)
        a_ref[b] = jnp.concatenate([q1, q1, q2, q1, q3, q2], axis=0).T.astype(jnp.bfloat16)
        return carry

    lax.fori_loop(0, nb + 1, set_block, 0, unroll=11 if nb + 1 == 33 else 1)


def pull_kernel(bd, kind_ref, d_ref, h_ref, w1, w2, wo, push_ref, f_ref):
    kind = kind_ref[...]
    h1 = h_ref[0]
    h2 = h_ref[1]
    pre2 = dot(wo[...], one_hot(kind), 0) * (1.0 - h2 * h2)
    pre1 = sum(dot(w2[e], jnp.where(kind == e, pre2, 0.0), 0) for e in range(ELEM))
    pre1 = pre1 * (1.0 - h1 * h1)
    f_ref[...] = sum(dot(w1[e], jnp.where(kind == e, pre1, 0.0), 0)
                     for e in range(ELEM)) * (ELEM / NBR)
    for a in range(bd):
        lanes = slice(a * BLOCK, (a + 1) * BLOCK)
        offs = [d_ref[d, :, lanes] for d in range(3)]
        nk = d_ref[3, :, lanes]
        r2 = offs[0] * offs[0] + offs[1] * offs[1] + offs[2] * offs[2]
        u = 1.0 - r2 * (1.0 / cutoff_sq)
        s1 = jnp.zeros_like(r2)
        s2 = jnp.zeros_like(r2)
        for k in range(RAD):
            sel = jnp.zeros_like(r2)
            for e in range(ELEM):
                sel = jnp.where(nk == e, f_ref[e * RAD + k:e * RAD + k + 1, lanes], sel)
            term = sel * jnp.exp(-RATES[k] * r2)
            s1 = s1 + term
            s2 = s2 + RATES[k] * term
        grad = -u * ((2.0 / cutoff_sq) * s1 + u * s2)
        for d in range(3):
            push_ref[d, :, lanes] = 2.0 * grad * offs[d]


def solve_kernel(pow2, nd, bd, nb, slots, stored, parts, me_ref, pair_ref, count_ref, hard_ref,
                 *refs):
    pieces = refs[:parts]
    (g_ref, r_ref, mid_ref, a_ref, push_ref, nbr_ref, charge_ref, part_ref, x_ref, p_ref, pc_ref,
     y_ref, s_ref, t_ref, left_ref, right_ref) = refs[parts:]
    flat_refs = (left_ref, right_ref)
    me = me_ref[0]
    cross = slots - bd
    sub = lax.broadcasted_iota(jnp.int32, (BLOCK, BLOCK), 0)
    ident = sub == lax.broadcasted_iota(jnp.int32, (BLOCK, BLOCK), 1)
    sub8 = lax.broadcasted_iota(jnp.int32, (8, BLOCK), 0)

    join_pieces(pieces, x_ref)
    p_ref[...] = jnp.zeros_like(p_ref)
    hards = []
    for q in range(nd):
        at = piece_of(q, me, pow2)
        span = slice(q * bd, (q + 1) * bd)
        p_ref[span, :] = -x_ref[at]
        hards.append(pick(g_ref[at, 3 * bd:4 * bd, :], [hard_ref[e] for e in range(ELEM)]))
    hard = jnp.concatenate(hards, axis=0)

    def set_charge(b, carry):
        pc_ref[b] = column(p_ref[pl.ds(b, 1), :])
        return carry

    def set_charges():
        if nb > 64:
            lax.fori_loop(0, nb, set_charge, 0)
            return
        turned = jnp.concatenate(split3(p_ref[0:nb]), axis=0).T.astype(jnp.bfloat16)
        ids = lax.broadcasted_iota(jnp.int32, (3 * nb, BLOCK), 0) % nb
        for b in range(0, nb, 2):
            chosen = [jnp.where(ids == b + m, 1.0, 0.0).astype(jnp.bfloat16) for m in range(2)]
            cols = jnp.dot(turned, jnp.concatenate(chosen, axis=1),
                           preferred_element_type=jnp.float32)
            for m in range(2):
                pc_ref[b + m] = cols[:, m * BLOCK:(m + 1) * BLOCK]

    pc_ref[nb] = jnp.zeros((BLOCK, BLOCK), jnp.float32)
    set_charges()

    def slot_of(q):
        return q ^ me if nd == 8 else q

    def power(j, i):
        rel = r_ref[i] - mid_ref[j]
        size = jnp.sum(rel * rel, axis=0, keepdims=True)
        tile = jnp.where(sub8 == 3, size * -SCALE, jnp.where(sub8 == 4, 1.0, rel))
        p1, p2, p3 = split3(tile)
        right = jnp.concatenate([p1, p2, p1, p3, p1, p2], axis=0).astype(jnp.bfloat16)
        return jnp.dot(a_ref[j], right, preferred_element_type=jnp.float32)

    def gamma(j, i):
        return jnp.exp2(power(j, i))

    def own_gamma(b):
        return jnp.where(ident, 0.0, gamma(b, b))

    def entry(t, j, i):
        return t_ref[t] if stored else gamma(j, i)

    def own_entry(b):
        return t_ref[b] if stored else own_gamma(b)

    size = 4 if cross % 4 == 0 else 1
    wide = 8
    piece = piece_of(me, me, pow2)

    def list_piece(q, carry):
        place, own_place = carry
        number = count_ref[q] - bd

        def list_group(k, inner):
            spots = [(side, m) for side in range(2) for m in range(size)]
            first = 2 * slots * q + bd + size * k
            found = [pair_ref[first + side * slots + m] for side, m in spots]
            for (side, m), block in zip(spots, found):
                flat_refs[side][place + size * k + m] = block
            return inner

        lax.fori_loop(0, (number + size - 1) // size, list_group, 0)
        return place + number, jnp.where(q == piece, place, own_place)

    pairs, own_place = lax.fori_loop(0, nd, list_piece, (jnp.int32(0), jnp.int32(0)))
    for m in range(wide):
        for side in range(2):
            flat_refs[side][pairs + m] = nb

    def ends_of(g, width):
        ends = []
        for m in range(width):
            e = g * width + m
            left, right = flat_refs[0][e], flat_refs[1][e]
            ends += [(nb + 2 * e, left, right), (nb + 2 * e + 1, right, left)]
        return ends

    def first_diag(b, carry):
        val = own_gamma(b)
        if stored:
            t_ref[b] = val
        s_ref[b] = fold(val)
        y_ref[b] = fold(val * pc_ref[b])
        return carry

    lax.fori_loop(0, nb, first_diag, 0, unroll=16)

    def first_step(g, carry):
        found = []
        for t, j, i in ends_of(g, wide):
            val = gamma(j, i)
            if stored:
                t_ref[t] = val
            found.append((i, fold(val), fold(val * pc_ref[j])))
        for i, one, two in found:
            s_ref[i] = s_ref[i] + one
            y_ref[i] = y_ref[i] + two
        return carry

    lax.fori_loop(0, (pairs + wide - 1) // wide, first_step, 0)

    def gathered(ref):
        return jnp.sum(ref[0:nb], axis=1)

    diag = hard + gathered(s_ref)

    def next_step(g, carry):
        found = [(i, fold(entry(t, j, i) * pc_ref[j])) for t, j, i in ends_of(g, wide)]
        for i, one in found:
            y_ref[i] = y_ref[i] + one
        return carry

    def next_diag(b, carry):
        y_ref[b] = fold(own_entry(b) * pc_ref[b])
        return carry

    def matvec():
        set_charges()
        lax.fori_loop(0, nb, next_diag, 0, unroll=8)
        lax.fori_loop(0, (pairs + wide - 1) // wide, next_step, 0)

    def total(vals):
        return jnp.sum(jnp.sum(vals, axis=0, keepdims=True), axis=1, keepdims=True)

    res = p_ref[0:nb]
    p = res
    x = jnp.zeros_like(res)
    rho = total(res * res)
    for it in range(ITERS):
        if it:
            matvec()
        image = diag * p + gathered(y_ref)
        step = rho / total(p * image)
        x = x + step * p
        if it + 1 < ITERS:
            res = res - step * image
            rho2 = total(res * res)
            p = res + (rho2 / rho) * p
            rho = rho2
            p_ref[0:nb] = p
    p_ref[0:nb] = x
    for a in range(bd):
        charge_ref[a:a + 1, :] = p_ref[pl.ds(me * bd + a, 1), :]
        set_charge(me * bd + a, 0)
    mine = jnp.concatenate([charge_ref[a:a + 1, :] for a in range(bd)], axis=1)
    width = bd * BLOCK

    several = 4

    bf16 = jnp.bfloat16
    zero16 = jnp.zeros((16, width), bf16)
    one16 = jnp.ones((16, width), bf16)
    lines = lax.broadcasted_iota(jnp.int32, (16, width), 0).astype(jnp.float32)
    wanted = [(lines + 16.0 * k).astype(bf16) for k in range(max(BLOCK, nb) // 16)]

    def spread(row):
        return jnp.broadcast_to(row, (16, width)).astype(bf16)

    def scatter(k, acc):
        lefts = []
        rights = []
        for m in range(several):
            s = k * several + m
            idx = nbr_ref[pl.ds(s, 1), :]
            block = spread((idx >> 7).astype(jnp.float32))
            lane = spread((idx & 127).astype(jnp.float32))
            rights.append(jnp.concatenate(
                [jnp.where(wanted[r] == lane, one16, zero16) for r in range(BLOCK // 16)], axis=0))
            hits = [wanted[r] == block for r in range(nb // 16)]
            upper = []
            lower = []
            for d in range(3):
                val = push_ref[d, pl.ds(s, 1), :] * mine
                top = val.astype(bf16).astype(jnp.float32)
                top16 = spread(top)
                low16 = spread(val - top)
                upper += [jnp.where(hit, top16, zero16) for hit in hits]
                lower += [jnp.where(hit, low16, zero16) for hit in hits]
            lefts.append(jnp.concatenate(upper + lower, axis=0))
        return acc + lax.dot_general(jnp.concatenate(rights, axis=1),
                                     jnp.concatenate(lefts, axis=1), (((1,), (1,)), ((), ())),
                                     preferred_element_type=jnp.float32)

    acc = lax.fori_loop(0, NBR // several, scatter, jnp.zeros((BLOCK, 6 * nb), jnp.float32))
    acc = acc.T
    acc = acc[:3 * nb] + acc[3 * nb:]
    for q in range(nd):
        for d in range(3):
            part_ref[slot_of(q), d * bd:(d + 1) * bd, :] = acc[d * nb + q * bd:d * nb + (q + 1) * bd]

    def moments(rel, weights, side):
        tile = jnp.where(sub8 == 3, 1.0, rel)
        rows = jnp.concatenate(split3(tile) + [jnp.zeros_like(rel)], axis=0).astype(jnp.bfloat16)
        out = lax.dot_general(jnp.concatenate([rows, rows], axis=1),
                              jnp.concatenate(weights, axis=side), (((1,), (side,)), ((), ())),
                              preferred_element_type=jnp.float32)
        return out[0:8] + out[8:16] + out[16:24]

    def force_of(rel, found):
        return (rel * found[3:4] - found) * (0.5 / sigma_sq)

    def weigh(val, j, i):
        both = pc_ref[j] + p_ref[pl.ds(i, 1), :]
        weight = val * (both * both)
        top = weight.astype(jnp.bfloat16)
        return top, (weight - top.astype(jnp.float32)).astype(jnp.bfloat16)

    s_ref[...] = jnp.zeros_like(s_ref)
    for a in range(bd):
        b = me * bd + a
        rel = r_ref[b] - mid_ref[b]
        force = force_of(rel, moments(rel, weigh(own_entry(b), b, b), 0))
        lanes = slice(a * BLOCK, (a + 1) * BLOCK)
        for d in range(3):
            away = jnp.sum(push_ref[d, :, lanes], axis=0, keepdims=True) * charge_ref[a:a + 1, :]
            force = jnp.where(sub8 == d, force - away, force)
        s_ref[b] = force
    together = 4 if cross % 4 == 0 else 1

    def pair_force(k, carry):
        found = []
        for m in range(together):
            e = k * together + m
            spot = 2 * slots * piece + bd + e
            j, i = pair_ref[spot], pair_ref[spot + slots]
            mid = mid_ref[j]
            rel_j = r_ref[j] - mid
            rel_i = r_ref[i] - mid
            weights = weigh(entry(nb + 2 * (own_place + e), j, i), j, i)
            found.append((i, force_of(rel_i, moments(rel_j, weights, 0))))
            found.append((j, force_of(rel_j, moments(rel_i, weights, 1))))
        for b, force in found:
            s_ref[b] = s_ref[b] + force
        return carry

    lax.fori_loop(0, (count_ref[piece] - bd + together - 1) // together, pair_force, 0)
    for q in range(nd):
        for d in range(3):
            for r in range(bd):
                at = slice(d * bd + r, d * bd + r + 1)
                part_ref[slot_of(q), at, :] = part_ref[slot_of(q), at, :] + s_ref[q * bd + r, d:d + 1, :]


def swap(vals, step, n):
    return lax.ppermute(vals, "blk", [(i, i ^ step) for i in range(n)])


def gather_far_first(own, n):
    if n & (n - 1):
        return [lax.all_gather(own, "blk")]
    got = own[None]
    step = n // 2
    while step:
        both = jnp.stack([got, swap(got, step, n)], axis=1)
        got = both.reshape((2 * got.shape[0],) + own.shape)
        step //= 2
    return [got]


def gather_near_first(own, n, beside):
    if n & (n - 1):
        return [lax.all_gather(own, "blk")], beside
    got = own[None]
    step = 1
    while step < n:
        got = jnp.concatenate([got, swap(got, step, n)], axis=0)
        if step == n // 4:
            got, beside = lax.optimization_barrier((got, beside))
        step *= 2
    return [got], beside


def reduce_parts(part, n):
    if n != 8:
        return jnp.sum(lax.all_to_all(part, "blk", 0, 0), axis=0)
    mine = part[0::2] + swap(part[1::2], 1, n)
    far = [swap(mine[k], 2 * k, n) for k in (1, 2, 3)]
    return mine[0] + far[0] + far[1] + far[2]


def on_device(positions, species, neighbors, pair_lists, hardness, w_first, b_first, w_second,
              b_second, w_out, b_out):
    n = lax.axis_size("blk")
    me = lax.axis_index("blk")
    atoms = positions.shape[1]
    bd = atoms // BLOCK
    nb = bd * n
    slots = pair_lists.shape[1]
    hid = w_first.shape[1]
    f32 = jnp.float32
    kind = species.reshape(1, atoms)
    small = pltpu.CompilerParams(vmem_limit_bytes=24 << 20)
    raw = (positions, kind, pair_lists, neighbors, w_first.transpose(1, 0, 2), b_first,
           w_second.transpose(1, 0, 2), b_second, w_out, b_out.reshape(1, ELEM))
    raw = tuple(pltpu.with_memory_space_constraint(r, pltpu.HBM) for r in raw)
    own, pos, kinds, _, nbr, v1, b1, v2, b2, wo, bo = pl.pallas_call(
        functools.partial(pack_kernel, len(raw)),
        out_shape=(jax.ShapeDtypeStruct((PACK, BLOCK), f32),)
        + tuple(jax.ShapeDtypeStruct(r.shape, r.dtype) for r in raw),
        in_specs=[spec(pltpu.HBM)] * len(raw), out_specs=(spec(VM),) * (1 + len(raw)),
        scratch_shapes=[pltpu.SemaphoreType.DMA((len(raw),))],
        compiler_params=small, name="pack",
    )(*raw)
    pow2 = n & (n - 1) == 0
    places = gather_far_first(own, n)
    chi, offs, hidden, whole, w1, w2 = pl.pallas_call(
        functools.partial(chi_kernel, pow2, n, bd, len(places)),
        out_shape=(jax.ShapeDtypeStruct((bd, BLOCK), f32),
                   jax.ShapeDtypeStruct((4, NBR, atoms), f32),
                   jax.ShapeDtypeStruct((2, hid, atoms), f32),
                   jax.ShapeDtypeStruct((n, PACK, BLOCK), f32),
                   jax.ShapeDtypeStruct(w_first.shape, f32),
                   jax.ShapeDtypeStruct(w_second.shape, f32)),
        in_specs=[spec(SM)] + [spec(VM)] * (9 + len(places)),
        out_specs=(spec(VM),) * 6,
        scratch_shapes=[VM((DESC, atoms), f32)],
        compiler_params=small,
        name="chi",
    )(me[None], *places, pos, nbr, kinds, v1, b1, v2, b2, wo, bo)
    tiles = pl.pallas_call(
        functools.partial(tile_kernel, pow2, n, bd, nb),
        out_shape=(jax.ShapeDtypeStruct((nb + 1, 8, BLOCK), f32),
                   jax.ShapeDtypeStruct((nb + 1, 8, BLOCK), f32),
                   jax.ShapeDtypeStruct((nb + 1, BLOCK, 48), jnp.bfloat16)),
        in_specs=[spec(SM), spec(VM)],
        out_specs=(spec(VM),) * 3,
        compiler_params=small,
        name="tiles",
    )(me[None], whole)
    all_chi, (rows, mids, left) = gather_near_first(chi, n, tiles)
    push = pl.pallas_call(
        functools.partial(pull_kernel, bd),
        out_shape=jax.ShapeDtypeStruct((3, NBR, atoms), f32),
        in_specs=[spec(VM)] * 6,
        out_specs=spec(VM),
        scratch_shapes=[VM((DESC, atoms), f32)],
        compiler_params=small,
        name="pull",
    )(kinds, offs, hidden, w1, w2, wo)
    lists = whole[:, 4 * bd:4 * bd + 2, :slots].astype(jnp.int32)
    counts = jnp.sum((lists[:, 0] >= 0).astype(jnp.int32), axis=1)
    lists = jnp.where(lists < 0, nb, lists)
    lists = lists.reshape(-1)
    entries = nb + 2 * (n * slots - nb)
    stored = entries * BLOCK * BLOCK * 4 <= STORE_LIMIT
    charges, part = pl.pallas_call(
        functools.partial(solve_kernel, pow2, n, bd, nb, slots, stored, len(all_chi)),
        out_shape=(jax.ShapeDtypeStruct((bd, BLOCK), f32),
                   jax.ShapeDtypeStruct((n, 3 * bd, BLOCK), f32)),
        in_specs=[spec(SM)] * 4 + [spec(VM)] * (6 + len(all_chi)),
        out_specs=(spec(VM),) * 2,
        scratch_shapes=[VM((n, bd, BLOCK), f32), VM((nb + 8, BLOCK), f32),
                        VM((nb + 1, BLOCK, BLOCK), f32), VM((nb + 1, 8, BLOCK), f32),
                        VM((nb + 1, 8, BLOCK), f32),
                        VM((entries + 16 if stored else 1, BLOCK, BLOCK), f32),
                        SM((n * (slots - bd) + 12,), jnp.int32),
                        SM((n * (slots - bd) + 12,), jnp.int32)],
        compiler_params=pltpu.CompilerParams(vmem_limit_bytes=(42 if stored else 58) << 20),
        name="solve",
    )(me[None], lists, counts, hardness, *all_chi, whole, rows, mids, left, push, nbr)
    forces = reduce_parts(part, n)
    return charges.reshape(atoms), forces.reshape(3, atoms)


def solution(mesh):
    both = ("cell", "blk")
    placed = (P(None, both), P(both), P(None, both), P(None, both)) + (P(),) * 7
    return jax.shard_map(
        on_device,
        mesh=mesh,
        in_specs=placed,
        out_specs=(P(both), P(None, both)),
        check_vma=False,
    )
```

```python
import functools
import math

import jax
import jax.numpy as jnp
import numpy as np
from jax import lax
from jax.experimental import pallas as pl
from jax.experimental.pallas import tpu as pltpu
from jax.sharding import PartitionSpec as P

ELEM = 4
RAD = 16
DESC = ELEM * RAD
BLOCK = 128
NBR = 32
ITERS = 3
PACK = 24
STORE_LIMIT = 36 << 20

coulomb_scale = 0.5
sigma_sq = 4.0
cutoff_sq = 49.0
highest = lax.Precision.HIGHEST
RATES = [0.005 * 200.0 ** (k / (RAD - 1)) for k in range(RAD)]
VM = pltpu.VMEM
SM = pltpu.SMEM
SCALE = math.log2(math.e) / (2.0 * sigma_sq)


def spec(space):
    return pl.BlockSpec(memory_space=space)


def piece_of(q, me, pow2):
    return q ^ me if pow2 else q


def dot(a, b, lhs=1):
    return lax.dot_general(a, b, (((lhs,), (0,)), ((), ())), precision=highest,
                           preferred_element_type=jnp.float32)


def column(row):
    return jnp.broadcast_to(row, (BLOCK, BLOCK)).T


def pick(kind, mats):
    out = jnp.where(kind == 0, mats[0], 0.0)
    for e in range(1, ELEM):
        out = jnp.where(kind == e, mats[e], out)
    return out


def one_hot(kind):
    ids = lax.broadcasted_iota(jnp.int32, (ELEM, kind.shape[1]), 0)
    return jnp.where(ids == kind, 1.0, 0.0)


def start_copies(sources, targets, sems):
    copies = [pltpu.make_async_copy(source, target, sems.at[k])
              for k, (source, target) in enumerate(zip(sources, targets))]
    for copy in copies:
        copy.start()
    return copies


def stage_kernel(count, *refs):
    for copy in start_copies(refs[:count], refs[count:2 * count], refs[-1]):
        copy.wait()


def pack_kernel(pos_hbm, kind_hbm, pairs_hbm, own_ref, pos_ref, kind_ref, pairs_ref, sems):
    copies = start_copies((pos_hbm, kind_hbm, pairs_hbm), (pos_ref, kind_ref, pairs_ref), sems)
    own_ref[...] = jnp.zeros_like(own_ref)
    for copy in copies:
        copy.wait()
    bd = pos_ref.shape[1] // BLOCK
    for a in range(bd):
        lanes = slice(a * BLOCK, (a + 1) * BLOCK)
        for d in range(3):
            own_ref[d * bd + a:d * bd + a + 1, :] = pos_ref[d:d + 1, lanes]
        own_ref[3 * bd + a:3 * bd + a + 1, :] = kind_ref[:, lanes].astype(jnp.float32)
    slots = pairs_ref.shape[1]
    for side in range(2):
        own_ref[4 * bd + side:4 * bd + side + 1, :slots] = (
            pairs_ref[side:side + 1, :].astype(jnp.float32))


def join_pieces(pieces, out_ref):
    first = 0
    for piece in pieces:
        count = piece.shape[0]
        out_ref[first:first + count] = piece[...]
        first += count


def chi_kernel(pow2, nd, bd, parts, me_ref, *refs):
    pieces = refs[:parts]
    (pos_ref, nbr_ref, kind_ref, v1, b1, v2, b2, wo, bo,
     chi_ref, d_ref, h_ref, g_ref, w1, w2, f_ref) = refs[parts:]
    me = me_ref[0]
    chunk = min(nd, 8)
    join_pieces(pieces, g_ref)
    for turned, kept in ((v1, w1), (v2, w2)):
        for h in range(turned.shape[0]):
            for e in range(ELEM):
                kept[e, h:h + 1, :] = turned[h, e:e + 1, :]
    for a in range(bd):
        lanes = slice(a * BLOCK, (a + 1) * BLOCK)

        def group(g, carry):
            rows8 = pl.ds(pl.multiple_of(g * 8, 8), 8)
            idx = nbr_ref[rows8, lanes]
            hi = idx >> 7
            lo = idx & 127

            def look(part, vals):
                for step in range(chunk):
                    q = part * chunk + step
                    at = piece_of(q, me, pow2)
                    for r in range(bd):
                        hit = hi == q * bd + r
                        new = []
                        for d in range(4):
                            row = jnp.broadcast_to(g_ref[at, d * bd + r:d * bd + r + 1, :],
                                                   (8, BLOCK))
                            new.append(jnp.where(hit, jnp.take_along_axis(row, lo, axis=1),
                                                 vals[d]))
                        vals = tuple(new)
                return vals

            vals = (jnp.zeros((8, BLOCK), jnp.float32),) * 4
            if nd == chunk:
                vals = look(0, vals)
            else:
                vals = lax.fori_loop(0, nd // chunk, look, vals)
            live = idx >= 0
            for d in range(3):
                d_ref[d, rows8, lanes] = jnp.where(live, pos_ref[d:d + 1, lanes] - vals[d], 0.0)
            d_ref[3, rows8, lanes] = jnp.where(live, vals[3], -1.0)
            return carry

        lax.fori_loop(0, NBR // 8, group, 0, unroll=4 if nd == chunk else 1)
        offs = [d_ref[d, :, lanes] for d in range(3)]
        nk = d_ref[3, :, lanes]
        r2 = offs[0] * offs[0] + offs[1] * offs[1] + offs[2] * offs[2]
        u = 1.0 - r2 * (1.0 / cutoff_sq)
        shell = u * u * (ELEM / NBR)
        for k in range(RAD):
            val = shell * jnp.exp(-RATES[k] * r2)
            for e in range(ELEM):
                f_ref[e * RAD + k:e * RAD + k + 1, lanes] = jnp.sum(
                    jnp.where(nk == e, val, 0.0), axis=0, keepdims=True)
    kind = kind_ref[...]
    hot = one_hot(kind)
    feats = f_ref[...]
    h1 = jnp.tanh(pick(kind, [dot(w1[e], feats) for e in range(ELEM)]) + dot(b1[...], hot, 0))
    h2 = jnp.tanh(pick(kind, [dot(w2[e], h1) for e in range(ELEM)]) + dot(b2[...], hot, 0))
    h_ref[0] = h1
    h_ref[1] = h2
    chi = jnp.sum(dot(wo[...], hot, 0) * h2, axis=0, keepdims=True) + dot(bo[...], hot)
    for a in range(bd):
        chi_ref[a:a + 1, :] = chi[:, a * BLOCK:(a + 1) * BLOCK]


def fold(vals):
    tiles = vals.reshape(BLOCK // 8, 8, BLOCK)
    terms = [tiles[k] for k in range(BLOCK // 8)]
    while len(terms) > 1:
        terms = [terms[k] + terms[k + 1] for k in range(0, len(terms), 2)]
    return terms[0]


def split3(vals):
    parts = []
    for _ in range(3):
        top = vals.astype(jnp.bfloat16).astype(jnp.float32)
        parts.append(top)
        vals = vals - top
    return parts


def tile_kernel(pow2, nd, bd, nb, me_ref, g_ref, r_ref, mid_ref, a_ref):
    me = me_ref[0]
    sub8 = lax.broadcasted_iota(jnp.int32, (8, BLOCK), 0)
    r_ref[...] = jnp.zeros_like(r_ref)
    for q in range(nd):
        at = piece_of(q, me, pow2)
        for r in range(bd):
            for d in range(3):
                r_ref[q * bd + r, d:d + 1, :] = g_ref[at, d * bd + r:d * bd + r + 1, :]

    def set_block(b, carry):
        mid = jnp.broadcast_to(r_ref[b][:, 0:1], (8, BLOCK))
        mid_ref[b] = mid
        rel = r_ref[b] - mid
        size = jnp.sum(rel * rel, axis=0, keepdims=True)
        tile = jnp.where(sub8 == 3, 1.0,
                         jnp.where(sub8 == 4, size * -SCALE - 1.0, rel * (2.0 * SCALE)))
        q1, q2, q3 = split3(tile)
        a_ref[b] = jnp.concatenate([q1, q1, q2, q1, q3, q2], axis=0).T.astype(jnp.bfloat16)
        return carry

    lax.fori_loop(0, nb + 1, set_block, 0, unroll=11 if nb + 1 == 33 else 1)


def pull_kernel(bd, kind_ref, d_ref, h_ref, w1, w2, wo, push_ref, f_ref):
    kind = kind_ref[...]
    h1 = h_ref[0]
    h2 = h_ref[1]
    pre2 = dot(wo[...], one_hot(kind), 0) * (1.0 - h2 * h2)
    pre1 = sum(dot(w2[e], jnp.where(kind == e, pre2, 0.0), 0) for e in range(ELEM))
    pre1 = pre1 * (1.0 - h1 * h1)
    f_ref[...] = sum(dot(w1[e], jnp.where(kind == e, pre1, 0.0), 0)
                     for e in range(ELEM)) * (ELEM / NBR)
    for a in range(bd):
        lanes = slice(a * BLOCK, (a + 1) * BLOCK)
        offs = [d_ref[d, :, lanes] for d in range(3)]
        nk = d_ref[3, :, lanes]
        r2 = offs[0] * offs[0] + offs[1] * offs[1] + offs[2] * offs[2]
        u = 1.0 - r2 * (1.0 / cutoff_sq)
        s1 = jnp.zeros_like(r2)
        s2 = jnp.zeros_like(r2)
        for k in range(RAD):
            sel = jnp.zeros_like(r2)
            for e in range(ELEM):
                sel = jnp.where(nk == e, f_ref[e * RAD + k:e * RAD + k + 1, lanes], sel)
            term = sel * jnp.exp(-RATES[k] * r2)
            s1 = s1 + term
            s2 = s2 + RATES[k] * term
        grad = -u * ((2.0 / cutoff_sq) * s1 + u * s2)
        for d in range(3):
            push_ref[d, :, lanes] = 2.0 * grad * offs[d]


def solve_kernel(pow2, nd, bd, nb, slots, stored, parts, me_ref, pair_ref, count_ref, hard_ref,
                 *refs):
    pieces = refs[:parts]
    (g_ref, r_ref, mid_ref, a_ref, push_ref, nbr_ref, charge_ref, part_ref, x_ref, p_ref, pc_ref,
     y_ref, s_ref, t_ref, left_ref, right_ref) = refs[parts:]
    flat_refs = (left_ref, right_ref)
    me = me_ref[0]
    cross = slots - bd
    sub = lax.broadcasted_iota(jnp.int32, (BLOCK, BLOCK), 0)
    ident = sub == lax.broadcasted_iota(jnp.int32, (BLOCK, BLOCK), 1)
    sub8 = lax.broadcasted_iota(jnp.int32, (8, BLOCK), 0)

    join_pieces(pieces, x_ref)
    p_ref[...] = jnp.zeros_like(p_ref)
    hards = []
    for q in range(nd):
        at = piece_of(q, me, pow2)
        span = slice(q * bd, (q + 1) * bd)
        p_ref[span, :] = -x_ref[at]
        hards.append(pick(g_ref[at, 3 * bd:4 * bd, :], [hard_ref[e] for e in range(ELEM)]))
    hard = jnp.concatenate(hards, axis=0)

    def set_charge(b, carry):
        pc_ref[b] = column(p_ref[pl.ds(b, 1), :])
        return carry

    def set_charges():
        if nb > 64:
            lax.fori_loop(0, nb, set_charge, 0)
            return
        turned = jnp.concatenate(split3(p_ref[0:nb]), axis=0).T.astype(jnp.bfloat16)
        ids = lax.broadcasted_iota(jnp.int32, (3 * nb, BLOCK), 0) % nb
        for b in range(0, nb, 2):
            chosen = [jnp.where(ids == b + m, 1.0, 0.0).astype(jnp.bfloat16) for m in range(2)]
            cols = jnp.dot(turned, jnp.concatenate(chosen, axis=1),
                           preferred_element_type=jnp.float32)
            for m in range(2):
                pc_ref[b + m] = cols[:, m * BLOCK:(m + 1) * BLOCK]

    pc_ref[nb] = jnp.zeros((BLOCK, BLOCK), jnp.float32)
    set_charges()

    def slot_of(q):
        return q ^ me if nd == 8 else q

    def power(j, i):
        rel = r_ref[i] - mid_ref[j]
        size = jnp.sum(rel * rel, axis=0, keepdims=True)
        tile = jnp.where(sub8 == 3, size * -SCALE, jnp.where(sub8 == 4, 1.0, rel))
        p1, p2, p3 = split3(tile)
        right = jnp.concatenate([p1, p2, p1, p3, p1, p2], axis=0).astype(jnp.bfloat16)
        return jnp.dot(a_ref[j], right, preferred_element_type=jnp.float32)

    def gamma(j, i):
        return jnp.exp2(power(j, i))

    def own_gamma(b):
        return jnp.where(ident, 0.0, gamma(b, b))

    def entry(t, j, i):
        return t_ref[t] if stored else gamma(j, i)

    def own_entry(b):
        return t_ref[b] if stored else own_gamma(b)

    size = 4 if cross % 4 == 0 else 1
    wide = 8
    piece = piece_of(me, me, pow2)

    def list_piece(q, carry):
        place, own_place = carry
        number = count_ref[q] - bd

        def list_group(k, inner):
            spots = [(side, m) for side in range(2) for m in range(size)]
            first = 2 * slots * q + bd + size * k
            found = [pair_ref[first + side * slots + m] for side, m in spots]
            for (side, m), block in zip(spots, found):
                flat_refs[side][place + size * k + m] = block
            return inner

        lax.fori_loop(0, (number + size - 1) // size, list_group, 0)
        return place + number, jnp.where(q == piece, place, own_place)

    pairs, own_place = lax.fori_loop(0, nd, list_piece, (jnp.int32(0), jnp.int32(0)))
    for m in range(wide):
        for side in range(2):
            flat_refs[side][pairs + m] = nb

    def ends_of(g, width):
        ends = []
        for m in range(width):
            e = g * width + m
            left, right = flat_refs[0][e], flat_refs[1][e]
            ends += [(nb + 2 * e, left, right), (nb + 2 * e + 1, right, left)]
        return ends

    def first_diag(b, carry):
        val = own_gamma(b)
        if stored:
            t_ref[b] = val
        s_ref[b] = fold(val)
        y_ref[b] = fold(val * pc_ref[b])
        return carry

    lax.fori_loop(0, nb, first_diag, 0, unroll=16)

    def first_step(g, carry):
        found = []
        for t, j, i in ends_of(g, wide):
            val = gamma(j, i)
            if stored:
                t_ref[t] = val
            found.append((i, fold(val), fold(val * pc_ref[j])))
        for i, one, two in found:
            s_ref[i] = s_ref[i] + one
            y_ref[i] = y_ref[i] + two
        return carry

    lax.fori_loop(0, (pairs + wide - 1) // wide, first_step, 0)

    def gathered(ref):
        return jnp.sum(ref[0:nb], axis=1)

    diag = hard + gathered(s_ref)

    def next_step(g, carry):
        found = [(i, fold(entry(t, j, i) * pc_ref[j])) for t, j, i in ends_of(g, wide)]
        for i, one in found:
            y_ref[i] = y_ref[i] + one
        return carry

    def next_diag(b, carry):
        y_ref[b] = fold(own_entry(b) * pc_ref[b])
        return carry

    def matvec():
        set_charges()
        lax.fori_loop(0, nb, next_diag, 0, unroll=8)
        lax.fori_loop(0, (pairs + wide - 1) // wide, next_step, 0)

    def total(vals):
        return jnp.sum(jnp.sum(vals, axis=0, keepdims=True), axis=1, keepdims=True)

    res = p_ref[0:nb]
    p = res
    x = jnp.zeros_like(res)
    rho = total(res * res)
    for it in range(ITERS):
        if it:
            matvec()
        image = diag * p + gathered(y_ref)
        step = rho / total(p * image)
        x = x + step * p
        if it + 1 < ITERS:
            res = res - step * image
            rho2 = total(res * res)
            p = res + (rho2 / rho) * p
            rho = rho2
            p_ref[0:nb] = p
    p_ref[0:nb] = x
    for a in range(bd):
        charge_ref[a:a + 1, :] = p_ref[pl.ds(me * bd + a, 1), :]
        set_charge(me * bd + a, 0)
    mine = jnp.concatenate([charge_ref[a:a + 1, :] for a in range(bd)], axis=1)
    width = bd * BLOCK

    several = 8

    bf16 = jnp.bfloat16
    zero16 = jnp.zeros((16, width), bf16)
    one16 = jnp.ones((16, width), bf16)
    lines = lax.broadcasted_iota(jnp.int32, (16, width), 0).astype(jnp.float32)
    wanted = [(lines + 16.0 * k).astype(bf16) for k in range(max(BLOCK, nb) // 16)]

    def spread(row):
        return jnp.broadcast_to(row, (16, width)).astype(bf16)

    def scatter(k, acc):
        lefts = []
        rights = []
        for m in range(several):
            s = k * several + m
            idx = nbr_ref[pl.ds(s, 1), :]
            block = spread((idx >> 7).astype(jnp.float32))
            lane = spread((idx & 127).astype(jnp.float32))
            rights.append(jnp.concatenate(
                [jnp.where(wanted[r] == lane, one16, zero16) for r in range(BLOCK // 16)], axis=0))
            hits = [wanted[r] == block for r in range(nb // 16)]
            upper = []
            lower = []
            for d in range(3):
                val = push_ref[d, pl.ds(s, 1), :] * mine
                top = val.astype(bf16).astype(jnp.float32)
                top16 = spread(top)
                low16 = spread(val - top)
                upper += [jnp.where(hit, top16, zero16) for hit in hits]
                lower += [jnp.where(hit, low16, zero16) for hit in hits]
            lefts.append(jnp.concatenate(upper + lower, axis=0))
        return acc + lax.dot_general(jnp.concatenate(rights, axis=1),
                                     jnp.concatenate(lefts, axis=1), (((1,), (1,)), ((), ())),
                                     preferred_element_type=jnp.float32)

    acc = lax.fori_loop(0, NBR // several, scatter, jnp.zeros((BLOCK, 6 * nb), jnp.float32))
    acc = acc.T
    acc = acc[:3 * nb] + acc[3 * nb:]
    for q in range(nd):
        for d in range(3):
            part_ref[slot_of(q), d * bd:(d + 1) * bd, :] = acc[d * nb + q * bd:d * nb + (q + 1) * bd]

    def moments(rel, weights, side):
        tile = jnp.where(sub8 == 3, 1.0, rel)
        rows = jnp.concatenate(split3(tile) + [jnp.zeros_like(rel)], axis=0).astype(jnp.bfloat16)
        out = lax.dot_general(jnp.concatenate([rows, rows], axis=1),
                              jnp.concatenate(weights, axis=side), (((1,), (side,)), ((), ())),
                              preferred_element_type=jnp.float32)
        return out[0:8] + out[8:16] + out[16:24]

    def force_of(rel, found):
        return (rel * found[3:4] - found) * (0.5 / sigma_sq)

    def weigh(val, j, i):
        both = pc_ref[j] + p_ref[pl.ds(i, 1), :]
        weight = val * (both * both)
        top = weight.astype(jnp.bfloat16)
        return top, (weight - top.astype(jnp.float32)).astype(jnp.bfloat16)

    s_ref[...] = jnp.zeros_like(s_ref)
    for a in range(bd):
        b = me * bd + a
        rel = r_ref[b] - mid_ref[b]
        force = force_of(rel, moments(rel, weigh(own_entry(b), b, b), 0))
        lanes = slice(a * BLOCK, (a + 1) * BLOCK)
        for d in range(3):
            away = jnp.sum(push_ref[d, :, lanes], axis=0, keepdims=True) * charge_ref[a:a + 1, :]
            force = jnp.where(sub8 == d, force - away, force)
        s_ref[b] = force
    together = 4 if cross % 4 == 0 else 1

    def pair_force(k, carry):
        found = []
        for m in range(together):
            e = k * together + m
            spot = 2 * slots * piece + bd + e
            j, i = pair_ref[spot], pair_ref[spot + slots]
            mid = mid_ref[j]
            rel_j = r_ref[j] - mid
            rel_i = r_ref[i] - mid
            weights = weigh(entry(nb + 2 * (own_place + e), j, i), j, i)
            found.append((i, force_of(rel_i, moments(rel_j, weights, 0))))
            found.append((j, force_of(rel_j, moments(rel_i, weights, 1))))
        for b, force in found:
            s_ref[b] = s_ref[b] + force
        return carry

    lax.fori_loop(0, (count_ref[piece] - bd + together - 1) // together, pair_force, 0)
    for q in range(nd):
        for d in range(3):
            for r in range(bd):
                at = slice(d * bd + r, d * bd + r + 1)
                part_ref[slot_of(q), at, :] = part_ref[slot_of(q), at, :] + s_ref[q * bd + r, d:d + 1, :]


def swap(vals, step, n):
    return lax.ppermute(vals, "blk", [(i, i ^ step) for i in range(n)])


def gather_far_first(own, n, beside):
    if n & (n - 1):
        return [lax.all_gather(own, "blk")], beside
    got = own[None]
    step = n // 2
    while step:
        both = jnp.stack([got, swap(got, step, n)], axis=1)
        got = both.reshape((2 * got.shape[0],) + own.shape)
        if step == n // 4:
            got, beside = lax.optimization_barrier((got, beside))
        step //= 2
    return [got], beside


def gather_near_first(own, n, beside):
    if n & (n - 1):
        return [lax.all_gather(own, "blk")], beside
    got = own[None]
    step = 1
    while step < n:
        got = jnp.concatenate([got, swap(got, step, n)], axis=0)
        if step == n // 4:
            got, beside = lax.optimization_barrier((got, beside))
        step *= 2
    return [got], beside


def reduce_parts(part, n):
    if n != 8:
        return jnp.sum(lax.all_to_all(part, "blk", 0, 0), axis=0)
    mine = part[0::2] + swap(part[1::2], 1, n)
    far = [swap(mine[k], 2 * k, n) for k in (1, 2, 3)]
    return mine[0] + far[0] + far[1] + far[2]


def on_device(positions, species, neighbors, pair_lists, hardness, w_first, b_first, w_second,
              b_second, w_out, b_out):
    n = lax.axis_size("blk")
    me = lax.axis_index("blk")
    atoms = positions.shape[1]
    bd = atoms // BLOCK
    nb = bd * n
    slots = pair_lists.shape[1]
    hid = w_first.shape[1]
    f32 = jnp.float32
    kind = species.reshape(1, atoms)
    small = pltpu.CompilerParams(vmem_limit_bytes=24 << 20)
    in_hbm = functools.partial(pltpu.with_memory_space_constraint, memory_space=pltpu.HBM)
    first = tuple(in_hbm(r) for r in (positions, kind, pair_lists))
    own, pos, kinds, _ = pl.pallas_call(
        pack_kernel,
        out_shape=(jax.ShapeDtypeStruct((PACK, BLOCK), f32),)
        + tuple(jax.ShapeDtypeStruct(r.shape, r.dtype) for r in first),
        in_specs=[spec(pltpu.HBM)] * 3, out_specs=(spec(VM),) * 4,
        scratch_shapes=[pltpu.SemaphoreType.DMA((3,))],
        compiler_params=small, name="pack",
    )(*first)
    later = tuple(in_hbm(r) for r in (
        neighbors, w_first.transpose(1, 0, 2), b_first, w_second.transpose(1, 0, 2), b_second,
        w_out, b_out.reshape(1, ELEM)))
    staged = pl.pallas_call(
        functools.partial(stage_kernel, len(later)),
        out_shape=tuple(jax.ShapeDtypeStruct(r.shape, r.dtype) for r in later),
        in_specs=[spec(pltpu.HBM)] * len(later), out_specs=(spec(VM),) * len(later),
        scratch_shapes=[pltpu.SemaphoreType.DMA((len(later),))],
        compiler_params=small, name="stage",
    )(*later)
    pow2 = n & (n - 1) == 0
    places, staged = gather_far_first(own, n, staged)
    nbr, v1, b1, v2, b2, wo, bo = staged
    chi, offs, hidden, whole, w1, w2 = pl.pallas_call(
        functools.partial(chi_kernel, pow2, n, bd, len(places)),
        out_shape=(jax.ShapeDtypeStruct((bd, BLOCK), f32),
                   jax.ShapeDtypeStruct((4, NBR, atoms), f32),
                   jax.ShapeDtypeStruct((2, hid, atoms), f32),
                   jax.ShapeDtypeStruct((n, PACK, BLOCK), f32),
                   jax.ShapeDtypeStruct(w_first.shape, f32),
                   jax.ShapeDtypeStruct(w_second.shape, f32)),
        in_specs=[spec(SM)] + [spec(VM)] * (9 + len(places)),
        out_specs=(spec(VM),) * 6,
        scratch_shapes=[VM((DESC, atoms), f32)],
        compiler_params=small,
        name="chi",
    )(me[None], *places, pos, nbr, kinds, v1, b1, v2, b2, wo, bo)
    tiles = pl.pallas_call(
        functools.partial(tile_kernel, pow2, n, bd, nb),
        out_shape=(jax.ShapeDtypeStruct((nb + 1, 8, BLOCK), f32),
                   jax.ShapeDtypeStruct((nb + 1, 8, BLOCK), f32),
                   jax.ShapeDtypeStruct((nb + 1, BLOCK, 48), jnp.bfloat16)),
        in_specs=[spec(SM), spec(VM)],
        out_specs=(spec(VM),) * 3,
        compiler_params=small,
        name="tiles",
    )(me[None], whole)
    all_chi, (rows, mids, left) = gather_near_first(chi, n, tiles)
    push = pl.pallas_call(
        functools.partial(pull_kernel, bd),
        out_shape=jax.ShapeDtypeStruct((3, NBR, atoms), f32),
        in_specs=[spec(VM)] * 6,
        out_specs=spec(VM),
        scratch_shapes=[VM((DESC, atoms), f32)],
        compiler_params=small,
        name="pull",
    )(kinds, offs, hidden, w1, w2, wo)
    lists = whole[:, 4 * bd:4 * bd + 2, :slots].astype(jnp.int32)
    counts = jnp.sum((lists[:, 0] >= 0).astype(jnp.int32), axis=1)
    lists = jnp.where(lists < 0, nb, lists)
    lists = lists.reshape(-1)
    entries = nb + 2 * (n * slots - nb)
    stored = entries * BLOCK * BLOCK * 4 <= STORE_LIMIT
    charges, part = pl.pallas_call(
        functools.partial(solve_kernel, pow2, n, bd, nb, slots, stored, len(all_chi)),
        out_shape=(jax.ShapeDtypeStruct((bd, BLOCK), f32),
                   jax.ShapeDtypeStruct((n, 3 * bd, BLOCK), f32)),
        in_specs=[spec(SM)] * 4 + [spec(VM)] * (6 + len(all_chi)),
        out_specs=(spec(VM),) * 2,
        scratch_shapes=[VM((n, bd, BLOCK), f32), VM((nb + 8, BLOCK), f32),
                        VM((nb + 1, BLOCK, BLOCK), f32), VM((nb + 1, 8, BLOCK), f32),
                        VM((nb + 1, 8, BLOCK), f32),
                        VM((entries + 16 if stored else 1, BLOCK, BLOCK), f32),
                        SM((n * (slots - bd) + 12,), jnp.int32),
                        SM((n * (slots - bd) + 12,), jnp.int32)],
        compiler_params=pltpu.CompilerParams(vmem_limit_bytes=(42 if stored else 58) << 20),
        name="solve",
    )(me[None], lists, counts, hardness, *all_chi, whole, rows, mids, left, push, nbr)
    forces = reduce_parts(part, n)
    return charges.reshape(atoms), forces.reshape(3, atoms)


def solution(mesh):
    both = ("cell", "blk")
    placed = (P(None, both), P(both), P(None, both), P(None, both)) + (P(),) * 7
    return jax.shard_map(
        on_device,
        mesh=mesh,
        in_specs=placed,
        out_specs=(P(both), P(None, both)),
        check_vma=False,
    )
```

```python
import functools
import math

import jax
import jax.numpy as jnp
import numpy as np
from jax import lax
from jax.experimental import pallas as pl
from jax.experimental.pallas import tpu as pltpu
from jax.sharding import PartitionSpec as P

ELEM = 4
RAD = 16
DESC = ELEM * RAD
BLOCK = 128
NBR = 32
ITERS = 3
PACK = 24
STORE_LIMIT = 36 << 20

coulomb_scale = 0.5
sigma_sq = 4.0
cutoff_sq = 49.0
highest = lax.Precision.HIGHEST
RATES = [0.005 * 200.0 ** (k / (RAD - 1)) for k in range(RAD)]
VM = pltpu.VMEM
SM = pltpu.SMEM
SCALE = math.log2(math.e) / (2.0 * sigma_sq)


def spec(space):
    return pl.BlockSpec(memory_space=space)


def piece_of(q, me, pow2):
    return q ^ me if pow2 else q


def dot(a, b, lhs=1):
    return lax.dot_general(a, b, (((lhs,), (0,)), ((), ())), precision=highest,
                           preferred_element_type=jnp.float32)


def column(row):
    return jnp.broadcast_to(row, (BLOCK, BLOCK)).T


def pick(kind, mats):
    out = jnp.where(kind == 0, mats[0], 0.0)
    for e in range(1, ELEM):
        out = jnp.where(kind == e, mats[e], out)
    return out


def one_hot(kind):
    ids = lax.broadcasted_iota(jnp.int32, (ELEM, kind.shape[1]), 0)
    return jnp.where(ids == kind, 1.0, 0.0)


def start_copies(sources, targets, sems):
    copies = [pltpu.make_async_copy(source, target, sems.at[k])
              for k, (source, target) in enumerate(zip(sources, targets))]
    for copy in copies:
        copy.start()
    return copies


def stage_kernel(count, *refs):
    for copy in start_copies(refs[:count], refs[count:2 * count], refs[-1]):
        copy.wait()


def pack_kernel(pos_hbm, kind_hbm, pairs_hbm, own_ref, pos_ref, kind_ref, pairs_ref, sems):
    copies = start_copies((pos_hbm, kind_hbm, pairs_hbm), (pos_ref, kind_ref, pairs_ref), sems)
    own_ref[...] = jnp.zeros_like(own_ref)
    for copy in copies:
        copy.wait()
    bd = pos_ref.shape[1] // BLOCK
    for a in range(bd):
        lanes = slice(a * BLOCK, (a + 1) * BLOCK)
        for d in range(3):
            own_ref[d * bd + a:d * bd + a + 1, :] = pos_ref[d:d + 1, lanes]
        own_ref[3 * bd + a:3 * bd + a + 1, :] = kind_ref[:, lanes].astype(jnp.float32)
    slots = pairs_ref.shape[1]
    for side in range(2):
        own_ref[4 * bd + side:4 * bd + side + 1, :slots] = (
            pairs_ref[side:side + 1, :].astype(jnp.float32))


def join_pieces(pieces, out_ref):
    first = 0
    for piece in pieces:
        count = piece.shape[0]
        out_ref[first:first + count] = piece[...]
        first += count


def chi_kernel(pow2, nd, bd, parts, me_ref, *refs):
    pieces = refs[:parts]
    (pos_ref, nbr_ref, kind_ref, v1, b1, v2, b2, wo, bo,
     chi_ref, d_ref, h_ref, g_ref, w1, w2, f_ref) = refs[parts:]
    me = me_ref[0]
    chunk = min(nd, 8)
    join_pieces(pieces, g_ref)
    for turned, kept in ((v1, w1), (v2, w2)):
        for h in range(turned.shape[0]):
            for e in range(ELEM):
                kept[e, h:h + 1, :] = turned[h, e:e + 1, :]
    for a in range(bd):
        lanes = slice(a * BLOCK, (a + 1) * BLOCK)

        def group(g, carry):
            rows8 = pl.ds(pl.multiple_of(g * 8, 8), 8)
            idx = nbr_ref[rows8, lanes]
            hi = idx >> 7
            lo = idx & 127

            def look(part, vals):
                for step in range(chunk):
                    q = part * chunk + step
                    at = piece_of(q, me, pow2)
                    for r in range(bd):
                        hit = hi == q * bd + r
                        new = []
                        for d in range(4):
                            row = jnp.broadcast_to(g_ref[at, d * bd + r:d * bd + r + 1, :],
                                                   (8, BLOCK))
                            new.append(jnp.where(hit, jnp.take_along_axis(row, lo, axis=1),
                                                 vals[d]))
                        vals = tuple(new)
                return vals

            vals = (jnp.zeros((8, BLOCK), jnp.float32),) * 4
            if nd == chunk:
                vals = look(0, vals)
            else:
                vals = lax.fori_loop(0, nd // chunk, look, vals)
            live = idx >= 0
            for d in range(3):
                d_ref[d, rows8, lanes] = jnp.where(live, pos_ref[d:d + 1, lanes] - vals[d], 0.0)
            d_ref[3, rows8, lanes] = jnp.where(live, vals[3], -1.0)
            return carry

        lax.fori_loop(0, NBR // 8, group, 0, unroll=4 if nd == chunk else 1)
        offs = [d_ref[d, :, lanes] for d in range(3)]
        nk = d_ref[3, :, lanes]
        r2 = offs[0] * offs[0] + offs[1] * offs[1] + offs[2] * offs[2]
        u = 1.0 - r2 * (1.0 / cutoff_sq)
        shell = u * u * (ELEM / NBR)
        for k in range(RAD):
            val = shell * jnp.exp(-RATES[k] * r2)
            for e in range(ELEM):
                f_ref[e * RAD + k:e * RAD + k + 1, lanes] = jnp.sum(
                    jnp.where(nk == e, val, 0.0), axis=0, keepdims=True)
    kind = kind_ref[...]
    hot = one_hot(kind)
    feats = f_ref[...]
    h1 = jnp.tanh(pick(kind, [dot(w1[e], feats) for e in range(ELEM)]) + dot(b1[...], hot, 0))
    h2 = jnp.tanh(pick(kind, [dot(w2[e], h1) for e in range(ELEM)]) + dot(b2[...], hot, 0))
    h_ref[0] = h1
    h_ref[1] = h2
    chi = jnp.sum(dot(wo[...], hot, 0) * h2, axis=0, keepdims=True) + dot(bo[...], hot)
    for a in range(bd):
        chi_ref[a:a + 1, :] = chi[:, a * BLOCK:(a + 1) * BLOCK]


def fold(vals):
    tiles = vals.reshape(BLOCK // 8, 8, BLOCK)
    terms = [tiles[k] for k in range(BLOCK // 8)]
    while len(terms) > 1:
        terms = [terms[k] + terms[k + 1] for k in range(0, len(terms), 2)]
    return terms[0]


def split3(vals):
    parts = []
    for _ in range(3):
        top = vals.astype(jnp.bfloat16).astype(jnp.float32)
        parts.append(top)
        vals = vals - top
    return parts


def tile_kernel(pow2, nd, bd, nb, me_ref, g_ref, r_ref, mid_ref, a_ref):
    me = me_ref[0]
    sub8 = lax.broadcasted_iota(jnp.int32, (8, BLOCK), 0)
    r_ref[...] = jnp.zeros_like(r_ref)
    for q in range(nd):
        at = piece_of(q, me, pow2)
        for r in range(bd):
            for d in range(3):
                r_ref[q * bd + r, d:d + 1, :] = g_ref[at, d * bd + r:d * bd + r + 1, :]

    def set_block(b, carry):
        mid = jnp.broadcast_to(r_ref[b][:, 0:1], (8, BLOCK))
        mid_ref[b] = mid
        rel = r_ref[b] - mid
        size = jnp.sum(rel * rel, axis=0, keepdims=True)
        tile = jnp.where(sub8 == 3, 1.0,
                         jnp.where(sub8 == 4, size * -SCALE - 1.0, rel * (2.0 * SCALE)))
        q1, q2, q3 = split3(tile)
        a_ref[b] = jnp.concatenate([q1, q1, q2, q1, q3, q2], axis=0).T.astype(jnp.bfloat16)
        return carry

    lax.fori_loop(0, nb + 1, set_block, 0, unroll=11 if nb + 1 == 33 else 1)


def pull_kernel(bd, kind_ref, d_ref, h_ref, w1, w2, wo, push_ref, f_ref):
    kind = kind_ref[...]
    h1 = h_ref[0]
    h2 = h_ref[1]
    pre2 = dot(wo[...], one_hot(kind), 0) * (1.0 - h2 * h2)
    pre1 = sum(dot(w2[e], jnp.where(kind == e, pre2, 0.0), 0) for e in range(ELEM))
    pre1 = pre1 * (1.0 - h1 * h1)
    f_ref[...] = sum(dot(w1[e], jnp.where(kind == e, pre1, 0.0), 0)
                     for e in range(ELEM)) * (ELEM / NBR)
    for a in range(bd):
        lanes = slice(a * BLOCK, (a + 1) * BLOCK)
        offs = [d_ref[d, :, lanes] for d in range(3)]
        nk = d_ref[3, :, lanes]
        r2 = offs[0] * offs[0] + offs[1] * offs[1] + offs[2] * offs[2]
        u = 1.0 - r2 * (1.0 / cutoff_sq)
        s1 = jnp.zeros_like(r2)
        s2 = jnp.zeros_like(r2)
        for k in range(RAD):
            sel = jnp.zeros_like(r2)
            for e in range(ELEM):
                sel = jnp.where(nk == e, f_ref[e * RAD + k:e * RAD + k + 1, lanes], sel)
            term = sel * jnp.exp(-RATES[k] * r2)
            s1 = s1 + term
            s2 = s2 + RATES[k] * term
        grad = -u * ((2.0 / cutoff_sq) * s1 + u * s2)
        for d in range(3):
            push_ref[d, :, lanes] = 2.0 * grad * offs[d]


def solve_kernel(pow2, nd, bd, nb, slots, stored, parts, me_ref, pair_ref, count_ref, hard_ref,
                 *refs):
    pieces = refs[:parts]
    (g_ref, r_ref, mid_ref, a_ref, push_ref, nbr_ref, charge_ref, part_ref, x_ref, p_ref, pc_ref,
     y_ref, s_ref, t_ref, left_ref, right_ref) = refs[parts:]
    flat_refs = (left_ref, right_ref)
    me = me_ref[0]
    cross = slots - bd
    sub = lax.broadcasted_iota(jnp.int32, (BLOCK, BLOCK), 0)
    ident = sub == lax.broadcasted_iota(jnp.int32, (BLOCK, BLOCK), 1)
    sub8 = lax.broadcasted_iota(jnp.int32, (8, BLOCK), 0)

    join_pieces(pieces, x_ref)
    p_ref[...] = jnp.zeros_like(p_ref)
    hards = []
    for q in range(nd):
        at = piece_of(q, me, pow2)
        span = slice(q * bd, (q + 1) * bd)
        p_ref[span, :] = -x_ref[at]
        hards.append(pick(g_ref[at, 3 * bd:4 * bd, :], [hard_ref[e] for e in range(ELEM)]))
    hard = jnp.concatenate(hards, axis=0)

    def set_charge(b, carry):
        pc_ref[b] = column(p_ref[pl.ds(b, 1), :])
        return carry

    def set_charges():
        if nb > 64:
            lax.fori_loop(0, nb, set_charge, 0)
            return
        turned = jnp.concatenate(split3(p_ref[0:nb]), axis=0).T.astype(jnp.bfloat16)
        ids = lax.broadcasted_iota(jnp.int32, (3 * nb, BLOCK), 0) % nb
        for b in range(0, nb, 2):
            chosen = [jnp.where(ids == b + m, 1.0, 0.0).astype(jnp.bfloat16) for m in range(2)]
            cols = jnp.dot(turned, jnp.concatenate(chosen, axis=1),
                           preferred_element_type=jnp.float32)
            for m in range(2):
                pc_ref[b + m] = cols[:, m * BLOCK:(m + 1) * BLOCK]

    pc_ref[nb] = jnp.zeros((BLOCK, BLOCK), jnp.float32)
    set_charges()

    def slot_of(q):
        return q ^ me if nd == 8 else q

    def power(j, i):
        rel = r_ref[i] - mid_ref[j]
        size = jnp.sum(rel * rel, axis=0, keepdims=True)
        tile = jnp.where(sub8 == 3, size * -SCALE, jnp.where(sub8 == 4, 1.0, rel))
        p1, p2, p3 = split3(tile)
        right = jnp.concatenate([p1, p2, p1, p3, p1, p2], axis=0).astype(jnp.bfloat16)
        return jnp.dot(a_ref[j], right, preferred_element_type=jnp.float32)

    def gamma(j, i):
        return jnp.exp2(power(j, i))

    def own_gamma(b):
        return jnp.where(ident, 0.0, gamma(b, b))

    def entry(t, j, i):
        return t_ref[t] if stored else gamma(j, i)

    def own_entry(b):
        return t_ref[b] if stored else own_gamma(b)

    size = 4 if cross % 4 == 0 else 1
    wide = 8
    piece = piece_of(me, me, pow2)

    def list_piece(q, carry):
        place, own_place = carry
        number = count_ref[q] - bd

        def list_group(k, inner):
            spots = [(side, m) for side in range(2) for m in range(size)]
            first = 2 * slots * q + bd + size * k
            found = [pair_ref[first + side * slots + m] for side, m in spots]
            for (side, m), block in zip(spots, found):
                flat_refs[side][place + size * k + m] = block
            return inner

        lax.fori_loop(0, (number + size - 1) // size, list_group, 0)
        return place + number, jnp.where(q == piece, place, own_place)

    pairs, own_place = lax.fori_loop(0, nd, list_piece, (jnp.int32(0), jnp.int32(0)))
    for m in range(wide):
        for side in range(2):
            flat_refs[side][pairs + m] = nb

    def ends_of(g, width):
        ends = []
        for m in range(width):
            e = g * width + m
            left, right = flat_refs[0][e], flat_refs[1][e]
            ends += [(nb + 2 * e, left, right), (nb + 2 * e + 1, right, left)]
        return ends

    def first_diag(b, carry):
        val = own_gamma(b)
        if stored:
            t_ref[b] = val
        s_ref[b] = fold(val)
        y_ref[b] = fold(val * pc_ref[b])
        return carry

    lax.fori_loop(0, nb, first_diag, 0, unroll=16)

    def first_step(g, carry):
        found = []
        for t, j, i in ends_of(g, wide):
            val = gamma(j, i)
            if stored:
                t_ref[t] = val
            found.append((i, fold(val), fold(val * pc_ref[j])))
        for i, one, two in found:
            s_ref[i] = s_ref[i] + one
            y_ref[i] = y_ref[i] + two
        return carry

    lax.fori_loop(0, (pairs + wide - 1) // wide, first_step, 0)

    def gathered(ref):
        return jnp.sum(ref[0:nb], axis=1)

    diag = hard + gathered(s_ref)

    def next_step(g, carry):
        found = [(i, fold(entry(t, j, i) * pc_ref[j])) for t, j, i in ends_of(g, wide)]
        for i, one in found:
            y_ref[i] = y_ref[i] + one
        return carry

    def next_diag(b, carry):
        y_ref[b] = fold(own_entry(b) * pc_ref[b])
        return carry

    def matvec():
        set_charges()
        lax.fori_loop(0, nb, next_diag, 0, unroll=8)
        lax.fori_loop(0, (pairs + wide - 1) // wide, next_step, 0)

    def total(vals):
        return jnp.sum(jnp.sum(vals, axis=0, keepdims=True), axis=1, keepdims=True)

    res = p_ref[0:nb]
    p = res
    x = jnp.zeros_like(res)
    rho = total(res * res)
    for it in range(ITERS):
        if it:
            matvec()
        image = diag * p + gathered(y_ref)
        step = rho / total(p * image)
        x = x + step * p
        if it + 1 < ITERS:
            res = res - step * image
            rho2 = total(res * res)
            p = res + (rho2 / rho) * p
            rho = rho2
            p_ref[0:nb] = p
    p_ref[0:nb] = x
    for a in range(bd):
        charge_ref[a:a + 1, :] = p_ref[pl.ds(me * bd + a, 1), :]
        set_charge(me * bd + a, 0)
    mine = jnp.concatenate([charge_ref[a:a + 1, :] for a in range(bd)], axis=1)
    width = bd * BLOCK

    several = 8

    bf16 = jnp.bfloat16
    zero16 = jnp.zeros((16, width), bf16)
    one16 = jnp.ones((16, width), bf16)
    lines = lax.broadcasted_iota(jnp.int32, (16, width), 0).astype(jnp.float32)
    wanted = [(lines + 16.0 * k).astype(bf16) for k in range(max(BLOCK, nb) // 16)]

    def spread(row):
        return jnp.broadcast_to(row, (16, width)).astype(bf16)

    def scatter(k, acc):
        lefts = []
        rights = []
        for m in range(several):
            s = k * several + m
            idx = nbr_ref[pl.ds(s, 1), :]
            block = spread((idx >> 7).astype(jnp.float32))
            lane = spread((idx & 127).astype(jnp.float32))
            rights.append(jnp.concatenate(
                [jnp.where(wanted[r] == lane, one16, zero16) for r in range(BLOCK // 16)], axis=0))
            hits = [wanted[r] == block for r in range(nb // 16)]
            upper = []
            lower = []
            for d in range(3):
                val = push_ref[d, pl.ds(s, 1), :] * mine
                top = val.astype(bf16).astype(jnp.float32)
                top16 = spread(top)
                low16 = spread(val - top)
                upper += [jnp.where(hit, top16, zero16) for hit in hits]
                lower += [jnp.where(hit, low16, zero16) for hit in hits]
            lefts.append(jnp.concatenate(upper + lower, axis=0))
        return acc + lax.dot_general(jnp.concatenate(rights, axis=1),
                                     jnp.concatenate(lefts, axis=1), (((1,), (1,)), ((), ())),
                                     preferred_element_type=jnp.float32)

    acc = lax.fori_loop(0, NBR // several, scatter, jnp.zeros((BLOCK, 6 * nb), jnp.float32))
    acc = acc.T
    acc = acc[:3 * nb] + acc[3 * nb:]
    for q in range(nd):
        for d in range(3):
            part_ref[slot_of(q), d * bd:(d + 1) * bd, :] = acc[d * nb + q * bd:d * nb + (q + 1) * bd]

    def moments(rel, weights, side):
        tile = jnp.where(sub8 == 3, 1.0, rel)
        rows = jnp.concatenate(split3(tile) + [jnp.zeros_like(rel)], axis=0).astype(jnp.bfloat16)
        out = lax.dot_general(jnp.concatenate([rows, rows], axis=1),
                              jnp.concatenate(weights, axis=side), (((1,), (side,)), ((), ())),
                              preferred_element_type=jnp.float32)
        return out[0:8] + out[8:16] + out[16:24]

    def force_of(rel, found):
        return (rel * found[3:4] - found) * (0.5 / sigma_sq)

    def weigh(val, j, i):
        both = pc_ref[j] + p_ref[pl.ds(i, 1), :]
        weight = val * (both * both)
        top = weight.astype(jnp.bfloat16)
        return top, (weight - top.astype(jnp.float32)).astype(jnp.bfloat16)

    s_ref[...] = jnp.zeros_like(s_ref)
    for a in range(bd):
        b = me * bd + a
        rel = r_ref[b] - mid_ref[b]
        force = force_of(rel, moments(rel, weigh(own_entry(b), b, b), 0))
        lanes = slice(a * BLOCK, (a + 1) * BLOCK)
        for d in range(3):
            away = jnp.sum(push_ref[d, :, lanes], axis=0, keepdims=True) * charge_ref[a:a + 1, :]
            force = jnp.where(sub8 == d, force - away, force)
        s_ref[b] = force
    together = 4 if cross % 4 == 0 else 1

    def pair_force(k, carry):
        found = []
        for m in range(together):
            e = k * together + m
            spot = 2 * slots * piece + bd + e
            j, i = pair_ref[spot], pair_ref[spot + slots]
            mid = mid_ref[j]
            rel_j = r_ref[j] - mid
            rel_i = r_ref[i] - mid
            weights = weigh(entry(nb + 2 * (own_place + e), j, i), j, i)
            found.append((i, force_of(rel_i, moments(rel_j, weights, 0))))
            found.append((j, force_of(rel_j, moments(rel_i, weights, 1))))
        for b, force in found:
            s_ref[b] = s_ref[b] + force
        return carry

    lax.fori_loop(0, (count_ref[piece] - bd + together - 1) // together, pair_force, 0)
    for q in range(nd):
        for d in range(3):
            for r in range(bd):
                at = slice(d * bd + r, d * bd + r + 1)
                part_ref[slot_of(q), at, :] = part_ref[slot_of(q), at, :] + s_ref[q * bd + r, d:d + 1, :]


def swap(vals, step, n):
    return lax.ppermute(vals, "blk", [(i, i ^ step) for i in range(n)])


def gather_far_first(own, n, beside):
    if n & (n - 1):
        return [lax.all_gather(own, "blk")], beside
    got = own[None]
    step = n // 2
    while step:
        both = jnp.stack([got, swap(got, step, n)], axis=1)
        got = both.reshape((2 * got.shape[0],) + own.shape)
        if step == n // 4:
            got, beside = lax.optimization_barrier((got, beside))
        step //= 2
    return [got], beside


def gather_near_first(own, n, beside):
    if n & (n - 1):
        return [lax.all_gather(own, "blk")], beside
    got = own[None]
    step = 1
    while step < n:
        got = jnp.concatenate([got, swap(got, step, n)], axis=0)
        if step == n // 4:
            got, beside = lax.optimization_barrier((got, beside))
        step *= 2
    return [got], beside


def reduce_parts(part, n):
    if n != 8:
        return jnp.sum(lax.all_to_all(part, "blk", 0, 0), axis=0)
    mine = part[0::2] + swap(part[1::2], 1, n)
    far = [swap(mine[k], 2 * k, n) for k in (1, 2, 3)]
    return mine[0] + far[0] + far[1] + far[2]


def on_device(positions, species, neighbors, pair_lists, hardness, w_first, b_first, w_second,
              b_second, w_out, b_out):
    n = lax.axis_size("blk")
    me = lax.axis_index("blk")
    atoms = positions.shape[1]
    bd = atoms // BLOCK
    nb = bd * n
    slots = pair_lists.shape[1]
    hid = w_first.shape[1]
    f32 = jnp.float32
    kind = species.reshape(1, atoms)
    small = pltpu.CompilerParams(vmem_limit_bytes=24 << 20)
    in_hbm = functools.partial(pltpu.with_memory_space_constraint, memory_space=pltpu.HBM)
    first = tuple(in_hbm(r) for r in (positions, kind, pair_lists))
    own, pos, kinds, _ = pl.pallas_call(
        pack_kernel,
        out_shape=(jax.ShapeDtypeStruct((PACK, BLOCK), f32),)
        + tuple(jax.ShapeDtypeStruct(r.shape, r.dtype) for r in first),
        in_specs=[spec(pltpu.HBM)] * 3, out_specs=(spec(VM),) * 4,
        scratch_shapes=[pltpu.SemaphoreType.DMA((3,))],
        compiler_params=small, name="pack",
    )(*first)
    later = tuple(in_hbm(r) for r in (
        neighbors, w_first.transpose(1, 0, 2), b_first, w_second.transpose(1, 0, 2), b_second,
        w_out, b_out.reshape(1, ELEM)))
    staged = pl.pallas_call(
        functools.partial(stage_kernel, len(later)),
        out_shape=tuple(jax.ShapeDtypeStruct(r.shape, r.dtype) for r in later),
        in_specs=[spec(pltpu.HBM)] * len(later), out_specs=(spec(VM),) * len(later),
        scratch_shapes=[pltpu.SemaphoreType.DMA((len(later),))],
        compiler_params=small, name="stage",
    )(*later)
    pow2 = n & (n - 1) == 0
    places, staged = gather_far_first(own, n, staged)
    nbr, v1, b1, v2, b2, wo, bo = staged
    chi, offs, hidden, whole, w1, w2 = pl.pallas_call(
        functools.partial(chi_kernel, pow2, n, bd, len(places)),
        out_shape=(jax.ShapeDtypeStruct((bd, BLOCK), f32),
                   jax.ShapeDtypeStruct((4, NBR, atoms), f32),
                   jax.ShapeDtypeStruct((2, hid, atoms), f32),
                   jax.ShapeDtypeStruct((n, PACK, BLOCK), f32),
                   jax.ShapeDtypeStruct(w_first.shape, f32),
                   jax.ShapeDtypeStruct(w_second.shape, f32)),
        in_specs=[spec(SM)] + [spec(VM)] * (9 + len(places)),
        out_specs=(spec(VM),) * 6,
        scratch_shapes=[VM((DESC, atoms), f32)],
        compiler_params=small,
        name="chi",
    )(me[None], *places, pos, nbr, kinds, v1, b1, v2, b2, wo, bo)
    lists = whole[:, 4 * bd:4 * bd + 2, :slots].astype(jnp.int32)
    counts = jnp.sum((lists[:, 0] >= 0).astype(jnp.int32), axis=1)
    lists = jnp.where(lists < 0, nb, lists)
    lists = lists.reshape(-1)
    tiles = pl.pallas_call(
        functools.partial(tile_kernel, pow2, n, bd, nb),
        out_shape=(jax.ShapeDtypeStruct((nb + 1, 8, BLOCK), f32),
                   jax.ShapeDtypeStruct((nb + 1, 8, BLOCK), f32),
                   jax.ShapeDtypeStruct((nb + 1, BLOCK, 48), jnp.bfloat16)),
        in_specs=[spec(SM), spec(VM)],
        out_specs=(spec(VM),) * 3,
        compiler_params=small,
        name="tiles",
    )(me[None], whole)
    all_chi, (rows, mids, left, counts) = gather_near_first(chi, n, (*tiles, counts))
    push = pl.pallas_call(
        functools.partial(pull_kernel, bd),
        out_shape=jax.ShapeDtypeStruct((3, NBR, atoms), f32),
        in_specs=[spec(VM)] * 6,
        out_specs=spec(VM),
        scratch_shapes=[VM((DESC, atoms), f32)],
        compiler_params=small,
        name="pull",
    )(kinds, offs, hidden, w1, w2, wo)
    entries = nb + 2 * (n * slots - nb)
    stored = entries * BLOCK * BLOCK * 4 <= STORE_LIMIT
    charges, part = pl.pallas_call(
        functools.partial(solve_kernel, pow2, n, bd, nb, slots, stored, len(all_chi)),
        out_shape=(jax.ShapeDtypeStruct((bd, BLOCK), f32),
                   jax.ShapeDtypeStruct((n, 3 * bd, BLOCK), f32)),
        in_specs=[spec(SM)] * 4 + [spec(VM)] * (6 + len(all_chi)),
        out_specs=(spec(VM),) * 2,
        scratch_shapes=[VM((n, bd, BLOCK), f32), VM((nb + 8, BLOCK), f32),
                        VM((nb + 1, BLOCK, BLOCK), f32), VM((nb + 1, 8, BLOCK), f32),
                        VM((nb + 1, 8, BLOCK), f32),
                        VM((entries + 16 if stored else 1, BLOCK, BLOCK), f32),
                        SM((n * (slots - bd) + 12,), jnp.int32),
                        SM((n * (slots - bd) + 12,), jnp.int32)],
        compiler_params=pltpu.CompilerParams(vmem_limit_bytes=(42 if stored else 58) << 20),
        name="solve",
    )(me[None], lists, counts, hardness, *all_chi, whole, rows, mids, left, push, nbr)
    forces = reduce_parts(part, n)
    return charges.reshape(atoms), forces.reshape(3, atoms)


def solution(mesh):
    both = ("cell", "blk")
    placed = (P(None, both), P(both), P(None, both), P(None, both)) + (P(),) * 7
    return jax.shard_map(
        on_device,
        mesh=mesh,
        in_specs=placed,
        out_specs=(P(both), P(None, both)),
        check_vma=False,
    )
```
